512 devices in a mesh: seq: 64 (over y, x, core), ch: 8 (over z).
Axes of the slice: x: 4, y: 8, z: 8, core: 2. Of those that a mesh axis runs over, the one named last changes fastest.
Arguments:
- inputs: bfloat16 [32768, 1024], P('seq', 'ch'), may hold values from -6 to 6
- conv_weight: bfloat16 [3, 1024], P(None, 'ch'), may hold values from -3 to 3
- mixing: bfloat16 [8, 512, 64, 128], P(None, 'seq'), may hold values from -0.5 to 0.5
- pattern: int32 [2, 512], P(None, 'seq'), may hold values from 0 to 7, as said below
- w_in: bfloat16 [1024, 4096], P(None, 'ch'), may hold values from -0.1875 to 0.1875
- w_out: bfloat16 [4096, 1024], P('ch'), may hold values from -0.09375 to 0.09375
- cotangent: bfloat16 [32768, 1024], P('seq', 'ch'), may hold values from -6 to 6
Outputs:
- layer_out: bfloat16 [32768, 1024], P('seq', 'ch')
- convolved: bfloat16 [32768, 1024], P('seq', 'ch')
- grad_input: bfloat16 [32768, 1024], P('seq', 'ch')
The draws below stay inside these ranges and needn't reach their ends.
Inputs may be any that keep to these rules, and one draw needn't show every extreme that they name: `pattern`: for each of the 2 factors and each aligned run of 8 blocks (the blocks of one device), entry j of the run is a number k != j with entry k equal to j.
All inputs are finite; a program needn't handle non-finite values.
Results may differ from the reference program's by a relative error of at most 0.025.
Values may be sent and summed in bfloat16 or wider, within the bound.
A program may use at most 64 MiB of HBM per device.

```python
import jax
import jax.numpy as jnp

D = 1024
HIDDEN_SIZE = 4096
BLOCK = 64
LOCAL = 2
BL = 8
NB = 512
TOKENS = 32768
LEVELS = 6
FACTORS = 8


def draw_pattern(key, part):
    count = LOCAL * (NB // BL)
    keys = jax.random.split(key, count)
    orders = jax.vmap(lambda sub_key: jax.random.permutation(sub_key, BL))(keys).astype(jnp.int32)
    spots = jnp.argsort(orders, axis=1, stable=True).astype(jnp.int32)
    mates = jnp.bitwise_xor(spots, 1)
    partner = jnp.take_along_axis(orders, mates, axis=1)
    return partner.reshape(LOCAL, NB).astype(jnp.int32)


def levels(own_key, dims, shards, low, largest):
    factor_of = 1.0
    for dim, blocks in shards:
        draws = jax.random.uniform(jax.random.fold_in(jax.random.fold_in(own_key, 6), dim), (blocks,), jnp.float32, low / len(shards), largest / len(shards))
        factor_of = factor_of * jnp.repeat(jnp.exp(draws), dims[dim] // blocks).reshape((-1,) + (1,) * (len(dims) - 1 - dim))
    return factor_of


def scatter_about(key, shape, deviation, reach, shards=(), kind=jnp.bfloat16):
    entries = jax.random.normal(key, shape, jnp.float32) * deviation
    if len(shards) > 0:
        entries = levels(key, shape, shards, -0.22, 0.18) * entries
    return jnp.clip(entries, min=-reach, max=reach).astype(kind)


def setup_inputs(seed: int = 0) -> dict:
    seeds = jax.random.split(jax.random.key(seed), 8)
    inputs = scatter_about(seeds[0], (TOKENS, D), 1.0, 6.0, ((0, 64), (1, 8)))
    conv_weight = scatter_about(seeds[1], (3, D), 0.6, 3.0, ((1, 8),))
    mixing = scatter_about(seeds[2], (FACTORS, NB, BLOCK, 2 * BLOCK), (2 * BLOCK) ** -0.5, 0.5, ((1, 64),))
    pattern = draw_pattern(jax.random.fold_in(seeds[7], 71), 0)
    w_in = scatter_about(seeds[4], (D, HIDDEN_SIZE), D ** -0.5, 0.1875, ((1, 8),))
    w_out = scatter_about(seeds[5], (HIDDEN_SIZE, D), HIDDEN_SIZE ** -0.5, 0.09375, ((0, 8),))
    cotangent = scatter_about(seeds[6], (TOKENS, D), 1.0, 6.0, ((0, 64), (1, 8)))
    return dict(inputs=inputs, conv_weight=conv_weight, mixing=mixing, pattern=pattern, w_in=w_in, w_out=w_out, cotangent=cotangent)


root_two_pi = 0.7978845608028654

def gelu_grad(hidden):
    inner_arg = root_two_pi * (hidden + 0.044715 * hidden * hidden * hidden)
    tanh_val = jnp.tanh(inner_arg)
    slope = root_two_pi * (1.0 + 3.0 * 0.044715 * hidden * hidden)
    return 0.5 * (1.0 + tanh_val) + 0.5 * hidden * (1.0 - tanh_val * tanh_val) * slope

def reference(inputs, conv_weight, mixing, pattern, w_in, w_out, cotangent):
    length = inputs.shape[0]
    taps = conv_weight.astype(jnp.float32)
    padded = jnp.pad(inputs.astype(jnp.float32), ((1, 1), (0, 0)))
    convolved = (taps[0] * padded[:-2] + taps[1] * padded[1:-1] + taps[2] * padded[2:]).astype(jnp.bfloat16)
    nblocks = length // BLOCK
    block_ids = jnp.arange(nblocks, dtype=jnp.int32)
    group_start = block_ids // BL * BL
    partners = []
    for factor in range(LOCAL):
        partners.append((group_start + pattern[factor]).astype(jnp.int32))
    for level in range(LEVELS):
        partners.append(jnp.bitwise_xor(block_ids, BL * 2 ** level).astype(jnp.int32))
    state = convolved.reshape(nblocks, BLOCK, D)
    for factor in range(FACTORS):
        weights = mixing[factor].astype(jnp.float32)
        current = state.astype(jnp.float32)
        mates = current[partners[factor]]
        updated = jnp.einsum('bij,bjd->bid', weights[:, :, :BLOCK], current) + jnp.einsum('bij,bjd->bid', weights[:, :, BLOCK:], mates)
        state = updated.astype(jnp.bfloat16)
    mixed = state.reshape(length, D)
    hidden = jnp.dot(mixed, w_in, preferred_element_type=jnp.float32)
    activation = jax.nn.gelu(hidden, approximate=True).astype(jnp.bfloat16)
    layer_out = (mixed.astype(jnp.float32) + jnp.dot(activation, w_out, preferred_element_type=jnp.float32)).astype(jnp.bfloat16)
    grad_act = jnp.dot(cotangent, w_out.T, preferred_element_type=jnp.float32)
    grad_hidden = (grad_act * gelu_grad(hidden)).astype(jnp.bfloat16)
    grad_mixed = (cotangent.astype(jnp.float32) + jnp.dot(grad_hidden, w_in.T, preferred_element_type=jnp.float32)).astype(jnp.bfloat16)
    grads = grad_mixed.reshape(nblocks, BLOCK, D)
    for factor in reversed(range(FACTORS)):
        weights = mixing[factor].astype(jnp.float32)
        current = grads.astype(jnp.float32)
        own_term = jnp.einsum('bji,bjd->bid', weights[:, :, :BLOCK], current)
        cross_term = jnp.einsum('bji,bjd->bid', weights[:, :, BLOCK:], current)
        grads = (own_term + cross_term[partners[factor]]).astype(jnp.bfloat16)
    grad_pad = jnp.pad(grads.reshape(length, D).astype(jnp.float32), ((1, 1), (0, 0)))
    grad_input = (taps[0] * grad_pad[2:] + taps[1] * grad_pad[1:-1] + taps[2] * grad_pad[:-2]).astype(jnp.bfloat16)
    return (layer_out, convolved, grad_input)
```

```python
import functools

import jax
import jax.numpy as jnp
from jax import lax
from jax.experimental import pallas as pl
from jax.experimental.pallas import tpu as pltpu
from jax.sharding import PartitionSpec as P

BLOCK = 64
LOCAL = 2
CH = 128
TILE = 16
MESH = pl.DeviceIdType.MESH
F32 = jnp.float32
BF16 = jnp.bfloat16
root_two_pi = 0.7978845608028654


def mod(value, size):
    return lax.rem(value + size, size)


def both(first, second, axis):
    return jnp.concatenate([first, second], axis=axis)


def forward_factor(weights, state, mates):
    return [
        jnp.dot(w, both(own, mate, 0), preferred_element_type=F32).astype(BF16)
        for w, own, mate in zip(weights, state, mates)
    ]


def transposed_terms(weights, grads):
    return [
        lax.dot_general(w, g, (((0,), (0,)), ((), ())), preferred_element_type=F32)
        for w, g in zip(weights, grads)
    ]


def kernel(nb, zs, *refs):
    (
        inputs, taps_ref, mixing, pattern, w_in_hbm, w_out_hbm, cot,
        layer_out, conv_out, grad_out,
        x_v, mixl, win, wout,
        halo, ghalo, st0, sx, st1, sy, wx, wy,
        cot_all, mixed_all, hid, gact, act, ghid,
        rs_send, rs_recv, rs_own, ro_send, ro_recv, ro_own, term,
        g2, g1s, g1, g0s, g0, cross, out2,
        load_sem, halo_sem, cot_sem, wx_sem, wy_sem, sx_sem, sy_sem,
        cr_sem, mr_sem, rs_sem, ro_sem, gy_sem, gx_sem, lo_sem, gh_sem,
    ) = refs
    levels = nb.bit_length() - 1
    rows = nb * BLOCK
    far = zs // 2
    half = nb // 2
    count = nb * nb
    s = lax.axis_index("seq")
    z = lax.axis_index("ch")
    y = lax.div(s, nb)
    q = lax.rem(s, nb)
    up = mod(z + 1, zs)
    down = mod(z - 1, zs)

    loads = [
        pltpu.make_async_copy(inputs, x_v, load_sem.at[0]),
        pltpu.make_async_copy(mixing.at[pl.ds(0, LOCAL)], mixl, load_sem.at[1]),
        pltpu.make_async_copy(w_out_hbm, wout, load_sem.at[2]),
        pltpu.make_async_copy(w_in_hbm, win, load_sem.at[3]),
    ]
    for load in loads:
        load.start()

    barrier = pltpu.get_barrier_semaphore()

    def greet(seq, ch):
        pl.semaphore_signal(barrier, inc=1, device_id=(seq, ch), device_id_type=MESH)

    diagonal = jnp.where(y == q, 1, 0)
    @pl.when(s > 0)
    def _():
        greet(s - 1, z)

    @pl.when(s < count - 1)
    def _():
        greet(s + 1, z)

    for d in range(1, nb):
        greet(y * nb + mod(q + d, nb), z)
        greet(mod(y + d, nb) * nb + q, z)
    for j in range(nb):
        @pl.when(q * nb + j != s)
        def _():
            greet(q * nb + j, z)

        @pl.when(j * nb + y != s)
        def _():
            greet(j * nb + y, z)

    greet(s, up)
    greet(s, down)
    ends = jnp.where(s > 0, 1, 0) + jnp.where(s < count - 1, 1, 0)
    pl.semaphore_wait(barrier, 2 * (nb - 1) + 2 * (nb - diagonal) + 2 + ends)

    class Swap:
        def __init__(self, src, dst, sems, pick_src, pick_dst, slot, peer):
            self.src, self.dst, self.sems = src, dst, sems
            self.pick_src, self.pick_dst, self.slot, self.peer = pick_src, pick_dst, slot, peer

        def remote(self, t, into):
            return pltpu.make_async_remote_copy(
                src_ref=self.pick_src(self.src, t),
                dst_ref=self.pick_dst(self.dst, into),
                send_sem=self.sems.at[0, t],
                recv_sem=self.sems.at[1, into],
                device_id=(self.peer(t), z),
                device_id_type=MESH,
            )

        def own(self):
            return pltpu.make_async_copy(
                self.pick_src(self.src, self.slot), self.pick_dst(self.dst, self.slot), self.sems.at[1, self.slot]
            )

        def start(self):
            for d in range(1, nb):
                self.remote(mod(self.slot + d, nb), self.slot).start()
            self.own().start()

        def wait(self):
            self.own().wait()
            for d in range(1, nb):
                t = mod(self.slot + d, nb)
                self.remote(t, t).wait_recv()

        def drain(self):
            for d in range(1, nb):
                self.remote(mod(self.slot + d, nb), self.slot).wait_send()

    def first(ref, t):
        return ref.at[t]

    def over_q(src, dst, sems, pick_src=first, pick_dst=first):
        return Swap(src, dst, sems, pick_src, pick_dst, q, lambda t: y * nb + t)

    def over_y(src, dst, sems):
        return Swap(src, dst, sems, first, first, y, lambda t: t * nb + q)

    class Turn:
        def __init__(self, src, dst, sems, pick_src, pick_dst, slot, to):
            self.src, self.dst, self.sems = src, dst, sems
            self.pick_src, self.pick_dst, self.slot, self.to = pick_src, pick_dst, slot, to

        def remote(self, t, into):
            return pltpu.make_async_remote_copy(
                src_ref=self.pick_src(self.src, t),
                dst_ref=self.pick_dst(self.dst, into),
                send_sem=self.sems.at[0, t],
                recv_sem=self.sems.at[1, into],
                device_id=(self.to(t), z),
                device_id_type=MESH,
            )

        def own(self, t):
            return pltpu.make_async_copy(
                self.pick_src(self.src, t), self.pick_dst(self.dst, self.slot), self.sems.at[1, self.slot]
            )

        def start(self):
            for t in range(nb):
                @pl.when(self.to(t) != s)
                def _():
                    self.remote(t, self.slot).start()

                @pl.when(self.to(t) == s)
                def _():
                    self.own(t).start()

        def wait(self):
            for t in range(nb):
                mine = jnp.logical_and(y == q, self.slot == t)

                @pl.when(mine)
                def _():
                    self.own(t).wait()

                @pl.when(jnp.logical_not(mine))
                def _():
                    self.remote(t, t).wait_recv()

        def drain(self):
            for t in range(nb):
                @pl.when(self.to(t) != s)
                def _():
                    self.remote(t, self.slot).wait_send()

    class Gather:
        def __init__(self, buf, sems):
            self.buf, self.sems = buf, sems

        def copy(self, way, step, h, chunk):
            part = self.buf.at[chunk, pl.ds(h * half, half)]
            return pltpu.make_async_remote_copy(
                src_ref=part,
                dst_ref=part,
                send_sem=self.sems.at[0, way, step, h],
                recv_sem=self.sems.at[1, way, step, h],
                device_id=(s, up if way == 0 else down),
                device_id_type=MESH,
            )

        def halves(self, step):
            for h in range(2):
                for way in range(2):
                    if step < far - 1 or h == way:
                        yield way, h

        def chunk(self, way, step):
            return mod(z - step, zs) if way == 0 else mod(z + step, zs)

        def step(self, step):
            if step > 0:
                for h in range(2):
                    for way in range(2):
                        self.copy(way, step - 1, h, self.chunk(way, step)).wait_recv()
                        if step < far - 1 or h == way:
                            self.copy(way, step, h, self.chunk(way, step)).start()
            else:
                for way, h in self.halves(0):
                    self.copy(way, 0, h, z).start()

        def finish(self):
            for way, h in self.halves(far - 1):
                self.copy(way, far - 1, h, self.chunk(way, far)).wait_recv()

        def drain(self):
            for step in range(far):
                for way, h in self.halves(step):
                    self.copy(way, step, h, self.chunk(way, step)).wait_send()

    class Scatter:
        def __init__(self, send, recv, own, sems, pair):
            self.send, self.recv, self.own, self.sems, self.pair = send, recv, own, sems, pair

        def copy(self, way, step, h):
            return pltpu.make_async_remote_copy(
                src_ref=self.send.at[way, step, pl.ds(h * half, half)],
                dst_ref=self.recv.at[way, step, pl.ds(h * half, half)],
                send_sem=self.sems.at[0, way, step, h],
                recv_sem=self.sems.at[1, way, step, h],
                device_id=(s, up if way == 0 else down),
                device_id_type=MESH,
            )

        def arrived(self, way, step, h):
            if step < 0 or (step == 0 and h != way):
                return None
            self.copy(way, step, h).wait_recv()
            return self.recv[way, step, pl.ds(h * half, half)].astype(F32).reshape(half * BLOCK, CH)

        def stage(self, k):
            step = far - k
            near = z if k == far else mod(z - k, zs)
            term[...] = self.pair(mod(z + k, zs), near)
            for h in range(2):
                lines = pl.ds(h * half * BLOCK, half * BLOCK)
                if k == far:
                    value = term[lines, pl.ds(0, CH)]
                    self.send[h, step, pl.ds(h * half, half)] = value.astype(BF16).reshape(half, BLOCK, CH)
                    self.copy(h, step, h).start()
                    self.own[lines, :] = term[lines, pl.ds(CH, CH)]
                    continue
                for way in range(2):
                    value = term[lines, pl.ds(way * CH, CH)]
                    came = self.arrived(way, step - 1, h)
                    if came is not None:
                        value = value + came
                    self.send[way, step, pl.ds(h * half, half)] = value.astype(BF16).reshape(half, BLOCK, CH)
                    self.copy(way, step, h).start()

        def finish(self):
            totals = []
            for h in range(2):
                value = self.own[pl.ds(h * half * BLOCK, half * BLOCK), :]
                for way in range(2):
                    came = self.arrived(way, far - 1, h)
                    if came is not None:
                        value = value + came
                totals.append(value)
            return both(totals[0], totals[1], 0)

        def drain(self):
            for step in range(far):
                for h in range(2):
                    for way in range(2):
                        if step > 0 or h == way:
                            self.copy(way, step, h).wait_send()

    def rim(src_head, src_tail, dst, sems):
        return (
            pltpu.make_async_remote_copy(
                src_ref=src_tail, dst_ref=dst.at[0], send_sem=sems.at[0, 0], recv_sem=sems.at[1, 0],
                device_id=(s + 1, z), device_id_type=MESH,
            ),
            pltpu.make_async_remote_copy(
                src_ref=src_head, dst_ref=dst.at[1], send_sem=sems.at[0, 1], recv_sem=sems.at[1, 1],
                device_id=(s - 1, z), device_id_type=MESH,
            ),
        )

    def rim_start(pair, dst):
        @pl.when(s < count - 1)
        def _():
            pair[0].start()

        @pl.when(s > 0)
        def _():
            pair[1].start()

        @pl.when(s == 0)
        def _():
            dst[0] = jnp.zeros((TILE, CH), BF16)

        @pl.when(s == count - 1)
        def _():
            dst[1] = jnp.zeros((TILE, CH), BF16)

    def rim_wait(pair):
        @pl.when(s > 0)
        def _():
            pair[0].wait_recv()

        @pl.when(s < count - 1)
        def _():
            pair[1].wait_recv()

    def rim_drain(pair):
        @pl.when(s < count - 1)
        def _():
            pair[0].wait_send()

        @pl.when(s > 0)
        def _():
            pair[1].wait_send()

    def convolve(value, edges, before, same, after):
        value = value.astype(F32)
        line = lax.broadcasted_iota(jnp.int32, value.shape, 0)
        above = edges[0].astype(F32)[TILE - 1 : TILE, :]
        below = edges[1].astype(F32)[0:1, :]
        earlier = jnp.where(line == 0, above, pltpu.roll(value, 1, 0))
        later = jnp.where(line == rows - 1, below, pltpu.roll(value, rows - 1, 0))
        return (before * earlier + same * value + after * later).astype(BF16)

    def put(ref, blocks):
        for i, block in enumerate(blocks):
            ref[i] = block

    def forward_levels(weights, state):
        for level in range(levels):
            state = forward_factor(
                [weights[level, i] for i in range(nb)], state, [state[i ^ (1 << level)] for i in range(nb)]
            )
        return state

    def backward_levels(weights, grads):
        for level in reversed(range(levels)):
            terms = transposed_terms([weights[level, i] for i in range(nb)], grads)
            grads = [
                (terms[i][:BLOCK] + terms[i ^ (1 << level)][BLOCK:]).astype(BF16) for i in range(nb)
            ]
        return grads

    edges = rim(inputs.at[pl.ds(0, TILE)], inputs.at[pl.ds(rows - TILE, TILE)], halo, halo_sem)
    rim_start(edges, halo)
    cot_turn = Turn(
        cot, cot_all, cot_sem,
        lambda ref, t: ref.at[pl.ds(t * BLOCK, BLOCK)],
        lambda ref, t: ref.at[z, t], y, lambda t: q * nb + t,
    )
    cot_turn.start()
    wx_swap = over_q(
        mixing, wx, wx_sem,
        lambda ref, t: ref.at[pl.ds(LOCAL, levels), t],
        lambda ref, t: ref.at[pl.ds(0, levels), t],
    )
    wx_swap.start()
    wy_turn = Turn(
        mixing, wy, wy_sem,
        lambda ref, t: ref.at[pl.ds(LOCAL + levels, levels), t],
        lambda ref, t: ref.at[pl.ds(0, levels), t], y, lambda t: q * nb + t,
    )

    taps = taps_ref[...].astype(F32)
    tap0, tap1, tap2 = taps[0:1], taps[1:2], taps[2:3]
    loads[0].wait()
    rim_wait(edges)
    convolved = convolve(x_v[...], (halo[0], halo[1]), tap0, tap1, tap2)
    conv_out[...] = convolved
    st0[...] = convolved.reshape(nb, BLOCK, CH)
    loads[1].wait()
    for factor in range(LOCAL):
        state = [st0[i] for i in range(nb)]
        mates = [st0[pattern[factor, i]] for i in range(nb)]
        put(st0, forward_factor([mixl[factor, i] for i in range(nb)], state, mates))

    sx_swap = over_q(st0, sx, sx_sem)
    sx_swap.start()
    wy_turn.start()
    cot_turn.wait()
    cot_ring = Gather(cot_all, cr_sem)
    cot_ring.step(0)
    wx_swap.wait()
    sx_swap.wait()
    put(st1, forward_levels(wx, [sx[i] for i in range(nb)]))

    sy_swap = over_y(st1, sy, sy_sem)
    sy_swap.start()
    cot_ring.step(1) if far > 1 else None
    wy_turn.wait()
    sy_swap.wait()
    mixed = forward_levels(wy, [sy[i] for i in range(nb)])
    for i in range(nb):
        mixed_all[z, i] = mixed[i]
    mixed_ring = Gather(mixed_all, mr_sem)
    mixed_ring.step(0)

    def chunks(buf, first_chunk, second_chunk):
        return both(buf[first_chunk].reshape(rows, CH), buf[second_chunk].reshape(rows, CH), 1)

    def channels(index):
        return pl.ds(pl.multiple_of(index * CH, CH), CH)

    def add_grad_act(a, b, start):
        value = lax.dot_general(
            chunks(cot_all, a, b), both(wout[:, channels(a)], wout[:, channels(b)], 1),
            (((1,), (1,)), ((), ())), preferred_element_type=F32,
        )
        gact[...] = value if start else gact[...] + value

    def add_hidden(a, b, start):
        value = jnp.dot(
            chunks(mixed_all, a, b), both(win[channels(a), :], win[channels(b), :], 0),
            preferred_element_type=F32,
        )
        hid[...] = value if start else hid[...] + value

    loads[2].wait()
    loads[3].wait()
    for step in range(1, far):
        if step > 1:
            cot_ring.step(step)
        add_grad_act(mod(z - step, zs), mod(z + step, zs), step == 1)
        mixed_ring.step(step)
        add_hidden(mod(z - step, zs), mod(z + step, zs), step == 1)
    cot_ring.finish()
    add_grad_act(z, mod(z + far, zs), far == 1)
    mixed_ring.finish()
    add_hidden(z, mod(z + far, zs), far == 1)

    @pl.loop(0, nb)
    def _(i):
        lines = pl.ds(pl.multiple_of(i * BLOCK, BLOCK), BLOCK)
        v = hid[lines, :]
        square = v * v
        tanh_val = jnp.tanh(root_two_pi * (v + 0.044715 * square * v))
        plus = 0.5 * (1.0 + tanh_val)
        act[lines, :] = (v * plus).astype(BF16)
        slope = root_two_pi * (1.0 + 3.0 * 0.044715 * square)
        slope = plus + 0.5 * v * (1.0 - tanh_val * tanh_val) * slope
        ghid[lines, :] = (gact[lines, :] * slope).astype(BF16)

    def grad_pair(a, b):
        return lax.dot_general(
            ghid[...], both(win[channels(a), :], win[channels(b), :], 0),
            (((1,), (1,)), ((), ())), preferred_element_type=F32,
        )

    def out_pair(a, b):
        return jnp.dot(
            act[...], both(wout[:, channels(a)], wout[:, channels(b)], 1), preferred_element_type=F32
        )

    grad_sum = Scatter(rs_send, rs_recv, rs_own, rs_sem, grad_pair)
    out_sum = Scatter(ro_send, ro_recv, ro_own, ro_sem, out_pair)
    for k in range(far, 0, -1):
        grad_sum.stage(k)
    out_sum.stage(far)
    total = grad_sum.finish()
    grad_mixed = (cot_all[z].astype(F32).reshape(rows, CH) + total).astype(BF16).reshape(nb, BLOCK, CH)

    put(g2, backward_levels(wy, [grad_mixed[i] for i in range(nb)]))
    gy_swap = over_y(g2, g1, gy_sem)
    gy_swap.start()
    rest = list(range(far - 1, 0, -1))
    for k in rest[:2]:
        out_sum.stage(k)
    gy_swap.wait()
    put(g1s, backward_levels(wx, [g1[i] for i in range(nb)]))
    gx_swap = over_q(g1s, g0, gx_sem)
    gx_swap.start()
    for k in rest[2:]:
        out_sum.stage(k)
    gx_swap.wait()
    grads = [g0[i] for i in range(nb)]
    for factor in reversed(range(LOCAL)):
        terms = transposed_terms([mixl[factor, i] for i in range(nb)], grads)
        put(cross, [t[BLOCK:] for t in terms])
        grads = [(terms[i][:BLOCK] + cross[pattern[factor, i]]).astype(BF16) for i in range(nb)]
    put(g0s, grads)
    gedges = rim(
        g0s.at[0, pl.ds(0, TILE)], g0s.at[nb - 1, pl.ds(BLOCK - TILE, TILE)], ghalo, gh_sem
    )
    rim_start(gedges, ghalo)
    branch = out_sum.finish()
    put_mixed = (mixed_all[z].astype(F32).reshape(rows, CH) + branch).astype(BF16)
    out2[...] = put_mixed.reshape(nb, BLOCK, CH)
    lo_turn = Turn(
        out2, layer_out, lo_sem, first,
        lambda ref, t: ref.at[pl.ds(t * BLOCK, BLOCK)], q, lambda t: t * nb + y,
    )
    lo_turn.start()
    rim_wait(gedges)
    grad_out[...] = convolve(g0s[...].reshape(rows, CH), (ghalo[0], ghalo[1]), tap2, tap1, tap0)
    lo_turn.wait()

    rim_drain(edges)
    rim_drain(gedges)
    for transfer in (
        cot_turn, wx_swap, wy_turn, sx_swap, sy_swap, cot_ring, mixed_ring,
        grad_sum, out_sum, gy_swap, gx_swap, lo_turn,
    ):
        transfer.drain()


def on_device(nb, zs, inputs, conv_weight, mixing, pattern, w_in, w_out, cotangent):
    rows, _ = inputs.shape
    levels = nb.bit_length() - 1
    hidden = w_in.shape[1]
    channels = w_in.shape[0]
    far = zs // 2
    vmem = pltpu.VMEM
    dma = pltpu.SemaphoreType.DMA
    blocks = (nb, BLOCK, CH)
    scratch = [
        vmem((rows, CH), BF16),
        vmem((LOCAL, *blocks), BF16),
        vmem((channels, hidden), BF16),
        vmem((hidden, channels), BF16),
        vmem((2, TILE, CH), BF16),
        vmem((2, TILE, CH), BF16),
        *[vmem(blocks, BF16)] * 4,
        *[vmem((levels, *blocks), BF16)] * 2,
        *[vmem((zs, *blocks), BF16)] * 2,
        *[vmem((rows, hidden), F32)] * 2,
        *[vmem((rows, hidden), BF16)] * 2,
        *[vmem((2, far, *blocks), BF16)] * 2,
        vmem((rows, CH), F32),
        *[vmem((2, far, *blocks), BF16)] * 2,
        vmem((rows, CH), F32),
        vmem((rows, 2 * CH), F32),
        *[vmem(blocks, BF16)] * 5,
        vmem(blocks, F32),
        vmem(blocks, BF16),
        dma((4,)),
        dma((2, 2)),
        *[dma((2, nb))] * 5,
        *[dma((2, 2, far, 2))] * 4,
        *[dma((2, nb))] * 3,
        dma((2, 2)),
    ]
    out = jax.ShapeDtypeStruct((rows, CH), BF16)
    hbm = pl.BlockSpec(memory_space=pl.ANY)
    local = pl.BlockSpec(memory_space=pltpu.VMEM)
    return pl.pallas_call(
        functools.partial(kernel, nb, zs),
        out_shape=(out, out, out),
        in_specs=[hbm, local, hbm, pl.BlockSpec(memory_space=pltpu.SMEM), hbm, hbm, hbm],
        out_specs=(local, local, local),
        scratch_shapes=scratch,
        compiler_params=pltpu.CompilerParams(
            collective_id=0, has_side_effects=True, vmem_limit_bytes=56 * 1024 * 1024
        ),
    )(inputs, conv_weight, mixing, pattern, w_in, w_out, cotangent)


def solution(mesh):
    seq, zs = mesh.shape["seq"], mesh.shape["ch"]
    nb = 1 << ((seq.bit_length() - 1) // 2)
    return jax.shard_map(
        functools.partial(on_device, nb, zs),
        mesh=mesh,
        in_specs=(
            P("seq", "ch"),
            P(None, "ch"),
            P(None, "seq", None, None),
            P(None, "seq"),
            P(None, "ch"),
            P("ch", None),
            P("seq", "ch"),
        ),
        out_specs=(P("seq", "ch"), P("seq", "ch"), P("seq", "ch")),
        check_vma=False,
    )
```

```python
import functools

import jax
import jax.numpy as jnp
from jax import lax
from jax.experimental import pallas as pl
from jax.experimental.pallas import tpu as pltpu
from jax.sharding import PartitionSpec as P

BLOCK = 64
LOCAL = 2
CH = 128
TILE = 16
SPLIT = BLOCK // TILE
MESH = pl.DeviceIdType.MESH
F32 = jnp.float32
BF16 = jnp.bfloat16
root_two_pi = 0.7978845608028654


def mod(value, size):
    return lax.rem(value + size, size)


def both(first, second, axis):
    return jnp.concatenate([first, second], axis=axis)


def forward_factor(weights, state, mates):
    return [
        jnp.dot(w, both(own, mate, 0), preferred_element_type=F32).astype(BF16)
        for w, own, mate in zip(weights, state, mates)
    ]


def transposed_terms(weights, grads):
    return [
        lax.dot_general(w, g, (((0,), (0,)), ((), ())), preferred_element_type=F32)
        for w, g in zip(weights, grads)
    ]


def kernel(nb, zs, *refs):
    (
        inputs, taps_hbm, mixing, pattern_hbm, w_in_hbm, w_out_hbm, cot,
        layer_out, conv_out, grad_out,
        x_v, cv, taps_ref, pattern, mixl, win, wout,
        halo, ghalo, st0, sx, st1, sy, wx, wy, wq,
        cot_all, mixed_all, hid, ga0, ga1, ga2, act, ghid,
        rs_send, rs_recv, rs_own, ro_send, ro_recv, ro_own, term,
        g2, g1s, g1, g0s, g0, cross, out2, cs1, cs2, go_v,
        load_sem, save_sem, halo_sem, wx_sem, wq_sem, wr_sem, wz_sem, sx_sem, sy_sem,
        cr_sem, mr_sem, rs_sem, ro_sem, ax_sem, ay_sem, cx_sem, cy_sem,
        gy_sem, gx_sem, lo_sem, gh_sem,
    ) = refs
    levels = nb.bit_length() - 1
    rows = nb * BLOCK
    far = zs // 2
    parts = min(4, nb)
    size = nb // parts
    lines_of = size * BLOCK
    count = nb * nb
    s = lax.axis_index("seq")
    z = lax.axis_index("ch")
    y = lax.div(s, nb)
    q = lax.rem(s, nb)
    up = mod(z + 1, zs)
    down = mod(z - 1, zs)
    up2 = mod(z + 2, zs)
    down2 = mod(z - 2, zs)
    quarter = lax.rem(z, SPLIT)
    strip = pl.ds(pl.multiple_of(quarter * TILE, TILE), TILE)

    loads = [
        pltpu.make_async_copy(inputs, x_v, load_sem.at[0]),
        pltpu.make_async_copy(mixing.at[pl.ds(0, LOCAL)], mixl, load_sem.at[1]),
        pltpu.make_async_copy(w_out_hbm, wout, load_sem.at[2]),
        pltpu.make_async_copy(w_in_hbm, win, load_sem.at[3]),
        pltpu.make_async_copy(taps_hbm, taps_ref, load_sem.at[4]),
        pltpu.make_async_copy(pattern_hbm, pattern, load_sem.at[5]),
    ]
    for load in loads:
        load.start()

    barrier = pltpu.get_barrier_semaphore()

    def greet(seq, ch):
        pl.semaphore_signal(barrier, inc=1, device_id=(seq, ch), device_id_type=MESH)

    @pl.when(s > 0)
    def _():
        greet(s - 1, z)

    @pl.when(s < count - 1)
    def _():
        greet(s + 1, z)

    for d in range(1, nb):
        greet(y * nb + mod(q + d, nb), z)
        greet(mod(y + d, nb) * nb + q, z)
    greet(s, up)
    greet(s, down)
    greet(s, up2)
    greet(s, down2)
    ends = jnp.where(s > 0, 1, 0) + jnp.where(s < count - 1, 1, 0)
    pl.semaphore_wait(barrier, 2 * (nb - 1) + 4 + ends)

    class Swap:
        def __init__(self, src, dst, sems, pick_src, pick_dst, slot, peer):
            self.src, self.dst, self.sems = src, dst, sems
            self.pick_src, self.pick_dst, self.slot, self.peer = pick_src, pick_dst, slot, peer

        def remote(self, t, into):
            return pltpu.make_async_remote_copy(
                src_ref=self.pick_src(self.src, t),
                dst_ref=self.pick_dst(self.dst, into),
                send_sem=self.sems.at[0, t],
                recv_sem=self.sems.at[1, into],
                device_id=(self.peer(t), z),
                device_id_type=MESH,
            )

        def own(self):
            return pltpu.make_async_copy(
                self.pick_src(self.src, self.slot), self.pick_dst(self.dst, self.slot), self.sems.at[1, self.slot]
            )

        def start(self):
            for d in range(1, nb):
                self.remote(mod(self.slot + d, nb), self.slot).start()
            self.own().start()

        def wait(self):
            self.own().wait()
            for d in range(1, nb):
                t = mod(self.slot + d, nb)
                self.remote(t, t).wait_recv()

        def drain(self):
            for d in range(1, nb):
                self.remote(mod(self.slot + d, nb), self.slot).wait_send()

    def first(ref, t):
        return ref.at[t]

    def over_q(src, dst, sems, pick_src=first, pick_dst=first):
        return Swap(src, dst, sems, pick_src, pick_dst, q, lambda t: y * nb + t)

    def over_y(src, dst, sems, pick_src=first, pick_dst=first):
        return Swap(src, dst, sems, pick_src, pick_dst, y, lambda t: t * nb + q)

    class Turn:
        def __init__(self, src, dst, sems, pick_src, pick_dst, slot, to):
            self.src, self.dst, self.sems = src, dst, sems
            self.pick_src, self.pick_dst, self.slot, self.to = pick_src, pick_dst, slot, to

        def remote(self, t, into):
            return pltpu.make_async_remote_copy(
                src_ref=self.pick_src(self.src, t),
                dst_ref=self.pick_dst(self.dst, into),
                send_sem=self.sems.at[0, t],
                recv_sem=self.sems.at[1, into],
                device_id=(self.to(t), z),
                device_id_type=MESH,
            )

        def own(self, t):
            return pltpu.make_async_copy(
                self.pick_src(self.src, t), self.pick_dst(self.dst, self.slot), self.sems.at[1, self.slot]
            )

        def start(self):
            for t in range(nb):
                @pl.when(self.to(t) != s)
                def _():
                    self.remote(t, self.slot).start()

                @pl.when(self.to(t) == s)
                def _():
                    self.own(t).start()

        def wait(self):
            for t in range(nb):
                mine = jnp.logical_and(y == q, self.slot == t)

                @pl.when(mine)
                def _():
                    self.own(t).wait()

                @pl.when(jnp.logical_not(mine))
                def _():
                    self.remote(t, t).wait_recv()

        def drain(self):
            for t in range(nb):
                @pl.when(self.to(t) != s)
                def _():
                    self.remote(t, self.slot).wait_send()

    def ours(way, p):
        return (p < parts // 2) == (way == 0)

    class Gather:
        def __init__(self, pick, first_pick, sems):
            self.pick, self.first_pick, self.sems = pick, first_pick, sems

        def copy(self, way, step, p, chunk):
            part = self.pick(chunk, p)
            return pltpu.make_async_remote_copy(
                src_ref=self.first_pick(p) if step == 0 else part,
                dst_ref=part,
                send_sem=self.sems.at[0, way, step, p],
                recv_sem=self.sems.at[1, way, step, p],
                device_id=(s, up if way == 0 else down),
                device_id_type=MESH,
            )

        def chunk(self, way, step):
            return mod(z - step, zs) if way == 0 else mod(z + step, zs)

        def each(self, step):
            for p in range(parts):
                for way in range(2):
                    if step < far - 1 or ours(way, p):
                        yield way, p

        def came(self, way, step, p):
            part = self.pick(self.chunk(way, step + 1), p)
            return pltpu.make_async_remote_copy(
                src_ref=part,
                dst_ref=part,
                send_sem=self.sems.at[0, way, step, p],
                recv_sem=self.sems.at[1, way, step, p],
                device_id=(s, up if way == 0 else down),
                device_id_type=MESH,
            )

        def step(self, step):
            for p in range(parts):
                for way in range(2):
                    if step > 0:
                        self.came(way, step - 1, p).wait_recv()
                    if step < far - 1 or ours(way, p):
                        self.copy(way, step, p, self.chunk(way, step)).start()

        def finish(self):
            for way, p in self.each(far - 1):
                self.came(way, far - 1, p).wait_recv()

        def drain(self):
            for step in range(far):
                for way, p in self.each(step):
                    self.copy(way, step, p, self.chunk(way, step)).wait_send()

    class Scatter:
        def __init__(self, send, recv, own, sems, pair):
            self.send, self.recv, self.own, self.sems, self.pair = send, recv, own, sems, pair

        def copy(self, way, step, p):
            return pltpu.make_async_remote_copy(
                src_ref=self.send.at[way, step, pl.ds(p * size, size)],
                dst_ref=self.recv.at[way, step, pl.ds(p * size, size)],
                send_sem=self.sems.at[0, way, step, p],
                recv_sem=self.sems.at[1, way, step, p],
                device_id=(s, up if way == 0 else down),
                device_id_type=MESH,
            )

        def arrived(self, way, step, p):
            if step < 0 or (step == 0 and not ours(way, p)):
                return None
            self.copy(way, step, p).wait_recv()
            return self.recv[way, step, pl.ds(p * size, size)].astype(F32).reshape(lines_of, CH)

        def stage(self, k):
            step = far - k
            near = z if k == far else mod(z - k, zs)
            term[...] = self.pair(mod(z + k, zs), near)
            for p in range(parts):
                lines = pl.ds(p * lines_of, lines_of)
                for way in range(2):
                    if k == far:
                        if not ours(way, p):
                            continue
                        value = term[lines, pl.ds(0, CH)]
                    else:
                        value = term[lines, pl.ds(way * CH, CH)]
                        came = self.arrived(way, step - 1, p)
                        if came is not None:
                            value = value + came
                    self.send[way, step, pl.ds(p * size, size)] = value.astype(BF16).reshape(size, BLOCK, CH)
                    self.copy(way, step, p).start()
            if k == far:
                self.own[...] = term[:, pl.ds(CH, CH)]

        def finish(self):
            totals = []
            for p in range(parts):
                value = self.own[pl.ds(p * lines_of, lines_of), :]
                for way in range(2):
                    came = self.arrived(way, far - 1, p)
                    if came is not None:
                        value = value + came
                totals.append(value)
            return jnp.concatenate(totals, axis=0)

        def drain(self):
            for step in range(far):
                for p in range(parts):
                    for way in range(2):
                        if step > 0 or ours(way, p):
                            self.copy(way, step, p).wait_send()

    class Spread:
        def __init__(self):
            hb = nb // 2
            self.cases = [
                (up, down, 1, pl.ds(0, nb)), (down, up, -1, pl.ds(0, nb)),
                (up2, down2, 2, pl.ds(0, hb)), (down2, up2, -2, pl.ds(hb, hb)),
            ]

        def copy(self, case, theirs):
            to, _, shift, slots = self.cases[case]
            index = lax.rem(quarter - shift + 2 * SPLIT, SPLIT) if theirs else quarter
            part = wy.at[pl.ds(0, levels), slots, pl.ds(pl.multiple_of(index * TILE, TILE), TILE)]
            return pltpu.make_async_remote_copy(
                src_ref=part, dst_ref=part, send_sem=wz_sem.at[0, case], recv_sem=wz_sem.at[1, case],
                device_id=(s, to), device_id_type=MESH,
            )

        def start(self):
            for case in range(4):
                self.copy(case, False).start()

        def wait(self):
            for case in range(4):
                self.copy(case, True).wait_recv()

        def drain(self):
            for case in range(4):
                self.copy(case, False).wait_send()

    def rim(src_head, src_tail, dst, sems):
        return (
            pltpu.make_async_remote_copy(
                src_ref=src_tail, dst_ref=dst.at[0], send_sem=sems.at[0, 0], recv_sem=sems.at[1, 0],
                device_id=(s + 1, z), device_id_type=MESH,
            ),
            pltpu.make_async_remote_copy(
                src_ref=src_head, dst_ref=dst.at[1], send_sem=sems.at[0, 1], recv_sem=sems.at[1, 1],
                device_id=(s - 1, z), device_id_type=MESH,
            ),
        )

    def rim_start(pair, dst):
        @pl.when(s < count - 1)
        def _():
            pair[0].start()

        @pl.when(s > 0)
        def _():
            pair[1].start()

        @pl.when(s == 0)
        def _():
            dst[0] = jnp.zeros((TILE, CH), BF16)

        @pl.when(s == count - 1)
        def _():
            dst[1] = jnp.zeros((TILE, CH), BF16)

    def rim_wait(pair):
        @pl.when(s > 0)
        def _():
            pair[0].wait_recv()

        @pl.when(s < count - 1)
        def _():
            pair[1].wait_recv()

    def rim_drain(pair):
        @pl.when(s < count - 1)
        def _():
            pair[0].wait_send()

        @pl.when(s > 0)
        def _():
            pair[1].wait_send()

    def convolve(value, edges, before, same, after):
        value = value.astype(F32)
        line = lax.broadcasted_iota(jnp.int32, value.shape, 0)
        above = edges[0].astype(F32)[TILE - 1 : TILE, :]
        below = edges[1].astype(F32)[0:1, :]
        earlier = jnp.where(line == 0, above, pltpu.roll(value, 1, 0))
        later = jnp.where(line == rows - 1, below, pltpu.roll(value, rows - 1, 0))
        return (before * earlier + same * value + after * later).astype(BF16)

    def put(ref, blocks):
        for i, block in enumerate(blocks):
            ref[i] = block

    def forward_levels(weights, state):
        for level in range(levels):
            state = forward_factor(
                [weights[level, i] for i in range(nb)], state, [state[i ^ (1 << level)] for i in range(nb)]
            )
        return state

    def backward_levels(weights, grads):
        for level in reversed(range(levels)):
            terms = transposed_terms([weights[level, i] for i in range(nb)], grads)
            grads = [
                (terms[i][:BLOCK] + terms[i ^ (1 << level)][BLOCK:]).astype(BF16) for i in range(nb)
            ]
        return grads

    edges = rim(inputs.at[pl.ds(0, TILE)], inputs.at[pl.ds(rows - TILE, TILE)], halo, halo_sem)
    rim_start(edges, halo)
    cot_ring = Gather(
        lambda chunk, p: cot_all.at[chunk, pl.ds(p * lines_of, lines_of)],
        lambda p: cot.at[pl.ds(p * lines_of, lines_of)], cr_sem,
    )
    cot_ring.step(0)
    own_cot = pltpu.make_async_copy(cot, cot_all.at[z], load_sem.at[6])
    own_cot.start()
    wq_swap = over_q(
        mixing, wq, wq_sem,
        lambda ref, t: ref.at[pl.ds(LOCAL + levels, levels), t, strip],
        lambda ref, t: ref.at[pl.ds(0, levels), t],
    )
    wq_swap.start()
    wx_swap = over_q(
        mixing, wx, wx_sem,
        lambda ref, t: ref.at[pl.ds(LOCAL, levels), t],
        lambda ref, t: ref.at[pl.ds(0, levels), t],
    )
    wx_swap.start()

    loads[4].wait()
    taps = taps_ref[...].astype(F32)
    tap0, tap1, tap2 = taps[0:1], taps[1:2], taps[2:3]
    loads[0].wait()
    rim_wait(edges)
    cv[...] = convolve(x_v[...], (halo[0], halo[1]), tap0, tap1, tap2)
    conv_save = pltpu.make_async_copy(cv, conv_out, save_sem.at[0])
    conv_save.start()
    st0[...] = cv[...].reshape(nb, BLOCK, CH)
    loads[1].wait()
    loads[5].wait()
    for factor in range(LOCAL):
        state = [st0[i] for i in range(nb)]
        mates = [st0[pattern[factor, i]] for i in range(nb)]
        put(st0, forward_factor([mixl[factor, i] for i in range(nb)], state, mates))

    sx_swap = over_q(st0, sx, sx_sem)
    sx_swap.start()
    if far > 1:
        cot_ring.step(1)
    wq_swap.wait()
    wr_swap = over_y(
        wq, wy, wr_sem,
        lambda ref, t: ref.at[pl.ds(0, levels), t],
        lambda ref, t: ref.at[pl.ds(0, levels), t, strip],
    )
    wr_swap.start()
    if far > 2:
        cot_ring.step(2)
    wx_swap.wait()
    sx_swap.wait()
    put(st1, forward_levels(wx, [sx[i] for i in range(nb)]))

    sy_swap = over_y(st1, sy, sy_sem)
    sy_swap.start()
    for step in range(3, far):
        cot_ring.step(step)
    wr_swap.wait()
    spread = Spread()
    spread.start()

    def channels(index):
        return pl.ds(pl.multiple_of(index * CH, CH), CH)

    cot_ring.finish()
    own_cot.wait()
    loads[2].wait()
    value = None
    for c in range(0, zs, 2):
        part = lax.dot_general(
            both(cot_all[c], cot_all[c + 1], 1), wout[:, pl.ds(c * CH, 2 * CH)],
            (((1,), (1,)), ((), ())), preferred_element_type=F32,
        )
        value = part if value is None else value + part
    ga0[...] = value.astype(BF16).reshape(ga0.shape)
    ax_swap = over_q(ga0, ga1, ax_sem)
    ax_swap.start()
    cx_swap = over_q(cot, cs1, cx_sem, lambda ref, t: ref.at[pl.ds(t * BLOCK, BLOCK)])
    cx_swap.start()
    sy_swap.wait()
    spread.wait()
    mixed = forward_levels(wy, [sy[i] for i in range(nb)])
    for i in range(nb):
        mixed_all[z, i] = mixed[i]
    mixed_ring = Gather(
        lambda chunk, p: mixed_all.at[chunk, pl.ds(p * size, size)],
        lambda p: mixed_all.at[z, pl.ds(p * size, size)], mr_sem,
    )
    mixed_ring.step(0)

    def add_hidden(a, b, start):
        value = jnp.dot(
            both(mixed_all[a].reshape(rows, CH), mixed_all[b].reshape(rows, CH), 1),
            both(win[channels(a), :], win[channels(b), :], 0),
            preferred_element_type=F32,
        )
        hid[...] = value if start else hid[...] + value

    ax_swap.wait()
    ay_swap = over_y(ga1, ga2, ay_sem)
    ay_swap.start()
    cx_swap.wait()
    cy_swap = over_y(cs1, cs2, cy_sem)
    cy_swap.start()
    loads[3].wait()
    for step in range(1, far):
        mixed_ring.step(step)
        add_hidden(mod(z - step, zs), mod(z + step, zs), step == 1)
    mixed_ring.finish()
    add_hidden(z, mod(z + far, zs), far == 1)
    ay_swap.wait()

    @pl.loop(0, nb)
    def _(i):
        lines = pl.ds(pl.multiple_of(i * BLOCK, BLOCK), BLOCK)
        v = hid[lines, :]
        square = v * v
        tanh_val = jnp.tanh(root_two_pi * (v + 0.044715 * square * v))
        plus = 0.5 * (1.0 + tanh_val)
        act[lines, :] = (v * plus).astype(BF16)
        slope = root_two_pi * (1.0 + 3.0 * 0.044715 * square)
        slope = plus + 0.5 * v * (1.0 - tanh_val * tanh_val) * slope
        ghid[lines, :] = (ga2[i].astype(F32) * slope).astype(BF16)

    def grad_pair(a, b):
        return lax.dot_general(
            ghid[...], both(win[channels(a), :], win[channels(b), :], 0),
            (((1,), (1,)), ((), ())), preferred_element_type=F32,
        )

    def out_pair(a, b):
        return jnp.dot(
            act[...], both(wout[:, channels(a)], wout[:, channels(b)], 1), preferred_element_type=F32
        )

    grad_sum = Scatter(rs_send, rs_recv, rs_own, rs_sem, grad_pair)
    out_sum = Scatter(ro_send, ro_recv, ro_own, ro_sem, out_pair)
    for k in range(far, 0, -1):
        grad_sum.stage(k)
    out_sum.stage(far)
    cy_swap.wait()
    total = grad_sum.finish()
    grad_mixed = (cs2[...].astype(F32).reshape(rows, CH) + total).astype(BF16).reshape(nb, BLOCK, CH)

    put(g2, backward_levels(wy, [grad_mixed[i] for i in range(nb)]))
    gy_swap = over_y(g2, g1, gy_sem)
    gy_swap.start()
    rest = list(range(far - 1, 0, -1))
    for k in rest[:2]:
        out_sum.stage(k)
    gy_swap.wait()
    put(g1s, backward_levels(wx, [g1[i] for i in range(nb)]))
    gx_swap = over_q(g1s, g0, gx_sem)
    gx_swap.start()
    for k in rest[2:]:
        out_sum.stage(k)
    gx_swap.wait()
    grads = [g0[i] for i in range(nb)]
    for factor in reversed(range(LOCAL)):
        terms = transposed_terms([mixl[factor, i] for i in range(nb)], grads)
        put(cross, [t[BLOCK:] for t in terms])
        grads = [(terms[i][:BLOCK] + cross[pattern[factor, i]]).astype(BF16) for i in range(nb)]
    put(g0s, grads)
    gedges = rim(
        g0s.at[0, pl.ds(0, TILE)], g0s.at[nb - 1, pl.ds(BLOCK - TILE, TILE)], ghalo, gh_sem
    )
    rim_start(gedges, ghalo)
    branch = out_sum.finish()
    whole = (mixed_all[z].astype(F32).reshape(rows, CH) + branch).astype(BF16)
    out2[...] = whole.reshape(nb, BLOCK, CH)
    lo_turn = Turn(
        out2, layer_out, lo_sem, first,
        lambda ref, t: ref.at[pl.ds(t * BLOCK, BLOCK)], q, lambda t: t * nb + y,
    )
    lo_turn.start()
    rim_wait(gedges)
    go_v[...] = convolve(g0s[...].reshape(rows, CH), (ghalo[0], ghalo[1]), tap2, tap1, tap0)
    grad_save = pltpu.make_async_copy(go_v, grad_out, save_sem.at[1])
    grad_save.start()

    rim_drain(edges)
    rim_drain(gedges)
    for transfer in (
        wq_swap, wx_swap, wr_swap, spread, sx_swap, sy_swap, ax_swap, ay_swap, cx_swap, cy_swap,
        cot_ring, mixed_ring, grad_sum, out_sum, gy_swap, gx_swap, lo_turn,
    ):
        transfer.drain()
    conv_save.wait()
    lo_turn.wait()
    grad_save.wait()


def on_device(nb, zs, inputs, conv_weight, mixing, pattern, w_in, w_out, cotangent):
    rows, _ = inputs.shape
    levels = nb.bit_length() - 1
    hidden = w_in.shape[1]
    channels = w_in.shape[0]
    far = zs // 2
    vmem = pltpu.VMEM
    dma = pltpu.SemaphoreType.DMA
    blocks = (nb, BLOCK, CH)
    parts = min(4, nb)
    deep = (nb, BLOCK, hidden)
    scratch = [
        vmem((rows, CH), BF16),
        vmem((rows, CH), BF16),
        vmem(conv_weight.shape, BF16),
        pltpu.SMEM(pattern.shape, jnp.int32),
        vmem((LOCAL, *blocks), BF16),
        vmem((channels, hidden), BF16),
        vmem((hidden, channels), BF16),
        vmem((2, TILE, CH), BF16),
        vmem((2, TILE, CH), BF16),
        *[vmem(blocks, BF16)] * 4,
        *[vmem((levels, *blocks), BF16)] * 2,
        vmem((levels, nb, TILE, CH), BF16),
        vmem((zs, rows, CH), BF16),
        vmem((zs, *blocks), BF16),
        vmem((rows, hidden), F32),
        *[vmem(deep, BF16)] * 3,
        *[vmem((rows, hidden), BF16)] * 2,
        *[vmem((2, far, *blocks), BF16)] * 2,
        vmem((rows, CH), F32),
        *[vmem((2, far, *blocks), BF16)] * 2,
        vmem((rows, CH), F32),
        vmem((rows, 2 * CH), F32),
        *[vmem(blocks, BF16)] * 5,
        vmem(blocks, F32),
        *[vmem(blocks, BF16)] * 3,
        vmem((rows, CH), BF16),
        dma((7,)),
        dma((2,)),
        dma((2, 2)),
        *[dma((2, nb))] * 3,
        dma((2, 4)),
        *[dma((2, nb))] * 2,
        *[dma((2, 2, far, parts))] * 4,
        *[dma((2, nb))] * 7,
        dma((2, 2)),
    ]
    out = jax.ShapeDtypeStruct((rows, CH), BF16)
    hbm = pl.BlockSpec(memory_space=pl.ANY)
    return pl.pallas_call(
        functools.partial(kernel, nb, zs),
        out_shape=(out, out, out),
        in_specs=[hbm] * 7,
        out_specs=(hbm, hbm, hbm),
        scratch_shapes=scratch,
        compiler_params=pltpu.CompilerParams(
            collective_id=0, has_side_effects=True, vmem_limit_bytes=56 * 1024 * 1024
        ),
    )(inputs, conv_weight, mixing, pattern, w_in, w_out, cotangent)


def solution(mesh):
    seq, zs = mesh.shape["seq"], mesh.shape["ch"]
    nb = 1 << ((seq.bit_length() - 1) // 2)
    return jax.shard_map(
        functools.partial(on_device, nb, zs),
        mesh=mesh,
        in_specs=(
            P("seq", "ch"),
            P(None, "ch"),
            P(None, "seq", None, None),
            P(None, "seq"),
            P(None, "ch"),
            P("ch", None),
            P("seq", "ch"),
        ),
        out_specs=(P("seq", "ch"), P("seq", "ch"), P("seq", "ch")),
        check_vma=False,
    )
```

```python
import functools

import jax
import jax.numpy as jnp
from jax import lax
from jax.experimental import pallas as pl
from jax.experimental.pallas import tpu as pltpu
from jax.sharding import PartitionSpec as P

BLOCK = 64
LOCAL = 2
CH = 128
TILE = 16
SPLIT = BLOCK // TILE
TOP = BLOCK - TILE
MESH = pl.DeviceIdType.MESH
F32 = jnp.float32
BF16 = jnp.bfloat16
root_two_pi = 0.7978845608028654


def mod(value, size):
    return lax.rem(value + size, size)


def both(first, second, axis):
    return jnp.concatenate([first, second], axis=axis)


def forward_factor(weights, state, mates):
    return [
        jnp.dot(w, both(own, mate, 0), preferred_element_type=F32).astype(BF16)
        for w, own, mate in zip(weights, state, mates)
    ]


def transposed_terms(weights, grads):
    return [
        lax.dot_general(w, g, (((0,), (0,)), ((), ())), preferred_element_type=F32)
        for w, g in zip(weights, grads)
    ]


def kernel(nb, zs, *refs):
    (
        inputs, taps_hbm, mixing, pattern_hbm, w_in_hbm, w_out_hbm, cot,
        layer_out, conv_out, grad_out,
        x_v, cv, taps_ref, pattern, mixl, win, wout,
        halo, ghalo, st0, sx, st1, sy, wx, wy, wq,
        cot_all, cb1, cb_all, gb, mixed_all, hid, ga0, ga1, ga2, act, ghid,
        rs_send, rs_recv, rs_own, ro_send, ro_recv, ro_own, term,
        g2, g1s, g1, g0s, g0, cross, out2, cs1, cs2, go_v,
        load_sem, save_sem, halo_sem, wx_sem, wq_sem, wr_sem, wz_sem, sx_sem, sy_sem,
        bx_sem, by_sem, br_sem, ring_sem, cr_sem, mr_sem, rs_sem, ro_sem, ax_sem, ay_sem, cx_sem, cy_sem,
        gy_sem, gx_sem, lo_sem, gh_sem,
    ) = refs
    levels = nb.bit_length() - 1
    rows = nb * BLOCK
    far = zs // 2
    parts = min(4, nb)
    size = nb // parts
    lines_of = size * BLOCK
    count = nb * nb
    s = lax.axis_index("seq")
    z = lax.axis_index("ch")
    y = lax.div(s, nb)
    q = lax.rem(s, nb)
    up = mod(z + 1, zs)
    down = mod(z - 1, zs)
    up2 = mod(z + 2, zs)
    down2 = mod(z - 2, zs)
    quarter = lax.rem(z, SPLIT)
    strip = pl.ds(pl.multiple_of(quarter * TILE, TILE), TILE)

    loads = [
        pltpu.make_async_copy(inputs, x_v, load_sem.at[0]),
        pltpu.make_async_copy(mixing.at[pl.ds(0, LOCAL)], mixl, load_sem.at[1]),
        pltpu.make_async_copy(w_out_hbm, wout, load_sem.at[2]),
        pltpu.make_async_copy(w_in_hbm, win, load_sem.at[3]),
        pltpu.make_async_copy(taps_hbm, taps_ref, load_sem.at[4]),
        pltpu.make_async_copy(pattern_hbm, pattern, load_sem.at[5]),
    ]
    for load in loads:
        load.start()

    barrier = pltpu.get_barrier_semaphore()

    def greet(seq, ch):
        pl.semaphore_signal(barrier, inc=1, device_id=(seq, ch), device_id_type=MESH)

    @pl.when(s > 0)
    def _():
        greet(s - 1, z)

    @pl.when(s < count - 1)
    def _():
        greet(s + 1, z)

    for d in range(1, nb):
        greet(y * nb + mod(q + d, nb), z)
        greet(mod(y + d, nb) * nb + q, z)
    greet(s, up)
    greet(s, down)
    greet(s, up2)
    greet(s, down2)
    ends = jnp.where(s > 0, 1, 0) + jnp.where(s < count - 1, 1, 0)
    pl.semaphore_wait(barrier, 2 * (nb - 1) + 4 + ends)

    def arrival(view, sem):
        pltpu.make_async_copy(view, view, sem).wait()

    class Swap:
        def __init__(self, src, dst, sems, slot, peer, pick_src=None, pick_dst=None, many_src=None, many_dst=None):
            self.src, self.dst, self.sems, self.slot, self.peer = src, dst, sems, slot, peer
            self.pick_src, self.pick_dst = pick_src or first, pick_dst or first
            self.many_src, self.many_dst = many_src or several, many_dst or several

        def recv_sem(self, t):
            return self.sems.at[1]

        def remote(self, t, into):
            return pltpu.make_async_remote_copy(
                src_ref=self.pick_src(self.src, t),
                dst_ref=self.pick_dst(self.dst, into),
                send_sem=self.sems.at[0],
                recv_sem=self.recv_sem(into),
                device_id=(self.peer(t), z),
                device_id_type=MESH,
            )

        def own(self):
            return pltpu.make_async_copy(
                self.pick_src(self.src, self.slot), self.pick_dst(self.dst, self.slot), self.recv_sem(self.slot)
            )

        def start(self):
            for d in range(1, nb):
                self.remote(mod(self.slot + d, nb), self.slot).start()
            self.own().start()

        def wait(self):
            arrival(self.many_dst(self.dst, nb), self.sems.at[1])

        def drain(self):
            arrival(self.many_src(self.src, nb - 1), self.sems.at[0])

    class Stream(Swap):
        def recv_sem(self, t):
            return self.sems.at[1 + t]

        def wait(self, t):
            arrival(self.pick_dst(self.dst, t), self.recv_sem(t))

    def first(ref, t):
        return ref.at[t]

    def several(ref, n):
        return ref.at[pl.ds(0, n)]

    def by_q(t):
        return y * nb + t

    def by_y(t):
        return t * nb + q

    class Turn:
        def __init__(self, src, dst, sems):
            self.src, self.dst, self.sems = src, dst, sems

        def start(self):
            for t in range(nb):
                into = self.dst.at[pl.ds(q * BLOCK, BLOCK)]

                @pl.when(t * nb + y != s)
                def _():
                    pltpu.make_async_remote_copy(
                        src_ref=self.src.at[t], dst_ref=into, send_sem=self.sems.at[0], recv_sem=self.sems.at[1],
                        device_id=(t * nb + y, z), device_id_type=MESH,
                    ).start()

                @pl.when(t * nb + y == s)
                def _():
                    pltpu.make_async_copy(self.src.at[t], into, self.sems.at[1]).start()

        def wait(self):
            arrival(self.dst, self.sems.at[1])

        def drain(self):
            @pl.when(y == q)
            def _():
                arrival(self.src.at[pl.ds(0, nb - 1)], self.sems.at[0])

            @pl.when(y != q)
            def _():
                arrival(self.src, self.sems.at[0])

    def ours(way, p, count=parts):
        return (p < count // 2) == (way == 0)

    class Gather:
        def __init__(self, buf, parts, pick, first_pick, send_sem, sems):
            self.parts = parts
            self.buf, self.pick, self.first_pick, self.send_sem, self.sems = buf, pick, first_pick, send_sem, sems

        def copy(self, way, step, p, chunk):
            part = self.pick(chunk, p)
            return pltpu.make_async_remote_copy(
                src_ref=self.first_pick(p) if step == 0 else part,
                dst_ref=part,
                send_sem=self.send_sem.at[0],
                recv_sem=self.sems.at[way, step, p],
                device_id=(s, up if way == 0 else down),
                device_id_type=MESH,
            )

        def chunk(self, way, step):
            return mod(z - step, zs) if way == 0 else mod(z + step, zs)

        def each(self, step):
            for p in range(self.parts):
                for way in range(2):
                    if step < far - 1 or ours(way, p, self.parts):
                        yield way, p

        def came(self, way, step, p):
            part = self.pick(self.chunk(way, step + 1), p)
            return pltpu.make_async_remote_copy(
                src_ref=part,
                dst_ref=part,
                send_sem=self.send_sem.at[0],
                recv_sem=self.sems.at[way, step, p],
                device_id=(s, up if way == 0 else down),
                device_id_type=MESH,
            )

        def step(self, step):
            for p in range(self.parts):
                for way in range(2):
                    if step > 0:
                        self.came(way, step - 1, p).wait_recv()
                    if step < far - 1 or ours(way, p, self.parts):
                        self.copy(way, step, p, self.chunk(way, step)).start()

        def finish(self):
            for way, p in self.each(far - 1):
                self.came(way, far - 1, p).wait_recv()

        def drain(self):
            arrival(self.buf.at[pl.ds(0, zs - 1)], self.send_sem.at[0])

    class Scatter:
        def __init__(self, send, recv, own, send_sem, sems, pair):
            self.send, self.recv, self.own, self.send_sem, self.sems, self.pair = send, recv, own, send_sem, sems, pair

        def at(self, way, step, p):
            slot = zs - 2 if step == 0 else 2 * (step - 1) + way
            return slot, pl.ds(p * size, size)

        def copy(self, way, step, p):
            slot, blocks = self.at(way, step, p)
            return pltpu.make_async_remote_copy(
                src_ref=self.send.at[slot, blocks],
                dst_ref=self.recv.at[slot, blocks],
                send_sem=self.send_sem.at[0],
                recv_sem=self.sems.at[way, step, p],
                device_id=(s, up if way == 0 else down),
                device_id_type=MESH,
            )

        def arrived(self, way, step, p):
            if step < 0 or (step == 0 and not ours(way, p)):
                return None
            self.copy(way, step, p).wait_recv()
            slot, blocks = self.at(way, step, p)
            return self.recv[slot, blocks].astype(F32).reshape(lines_of, CH)

        def pass_on(self, way, step, p, value):
            slot, blocks = self.at(way, step, p)
            self.send[slot, blocks] = value.astype(BF16).reshape(size, BLOCK, CH)
            self.copy(way, step, p).start()

        def stage(self, k):
            step = far - k
            near = z if k == far else mod(z - k, zs)
            term[...] = self.pair(mod(z + k, zs), near)
            todo = [(way, p) for p in range(parts) for way in range(2)]
            if k == far:
                todo = [(way, p) for way, p in todo if ours(way, p)]
            elif k == far - 1:
                todo.sort(key=lambda item: ours(*item))
            for way, p in todo:
                value = term[pl.ds(p * lines_of, lines_of), pl.ds(0 if k == far else way * CH, CH)]
                came = self.arrived(way, step - 1, p)
                self.pass_on(way, step, p, value if came is None else value + came)
            if k == far:
                self.own[...] = term[:, pl.ds(CH, CH)]

        def finish(self):
            totals = []
            for p in range(parts):
                value = self.own[pl.ds(p * lines_of, lines_of), :]
                for way in range(2):
                    came = self.arrived(way, far - 1, p)
                    if came is not None:
                        value = value + came
                totals.append(value)
            return jnp.concatenate(totals, axis=0)

        def drain(self):
            arrival(self.send, self.send_sem.at[0])

    class Spread:
        def __init__(self):
            hb = nb // 2
            self.cases = [
                (up, down, 1, pl.ds(0, nb)), (down, up, -1, pl.ds(0, nb)),
                (up2, down2, 2, pl.ds(0, hb)), (down2, up2, -2, pl.ds(hb, hb)),
            ]

        def copy(self, case, theirs):
            to, _, shift, slots = self.cases[case]
            index = lax.rem(quarter - shift + 2 * SPLIT, SPLIT) if theirs else quarter
            part = wy.at[pl.ds(0, levels), slots, pl.ds(pl.multiple_of(index * TILE, TILE), TILE)]
            return pltpu.make_async_remote_copy(
                src_ref=part, dst_ref=part, send_sem=wz_sem.at[0, case], recv_sem=wz_sem.at[1, case],
                device_id=(s, to), device_id_type=MESH,
            )

        def start(self):
            for case in range(4):
                self.copy(case, False).start()

        def wait(self):
            for case in range(4):
                self.copy(case, True).wait_recv()

        def drain(self):
            for case in range(4):
                self.copy(case, False).wait_send()

    def rim(src_head, src_tail, dst, sems):
        return (
            pltpu.make_async_remote_copy(
                src_ref=src_tail, dst_ref=dst.at[0], send_sem=sems.at[0, 0], recv_sem=sems.at[1, 0],
                device_id=(s + 1, z), device_id_type=MESH,
            ),
            pltpu.make_async_remote_copy(
                src_ref=src_head, dst_ref=dst.at[1], send_sem=sems.at[0, 1], recv_sem=sems.at[1, 1],
                device_id=(s - 1, z), device_id_type=MESH,
            ),
        )

    def rim_start(pair, dst):
        @pl.when(s < count - 1)
        def _():
            pair[0].start()

        @pl.when(s > 0)
        def _():
            pair[1].start()

        @pl.when(s == 0)
        def _():
            dst[0] = jnp.zeros((TILE, CH), BF16)

        @pl.when(s == count - 1)
        def _():
            dst[1] = jnp.zeros((TILE, CH), BF16)

    def rim_wait(pair):
        @pl.when(s > 0)
        def _():
            pair[0].wait_recv()

        @pl.when(s < count - 1)
        def _():
            pair[1].wait_recv()

    def rim_drain(pair):
        @pl.when(s < count - 1)
        def _():
            pair[0].wait_send()

        @pl.when(s > 0)
        def _():
            pair[1].wait_send()

    def convolve(value, edges, before, same, after):
        value = value.astype(F32)
        line = lax.broadcasted_iota(jnp.int32, value.shape, 0)
        above = edges[0].astype(F32)[TILE - 1 : TILE, :]
        below = edges[1].astype(F32)[0:1, :]
        earlier = jnp.where(line == 0, above, pltpu.roll(value, 1, 0))
        later = jnp.where(line == rows - 1, below, pltpu.roll(value, rows - 1, 0))
        return (before * earlier + same * value + after * later).astype(BF16)

    def put(ref, blocks):
        for i, block in enumerate(blocks):
            ref[i] = block

    def forward_levels(weights, state):
        for level in range(levels):
            state = forward_factor(
                [weights[level, i] for i in range(nb)], state, [state[i ^ (1 << level)] for i in range(nb)]
            )
        return state

    def backward_levels(weights, grads):
        for level in reversed(range(levels)):
            terms = transposed_terms([weights[level, i] for i in range(nb)], grads)
            grads = [
                (terms[i][:BLOCK] + terms[i ^ (1 << level)][BLOCK:]).astype(BF16) for i in range(nb)
            ]
        return grads

    edges = rim(inputs.at[pl.ds(0, TILE)], inputs.at[pl.ds(rows - TILE, TILE)], halo, halo_sem)
    rim_start(edges, halo)
    upper, last = pl.ds(0, TOP), pl.ds(TOP, TILE)
    cot_ring = Gather(
        cot_all, parts,
        lambda chunk, p: cot_all.at[chunk, pl.ds(p * size, size)],
        lambda p: cot.at[pl.ds(p * size, size), upper], ring_sem.at[pl.ds(0, 1)], cr_sem,
    )
    cot_ring.step(0)
    own_cot = pltpu.make_async_copy(cot.at[pl.ds(0, nb), upper], cot_all.at[z], load_sem.at[6])
    own_cot.start()
    low, high = pl.ds(LOCAL, levels), pl.ds(LOCAL + levels, levels)
    every = pl.ds(0, levels)
    wq_swap = Swap(
        mixing, wq, wq_sem, q, by_q,
        lambda ref, t: ref.at[high, t, strip], lambda ref, t: ref.at[every, t],
        lambda ref, n: ref.at[high, pl.ds(0, n), strip], lambda ref, n: ref.at[every, pl.ds(0, n)],
    )
    wq_swap.start()
    wx_swap = Swap(
        mixing, wx, wx_sem, q, by_q,
        lambda ref, t: ref.at[low, t], lambda ref, t: ref.at[every, t],
        lambda ref, n: ref.at[low, pl.ds(0, n)], lambda ref, n: ref.at[every, pl.ds(0, n)],
    )
    wx_swap.start()

    loads[4].wait()
    taps = taps_ref[...].astype(F32)
    tap0, tap1, tap2 = taps[0:1], taps[1:2], taps[2:3]
    loads[0].wait()
    rim_wait(edges)
    cv[...] = convolve(x_v[...], (halo[0], halo[1]), tap0, tap1, tap2)
    conv_save = pltpu.make_async_copy(cv, conv_out, save_sem.at[0])
    conv_save.start()
    st0[...] = cv[...].reshape(nb, BLOCK, CH)
    loads[1].wait()
    loads[5].wait()
    for factor in range(LOCAL):
        state = [st0[i] for i in range(nb)]
        mates = [st0[pattern[factor, i]] for i in range(nb)]
        put(st0, forward_factor([mixl[factor, i] for i in range(nb)], state, mates))

    sx_swap = Swap(st0, sx, sx_sem, q, by_q)
    sx_swap.start()
    bx_swap = Swap(
        cot, cb1, bx_sem, q, by_q,
        lambda ref, t: ref.at[t, last], None, lambda ref, n: ref.at[pl.ds(0, n), last],
    )
    bx_swap.start()
    if far > 1:
        cot_ring.step(1)
    wq_swap.wait()
    wr_swap = Swap(
        wq, wy, wr_sem, y, by_y,
        lambda ref, t: ref.at[every, t], lambda ref, t: ref.at[every, t, strip],
        lambda ref, n: ref.at[every, pl.ds(0, n)], lambda ref, n: ref.at[every, pl.ds(0, n), strip],
    )
    wr_swap.start()
    if far > 2:
        cot_ring.step(2)
    wx_swap.wait()
    sx_swap.wait()
    put(st1, forward_levels(wx, [sx[i] for i in range(nb)]))

    sy_swap = Swap(st1, sy, sy_sem, y, by_y)
    sy_swap.start()
    wr_swap.wait()
    spread = Spread()
    spread.start()
    bx_swap.wait()
    by_swap = Swap(
        cb1, cb_all, by_sem, y, by_y, None, lambda ref, t: ref.at[z, t], None, lambda ref, n: ref.at[z, pl.ds(0, n)]
    )
    by_swap.start()
    for step in range(3, far):
        cot_ring.step(step)

    def channels(index):
        return pl.ds(pl.multiple_of(index * CH, CH), CH)

    def grad_act(buf):
        value = None
        lines = buf.shape[1] * buf.shape[2]
        for c in range(0, zs, 2):
            part = lax.dot_general(
                both(buf[c].reshape(lines, CH), buf[c + 1].reshape(lines, CH), 1), wout[:, pl.ds(c * CH, 2 * CH)],
                (((1,), (1,)), ((), ())), preferred_element_type=F32,
            )
            value = part if value is None else value + part
        return value

    cot_ring.finish()
    own_cot.wait()
    loads[2].wait()
    ga0[...] = grad_act(cot_all).astype(BF16).reshape(ga0.shape)
    ax_swap = Stream(ga0, ga1, ax_sem, q, by_q)
    ax_swap.start()
    cx_swap = Swap(
        cot, cs1, cx_sem, q, by_q,
        lambda ref, t: ref.at[t, upper], None, lambda ref, n: ref.at[pl.ds(0, n), upper],
    )
    cx_swap.start()
    sy_swap.wait()
    spread.wait()
    mixed = forward_levels(wy, [sy[i] for i in range(nb)])
    for i in range(nb):
        mixed_all[z, i] = mixed[i]
    mixed_ring = Gather(
        mixed_all, parts,
        lambda chunk, p: mixed_all.at[chunk, pl.ds(p * size, size)],
        lambda p: mixed_all.at[z, pl.ds(p * size, size)], ring_sem.at[pl.ds(1, 1)], mr_sem,
    )
    mixed_ring.step(0)
    by_swap.wait()
    wide = nb // 2
    last_ring = Gather(
        cb_all, 2,
        lambda chunk, p: cb_all.at[chunk, pl.ds(p * wide, wide)],
        lambda p: cb_all.at[z, pl.ds(p * wide, wide)], ring_sem.at[pl.ds(4, 1)], br_sem,
    )
    last_ring.step(0)

    def add_hidden(a, b, start):
        value = jnp.dot(
            both(mixed_all[a].reshape(rows, CH), mixed_all[b].reshape(rows, CH), 1),
            both(win[channels(a), :], win[channels(b), :], 0),
            preferred_element_type=F32,
        )
        hid[...] = value if start else hid[...] + value

    ay_swap = Swap(ga1, ga2, ay_sem, y, by_y)
    cy_swap = Swap(cs1, cs2, cy_sem, y, by_y)
    loads[3].wait()
    for d in range(nb):
        t = mod(q + d, nb)
        ax_swap.wait(t)

        @pl.when(t == y)
        def _():
            ay_swap.own().start()

        @pl.when(t != y)
        def _():
            ay_swap.remote(t, y).start()
    for step in range(1, far):
        mixed_ring.step(step)
        last_ring.step(step)
        add_hidden(mod(z - step, zs), mod(z + step, zs), step == 1)
    cx_swap.wait()
    cy_swap.start()
    last_ring.finish()
    gb[...] = grad_act(cb_all)
    mixed_ring.finish()
    add_hidden(z, mod(z + far, zs), far == 1)
    ay_swap.wait()

    @pl.loop(0, nb)
    def _(i):
        lines = pl.ds(pl.multiple_of(i * BLOCK, BLOCK), BLOCK)
        v = hid[lines, :]
        square = v * v
        tanh_val = jnp.tanh(root_two_pi * (v + 0.044715 * square * v))
        plus = 0.5 * (1.0 + tanh_val)
        act[lines, :] = (v * plus).astype(BF16)
        slope = root_two_pi * (1.0 + 3.0 * 0.044715 * square)
        slope = plus + 0.5 * v * (1.0 - tanh_val * tanh_val) * slope
        strip_of = pl.ds(pl.multiple_of(i * TILE, TILE), TILE)
        slope_in = both(ga2[i].astype(F32), gb[strip_of, :], 0)
        ghid[lines, :] = (slope_in * slope).astype(BF16)

    def grad_pair(a, b):
        return lax.dot_general(
            ghid[...], both(win[channels(a), :], win[channels(b), :], 0),
            (((1,), (1,)), ((), ())), preferred_element_type=F32,
        )

    def out_pair(a, b):
        return jnp.dot(
            act[...], both(wout[:, channels(a)], wout[:, channels(b)], 1), preferred_element_type=F32
        )

    grad_sum = Scatter(rs_send, rs_recv, rs_own, ring_sem.at[pl.ds(2, 1)], rs_sem, grad_pair)
    out_sum = Scatter(ro_send, ro_recv, ro_own, ring_sem.at[pl.ds(3, 1)], ro_sem, out_pair)
    for k in range(far, 1, -1):
        grad_sum.stage(k)
    out_sum.stage(far)
    grad_sum.stage(1)
    rest = list(range(far - 1, 0, -1))
    for k in rest[:1]:
        out_sum.stage(k)
    cy_swap.wait()
    total = grad_sum.finish()
    own_grad = both(cs2[...], cb_all[z], 1).astype(F32).reshape(rows, CH)
    grad_mixed = (own_grad + total).astype(BF16).reshape(nb, BLOCK, CH)

    put(g2, backward_levels(wy, [grad_mixed[i] for i in range(nb)]))
    gy_swap = Swap(g2, g1, gy_sem, y, by_y)
    gy_swap.start()
    for k in rest[1:2]:
        out_sum.stage(k)
    gy_swap.wait()
    put(g1s, backward_levels(wx, [g1[i] for i in range(nb)]))
    gx_swap = Swap(g1s, g0, gx_sem, q, by_q)
    gx_swap.start()
    for k in rest[2:]:
        out_sum.stage(k)
    branch = out_sum.finish()
    whole = (mixed_all[z].astype(F32).reshape(rows, CH) + branch).astype(BF16)
    out2[...] = whole.reshape(nb, BLOCK, CH)
    lo_turn = Turn(out2, layer_out, lo_sem)
    lo_turn.start()
    gx_swap.wait()
    grads = [g0[i] for i in range(nb)]
    for factor in reversed(range(LOCAL)):
        terms = transposed_terms([mixl[factor, i] for i in range(nb)], grads)
        put(cross, [t[BLOCK:] for t in terms])
        grads = [(terms[i][:BLOCK] + cross[pattern[factor, i]]).astype(BF16) for i in range(nb)]
    put(g0s, grads)
    gedges = rim(
        g0s.at[0, pl.ds(0, TILE)], g0s.at[nb - 1, pl.ds(BLOCK - TILE, TILE)], ghalo, gh_sem
    )
    rim_start(gedges, ghalo)
    rim_wait(gedges)
    go_v[...] = convolve(g0s[...].reshape(rows, CH), (ghalo[0], ghalo[1]), tap2, tap1, tap0)
    grad_save = pltpu.make_async_copy(go_v, grad_out, save_sem.at[1])
    grad_save.start()

    rim_drain(edges)
    rim_drain(gedges)
    for transfer in (
        wq_swap, wx_swap, wr_swap, spread, sx_swap, sy_swap, ax_swap, ay_swap, cx_swap, cy_swap, bx_swap, by_swap,
        cot_ring, last_ring, mixed_ring, grad_sum, out_sum, gy_swap, gx_swap, lo_turn,
    ):
        transfer.drain()
    conv_save.wait()
    lo_turn.wait()
    grad_save.wait()


def publish(*refs):
    sources, targets, sem = refs[:3], refs[3:6], refs[6]
    copies = [pltpu.make_async_copy(a, b, sem.at[i]) for i, (a, b) in enumerate(zip(sources, targets))]
    for copy in copies:
        copy.start()
    for copy in copies:
        copy.wait()


def on_device(nb, zs, inputs, conv_weight, mixing, pattern, w_in, w_out, cotangent):
    rows, _ = inputs.shape
    levels = nb.bit_length() - 1
    hidden = w_in.shape[1]
    channels = w_in.shape[0]
    far = zs // 2
    vmem = pltpu.VMEM
    dma = pltpu.SemaphoreType.DMA
    blocks = (nb, BLOCK, CH)
    parts = min(4, nb)
    deep = (nb, TOP, hidden)
    scratch = [
        vmem((rows, CH), BF16),
        vmem((rows, CH), BF16),
        vmem(conv_weight.shape, BF16),
        pltpu.SMEM(pattern.shape, jnp.int32),
        vmem((LOCAL, *blocks), BF16),
        vmem((channels, hidden), BF16),
        vmem((hidden, channels), BF16),
        vmem((2, TILE, CH), BF16),
        vmem((2, TILE, CH), BF16),
        *[vmem(blocks, BF16)] * 4,
        *[vmem((levels, *blocks), BF16)] * 2,
        vmem((levels, nb, TILE, CH), BF16),
        vmem((zs, nb, TOP, CH), BF16),
        vmem((nb, TILE, CH), BF16),
        vmem((zs, nb, TILE, CH), BF16),
        vmem((nb * TILE, hidden), F32),
        vmem((zs, *blocks), BF16),
        vmem((rows, hidden), F32),
        *[vmem(deep, BF16)] * 3,
        *[vmem((rows, hidden), BF16)] * 2,
        *[vmem((zs - 1, *blocks), BF16)] * 2,
        vmem((rows, CH), F32),
        *[vmem((zs - 1, *blocks), BF16)] * 2,
        vmem((rows, CH), F32),
        vmem((rows, 2 * CH), F32),
        *[vmem(blocks, BF16)] * 5,
        vmem(blocks, F32),
        vmem(blocks, BF16),
        *[vmem((nb, TOP, CH), BF16)] * 2,
        vmem((rows, CH), BF16),
        dma((7,)),
        dma((2,)),
        dma((2, 2)),
        *[dma((2,))] * 3,
        dma((2, 4)),
        *[dma((2,))] * 4,
        dma((2, far, 2)),
        dma((5,)),
        *[dma((2, far, parts))] * 4,
        dma((1 + nb,)),
        *[dma((2,))] * 6,
        dma((2, 2)),
    ]
    out = jax.ShapeDtypeStruct((rows, CH), BF16)
    hbm = pl.BlockSpec(memory_space=pl.ANY)
    results = pl.pallas_call(
        functools.partial(kernel, nb, zs),
        out_shape=(out, out, out),
        in_specs=[hbm] * 7,
        out_specs=(hbm, hbm, hbm),
        scratch_shapes=scratch,
        compiler_params=pltpu.CompilerParams(
            collective_id=0, has_side_effects=True, vmem_limit_bytes=24 * 1024 * 1024
        ),
    )(*[pltpu.with_memory_space_constraint(v, pltpu.HBM) for v in (
        inputs, conv_weight, mixing, pattern, w_in, w_out, cotangent.reshape(blocks)
    )])
    return pl.pallas_call(
        publish,
        out_shape=(out, out, out),
        in_specs=[pl.BlockSpec(memory_space=pltpu.VMEM)] * 3,
        out_specs=(hbm, hbm, hbm),
        scratch_shapes=[dma((3,))],
        compiler_params=pltpu.CompilerParams(vmem_limit_bytes=4 * 1024 * 1024),
    )(*results)


def solution(mesh):
    seq, zs = mesh.shape["seq"], mesh.shape["ch"]
    nb = 1 << ((seq.bit_length() - 1) // 2)
    return jax.shard_map(
        functools.partial(on_device, nb, zs),
        mesh=mesh,
        in_specs=(
            P("seq", "ch"),
            P(None, "ch"),
            P(None, "seq", None, None),
            P(None, "seq"),
            P(None, "ch"),
            P("ch", None),
            P("seq", "ch"),
        ),
        out_specs=(P("seq", "ch"), P("seq", "ch"), P("seq", "ch")),
        check_vma=False,
    )
```

```python
import functools

import jax
import jax.numpy as jnp
from jax import lax
from jax.experimental import pallas as pl
from jax.experimental.pallas import tpu as pltpu
from jax.sharding import PartitionSpec as P

BLOCK = 64
LOCAL = 2
CH = 128
TILE = 16
SPLIT = BLOCK // TILE
TOP = BLOCK - TILE
MESH = pl.DeviceIdType.MESH
F32 = jnp.float32
BF16 = jnp.bfloat16
root_two_pi = 0.7978845608028654


def mod(value, size):
    return lax.rem(value + size, size)


def both(first, second, axis):
    return jnp.concatenate([first, second], axis=axis)


def forward_factor(weights, state, mates):
    return [
        jnp.dot(w, both(own, mate, 0), preferred_element_type=F32).astype(BF16)
        for w, own, mate in zip(weights, state, mates)
    ]


def transposed_terms(weights, grads):
    return [
        lax.dot_general(w, g, (((0,), (0,)), ((), ())), preferred_element_type=F32)
        for w, g in zip(weights, grads)
    ]


def kernel(nb, zs, *refs):
    (
        inputs, taps_hbm, mixing, pattern_hbm, w_in_hbm, w_out_hbm, cot,
        layer_out, conv_out, grad_out,
        x_v, cv, taps_ref, pattern, mixl, win, wout,
        halo, ghalo, st0, sx, st1, sy, wx, wy, wq,
        cot_all, cb1, cb_all, gb, mixed_all, hid, ga0, ga1, ga2, act, ghid,
        rs_send, rs_recv, rs_own, ro_send, ro_recv, ro_own, term,
        g2, g1s, g1, g0s, g0, cross, out2, cs1, cs2, go_v,
        load_sem, save_sem, halo_sem, wx_sem, wq_sem, wr_sem, wz_sem, sx_sem, sy_sem,
        bx_sem, by_sem, br_sem, ring_sem, cr_sem, mr_sem, rs_sem, ro_sem, ax_sem, ay_sem, cx_sem, cy_sem,
        gy_sem, gx_sem, lo_sem, gh_sem,
    ) = refs
    levels = nb.bit_length() - 1
    rows = nb * BLOCK
    far = zs // 2
    parts = min(4, nb)
    size = nb // parts
    lines_of = size * BLOCK
    count = nb * nb
    s = lax.axis_index("seq")
    z = lax.axis_index("ch")
    y = lax.div(s, nb)
    q = lax.rem(s, nb)
    up = mod(z + 1, zs)
    down = mod(z - 1, zs)
    up2 = mod(z + 2, zs)
    down2 = mod(z - 2, zs)
    quarter = lax.rem(z, SPLIT)
    strip = pl.ds(pl.multiple_of(quarter * TILE, TILE), TILE)

    loads = [
        pltpu.make_async_copy(inputs, x_v, load_sem.at[0]),
        pltpu.make_async_copy(mixing.at[pl.ds(0, LOCAL)], mixl, load_sem.at[1]),
        pltpu.make_async_copy(w_out_hbm, wout, load_sem.at[2]),
        pltpu.make_async_copy(w_in_hbm, win, load_sem.at[3]),
        pltpu.make_async_copy(taps_hbm, taps_ref, load_sem.at[4]),
        pltpu.make_async_copy(pattern_hbm, pattern, load_sem.at[5]),
    ]
    for load in loads:
        load.start()

    barrier = pltpu.get_barrier_semaphore()

    def greet(seq, ch):
        pl.semaphore_signal(barrier, inc=1, device_id=(seq, ch), device_id_type=MESH)

    @pl.when(s > 0)
    def _():
        greet(s - 1, z)

    @pl.when(s < count - 1)
    def _():
        greet(s + 1, z)

    for d in range(1, nb):
        greet(y * nb + mod(q + d, nb), z)
        greet(mod(y + d, nb) * nb + q, z)
    greet(s, up)
    greet(s, down)
    greet(s, up2)
    greet(s, down2)
    ends = jnp.where(s > 0, 1, 0) + jnp.where(s < count - 1, 1, 0)
    pl.semaphore_wait(barrier, 2 * (nb - 1) + 4 + ends)

    def arrival(view, sem):
        pltpu.make_async_copy(view, view, sem).wait()

    class Swap:
        def __init__(self, src, dst, sems, slot, peer, pick_src=None, pick_dst=None, many_src=None, many_dst=None):
            self.src, self.dst, self.sems, self.slot, self.peer = src, dst, sems, slot, peer
            self.pick_src, self.pick_dst = pick_src or first, pick_dst or first
            self.many_src, self.many_dst = many_src or several, many_dst or several

        def recv_sem(self, t):
            return self.sems.at[1]

        def remote(self, t, into):
            return pltpu.make_async_remote_copy(
                src_ref=self.pick_src(self.src, t),
                dst_ref=self.pick_dst(self.dst, into),
                send_sem=self.sems.at[0],
                recv_sem=self.recv_sem(into),
                device_id=(self.peer(t), z),
                device_id_type=MESH,
            )

        def own(self):
            return pltpu.make_async_copy(
                self.pick_src(self.src, self.slot), self.pick_dst(self.dst, self.slot), self.recv_sem(self.slot)
            )

        def start(self):
            for d in range(1, nb):
                self.remote(mod(self.slot + d, nb), self.slot).start()
            self.own().start()

        def wait(self):
            arrival(self.many_dst(self.dst, nb), self.sems.at[1])

        def drain(self):
            arrival(self.many_src(self.src, nb - 1), self.sems.at[0])

    class Stream(Swap):
        def recv_sem(self, t):
            return self.sems.at[1 + t]

        def wait(self, t):
            arrival(self.pick_dst(self.dst, t), self.recv_sem(t))

    def first(ref, t):
        return ref.at[t]

    def several(ref, n):
        return ref.at[pl.ds(0, n)]

    def by_q(t):
        return y * nb + t

    def by_y(t):
        return t * nb + q

    class Turn:
        def __init__(self, src, dst, sems):
            self.src, self.dst, self.sems = src, dst, sems

        def start(self, blocks):
            for t in blocks:
                into = self.dst.at[pl.ds(q * BLOCK, BLOCK)]

                @pl.when(t * nb + y != s)
                def _():
                    pltpu.make_async_remote_copy(
                        src_ref=self.src.at[t], dst_ref=into, send_sem=self.sems.at[0], recv_sem=self.sems.at[1],
                        device_id=(t * nb + y, z), device_id_type=MESH,
                    ).start()

                @pl.when(t * nb + y == s)
                def _():
                    pltpu.make_async_copy(self.src.at[t], into, self.sems.at[1]).start()

        def wait(self):
            arrival(self.dst, self.sems.at[1])

        def drain(self):
            @pl.when(y == q)
            def _():
                arrival(self.src.at[pl.ds(0, nb - 1)], self.sems.at[0])

            @pl.when(y != q)
            def _():
                arrival(self.src, self.sems.at[0])

    def ours(way, p, count=parts):
        return (p < count // 2) == (way == 0)

    class Gather:
        def __init__(self, buf, parts, pick, first_pick, send_sem, sems):
            self.parts = parts
            self.buf, self.pick, self.first_pick, self.send_sem, self.sems = buf, pick, first_pick, send_sem, sems

        def copy(self, way, step, p, chunk):
            part = self.pick(chunk, p)
            return pltpu.make_async_remote_copy(
                src_ref=self.first_pick(p) if step == 0 else part,
                dst_ref=part,
                send_sem=self.send_sem.at[0],
                recv_sem=self.sems.at[way, step, p],
                device_id=(s, up if way == 0 else down),
                device_id_type=MESH,
            )

        def chunk(self, way, step):
            return mod(z - step, zs) if way == 0 else mod(z + step, zs)

        def each(self, step):
            for p in range(self.parts):
                for way in range(2):
                    if step < far - 1 or ours(way, p, self.parts):
                        yield way, p

        def came(self, way, step, p):
            part = self.pick(self.chunk(way, step + 1), p)
            return pltpu.make_async_remote_copy(
                src_ref=part,
                dst_ref=part,
                send_sem=self.send_sem.at[0],
                recv_sem=self.sems.at[way, step, p],
                device_id=(s, up if way == 0 else down),
                device_id_type=MESH,
            )

        def step(self, step):
            for p in range(self.parts):
                for way in range(2):
                    if step > 0:
                        self.came(way, step - 1, p).wait_recv()
                    if step < far - 1 or ours(way, p, self.parts):
                        self.copy(way, step, p, self.chunk(way, step)).start()

        def finish(self):
            for way, p in self.each(far - 1):
                self.came(way, far - 1, p).wait_recv()

        def drain(self):
            arrival(self.buf.at[pl.ds(0, zs - 1)], self.send_sem.at[0])

    class Scatter:
        def __init__(self, send, recv, own, send_sem, sems, pair):
            self.send, self.recv, self.own, self.send_sem, self.sems, self.pair = send, recv, own, send_sem, sems, pair

        def at(self, way, step, p):
            slot = zs - 2 if step == 0 else 2 * (step - 1) + way
            return slot, pl.ds(p * size, size)

        def copy(self, way, step, p):
            slot, blocks = self.at(way, step, p)
            return pltpu.make_async_remote_copy(
                src_ref=self.send.at[slot, blocks],
                dst_ref=self.recv.at[slot, blocks],
                send_sem=self.send_sem.at[0],
                recv_sem=self.sems.at[way, step, p],
                device_id=(s, up if way == 0 else down),
                device_id_type=MESH,
            )

        def arrived(self, way, step, p):
            if step < 0 or (step == 0 and not ours(way, p)):
                return None
            self.copy(way, step, p).wait_recv()
            slot, blocks = self.at(way, step, p)
            return self.recv[slot, blocks].astype(F32).reshape(lines_of, CH)

        def pass_on(self, way, step, p, value):
            slot, blocks = self.at(way, step, p)
            self.send[slot, blocks] = value.astype(BF16).reshape(size, BLOCK, CH)
            self.copy(way, step, p).start()

        def stage(self, k):
            step = far - k
            near = z if k == far else mod(z - k, zs)
            term[...] = self.pair(mod(z + k, zs), near)
            todo = [(way, p) for p in range(parts) for way in range(2)]
            if k == far:
                todo = [(way, p) for way, p in todo if ours(way, p)]
            elif k == far - 1:
                todo.sort(key=lambda item: ours(*item))
            for way, p in todo:
                value = term[pl.ds(p * lines_of, lines_of), pl.ds(0 if k == far else way * CH, CH)]
                came = self.arrived(way, step - 1, p)
                self.pass_on(way, step, p, value if came is None else value + came)
            if k == far:
                self.own[...] = term[:, pl.ds(CH, CH)]

        def total(self, p):
            value = self.own[pl.ds(p * lines_of, lines_of), :]
            for way in range(2):
                came = self.arrived(way, far - 1, p)
                if came is not None:
                    value = value + came
            return value

        def finish(self):
            return jnp.concatenate([self.total(p) for p in range(parts)], axis=0)

        def drain(self):
            arrival(self.send, self.send_sem.at[0])

    class Spread:
        def __init__(self):
            hb = nb // 2
            self.cases = [
                (up, down, 1, pl.ds(0, nb)), (down, up, -1, pl.ds(0, nb)),
                (up2, down2, 2, pl.ds(0, hb)), (down2, up2, -2, pl.ds(hb, hb)),
            ]

        def copy(self, case, theirs):
            to, _, shift, slots = self.cases[case]
            index = lax.rem(quarter - shift + 2 * SPLIT, SPLIT) if theirs else quarter
            part = wy.at[pl.ds(0, levels), slots, pl.ds(pl.multiple_of(index * TILE, TILE), TILE)]
            return pltpu.make_async_remote_copy(
                src_ref=part, dst_ref=part, send_sem=wz_sem.at[0, case], recv_sem=wz_sem.at[1, case],
                device_id=(s, to), device_id_type=MESH,
            )

        def start(self):
            for case in range(4):
                self.copy(case, False).start()

        def wait(self):
            for case in range(4):
                self.copy(case, True).wait_recv()

        def drain(self):
            for case in range(4):
                self.copy(case, False).wait_send()

    def rim(src_head, src_tail, dst, sems):
        return (
            pltpu.make_async_remote_copy(
                src_ref=src_tail, dst_ref=dst.at[0], send_sem=sems.at[0, 0], recv_sem=sems.at[1, 0],
                device_id=(s + 1, z), device_id_type=MESH,
            ),
            pltpu.make_async_remote_copy(
                src_ref=src_head, dst_ref=dst.at[1], send_sem=sems.at[0, 1], recv_sem=sems.at[1, 1],
                device_id=(s - 1, z), device_id_type=MESH,
            ),
        )

    def rim_start(pair, dst):
        @pl.when(s < count - 1)
        def _():
            pair[0].start()

        @pl.when(s > 0)
        def _():
            pair[1].start()

        @pl.when(s == 0)
        def _():
            dst[0] = jnp.zeros((TILE, CH), BF16)

        @pl.when(s == count - 1)
        def _():
            dst[1] = jnp.zeros((TILE, CH), BF16)

    def rim_wait(pair):
        @pl.when(s > 0)
        def _():
            pair[0].wait_recv()

        @pl.when(s < count - 1)
        def _():
            pair[1].wait_recv()

    def rim_drain(pair):
        @pl.when(s < count - 1)
        def _():
            pair[0].wait_send()

        @pl.when(s > 0)
        def _():
            pair[1].wait_send()

    def convolve(value, edges, before, same, after):
        value = value.astype(F32)
        line = lax.broadcasted_iota(jnp.int32, value.shape, 0)
        above = edges[0].astype(F32)[TILE - 1 : TILE, :]
        below = edges[1].astype(F32)[0:1, :]
        earlier = jnp.where(line == 0, above, pltpu.roll(value, 1, 0))
        later = jnp.where(line == rows - 1, below, pltpu.roll(value, rows - 1, 0))
        return (before * earlier + same * value + after * later).astype(BF16)

    def put(ref, blocks):
        for i, block in enumerate(blocks):
            ref[i] = block

    def forward_levels(weights, state):
        for level in range(levels):
            state = forward_factor(
                [weights[level, i] for i in range(nb)], state, [state[i ^ (1 << level)] for i in range(nb)]
            )
        return state

    def backward_levels(weights, grads):
        for level in reversed(range(levels)):
            terms = transposed_terms([weights[level, i] for i in range(nb)], grads)
            grads = [
                (terms[i][:BLOCK] + terms[i ^ (1 << level)][BLOCK:]).astype(BF16) for i in range(nb)
            ]
        return grads

    edges = rim(inputs.at[pl.ds(0, TILE)], inputs.at[pl.ds(rows - TILE, TILE)], halo, halo_sem)
    rim_start(edges, halo)
    upper, last = pl.ds(0, TOP), pl.ds(TOP, TILE)
    cot_ring = Gather(
        cot_all, parts,
        lambda chunk, p: cot_all.at[chunk, pl.ds(p * size, size)],
        lambda p: cot.at[pl.ds(p * size, size), upper], ring_sem.at[pl.ds(0, 1)], cr_sem,
    )
    cot_ring.step(0)
    own_cot = pltpu.make_async_copy(cot.at[pl.ds(0, nb), upper], cot_all.at[z], load_sem.at[6])
    own_cot.start()
    low, high = pl.ds(LOCAL, levels), pl.ds(LOCAL + levels, levels)
    every = pl.ds(0, levels)
    wq_swap = Swap(
        mixing, wq, wq_sem, q, by_q,
        lambda ref, t: ref.at[high, t, strip], lambda ref, t: ref.at[every, t],
        lambda ref, n: ref.at[high, pl.ds(0, n), strip], lambda ref, n: ref.at[every, pl.ds(0, n)],
    )
    wq_swap.start()
    wx_swap = Swap(
        mixing, wx, wx_sem, q, by_q,
        lambda ref, t: ref.at[low, t], lambda ref, t: ref.at[every, t],
        lambda ref, n: ref.at[low, pl.ds(0, n)], lambda ref, n: ref.at[every, pl.ds(0, n)],
    )
    wx_swap.start()

    loads[4].wait()
    taps = taps_ref[...].astype(F32)
    tap0, tap1, tap2 = taps[0:1], taps[1:2], taps[2:3]
    loads[0].wait()
    rim_wait(edges)
    cv[...] = convolve(x_v[...], (halo[0], halo[1]), tap0, tap1, tap2)
    conv_save = pltpu.make_async_copy(cv, conv_out, save_sem.at[0])
    conv_save.start()
    st0[...] = cv[...].reshape(nb, BLOCK, CH)
    loads[1].wait()
    loads[5].wait()
    for factor in range(LOCAL):
        state = [st0[i] for i in range(nb)]
        mates = [st0[pattern[factor, i]] for i in range(nb)]
        put(st0, forward_factor([mixl[factor, i] for i in range(nb)], state, mates))

    sx_swap = Swap(st0, sx, sx_sem, q, by_q)
    sx_swap.start()
    bx_swap = Swap(
        cot, cb1, bx_sem, q, by_q,
        lambda ref, t: ref.at[t, last], None, lambda ref, n: ref.at[pl.ds(0, n), last],
    )
    bx_swap.start()
    if far > 1:
        cot_ring.step(1)
    wq_swap.wait()
    wr_swap = Swap(
        wq, wy, wr_sem, y, by_y,
        lambda ref, t: ref.at[every, t], lambda ref, t: ref.at[every, t, strip],
        lambda ref, n: ref.at[every, pl.ds(0, n)], lambda ref, n: ref.at[every, pl.ds(0, n), strip],
    )
    wr_swap.start()
    if far > 2:
        cot_ring.step(2)
    wx_swap.wait()
    sx_swap.wait()
    put(st1, forward_levels(wx, [sx[i] for i in range(nb)]))

    sy_swap = Swap(st1, sy, sy_sem, y, by_y)
    sy_swap.start()
    for step in range(3, far):
        cot_ring.step(step)
    wr_swap.wait()
    spread = Spread()
    spread.start()
    bx_swap.wait()
    by_swap = Swap(
        cb1, cb_all, by_sem, y, by_y, None, lambda ref, t: ref.at[z, t], None, lambda ref, n: ref.at[z, pl.ds(0, n)]
    )
    by_swap.start()

    def channels(index):
        return pl.ds(pl.multiple_of(index * CH, CH), CH)

    def grad_act(buf):
        value = None
        lines = buf.shape[1] * buf.shape[2]
        for c in range(0, zs, 2):
            part = lax.dot_general(
                both(buf[c].reshape(lines, CH), buf[c + 1].reshape(lines, CH), 1), wout[:, pl.ds(c * CH, 2 * CH)],
                (((1,), (1,)), ((), ())), preferred_element_type=F32,
            )
            value = part if value is None else value + part
        return value

    cot_ring.finish()
    own_cot.wait()
    loads[2].wait()
    ga0[...] = grad_act(cot_all).astype(BF16).reshape(ga0.shape)
    ax_swap = Stream(ga0, ga1, ax_sem, q, by_q)
    ax_swap.start()
    cx_swap = Swap(
        cot, cs1, cx_sem, q, by_q,
        lambda ref, t: ref.at[t, upper], None, lambda ref, n: ref.at[pl.ds(0, n), upper],
    )
    cx_swap.start()
    sy_swap.wait()
    spread.wait()
    mixed = forward_levels(wy, [sy[i] for i in range(nb)])
    for i in range(nb):
        mixed_all[z, i] = mixed[i]
    mixed_ring = Gather(
        mixed_all, parts,
        lambda chunk, p: mixed_all.at[chunk, pl.ds(p * size, size)],
        lambda p: mixed_all.at[z, pl.ds(p * size, size)], ring_sem.at[pl.ds(1, 1)], mr_sem,
    )
    mixed_ring.step(0)
    by_swap.wait()
    wide = nb // 2
    last_ring = Gather(
        cb_all, 2,
        lambda chunk, p: cb_all.at[chunk, pl.ds(p * wide, wide)],
        lambda p: cb_all.at[z, pl.ds(p * wide, wide)], ring_sem.at[pl.ds(4, 1)], br_sem,
    )
    last_ring.step(0)

    def add_hidden(a, b, start):
        value = jnp.dot(
            both(mixed_all[a].reshape(rows, CH), mixed_all[b].reshape(rows, CH), 1),
            both(win[channels(a), :], win[channels(b), :], 0),
            preferred_element_type=F32,
        )
        hid[...] = value if start else hid[...] + value

    ay_swap = Swap(ga1, ga2, ay_sem, y, by_y)
    cy_swap = Swap(cs1, cs2, cy_sem, y, by_y)
    loads[3].wait()
    for step in range(1, far):
        mixed_ring.step(step)
        last_ring.step(step)
        add_hidden(mod(z - step, zs), mod(z + step, zs), step == 1)
        if step == 1:
            for d in range(nb):
                t = mod(q + d, nb)
                ax_swap.wait(t)

                @pl.when(t == y)
                def _():
                    ay_swap.own().start()

                @pl.when(t != y)
                def _():
                    ay_swap.remote(t, y).start()
    cx_swap.wait()
    cy_swap.start()
    last_ring.finish()
    gb[...] = grad_act(cb_all)
    mixed_ring.finish()
    add_hidden(z, mod(z + far, zs), far == 1)
    ay_swap.wait()

    @pl.loop(0, nb)
    def _(i):
        lines = pl.ds(pl.multiple_of(i * BLOCK, BLOCK), BLOCK)
        v = hid[lines, :]
        square = v * v
        tanh_val = jnp.tanh(root_two_pi * (v + 0.044715 * square * v))
        plus = 0.5 * (1.0 + tanh_val)
        act[lines, :] = (v * plus).astype(BF16)
        slope = root_two_pi * (1.0 + 3.0 * 0.044715 * square)
        slope = plus + 0.5 * v * (1.0 - tanh_val * tanh_val) * slope
        strip_of = pl.ds(pl.multiple_of(i * TILE, TILE), TILE)
        slope_in = both(ga2[i].astype(F32), gb[strip_of, :], 0)
        ghid[lines, :] = (slope_in * slope).astype(BF16)

    def grad_pair(a, b):
        return lax.dot_general(
            ghid[...], both(win[channels(a), :], win[channels(b), :], 0),
            (((1,), (1,)), ((), ())), preferred_element_type=F32,
        )

    def out_pair(a, b):
        return jnp.dot(
            act[...], both(wout[:, channels(a)], wout[:, channels(b)], 1), preferred_element_type=F32
        )

    grad_sum = Scatter(rs_send, rs_recv, rs_own, ring_sem.at[pl.ds(2, 1)], rs_sem, grad_pair)
    out_sum = Scatter(ro_send, ro_recv, ro_own, ring_sem.at[pl.ds(3, 1)], ro_sem, out_pair)
    for k in range(far, 1, -1):
        grad_sum.stage(k)
    out_sum.stage(far)
    grad_sum.stage(1)
    rest = list(range(far - 1, 0, -1))
    for k in rest[:1]:
        out_sum.stage(k)
    cy_swap.wait()
    total = grad_sum.finish()
    own_grad = both(cs2[...], cb_all[z], 1).astype(F32).reshape(rows, CH)
    grad_mixed = (own_grad + total).astype(BF16).reshape(nb, BLOCK, CH)

    put(g2, backward_levels(wy, [grad_mixed[i] for i in range(nb)]))
    gy_swap = Swap(g2, g1, gy_sem, y, by_y)
    gy_swap.start()
    for k in rest[1:2]:
        out_sum.stage(k)
    for k in rest[2:]:
        out_sum.stage(k)
    gy_swap.wait()
    put(g1s, backward_levels(wx, [g1[i] for i in range(nb)]))
    gx_swap = Swap(g1s, g0, gx_sem, q, by_q)
    gx_swap.start()
    lo_turn = Turn(out2, layer_out, lo_sem)
    for p in range(parts):
        blocks = pl.ds(p * size, size)
        whole = mixed_all[z, blocks].astype(F32).reshape(lines_of, CH) + out_sum.total(p)
        out2[blocks] = whole.astype(BF16).reshape(size, BLOCK, CH)
        lo_turn.start(range(p * size, (p + 1) * size))
    gx_swap.wait()
    grads = [g0[i] for i in range(nb)]
    for factor in reversed(range(LOCAL)):
        terms = transposed_terms([mixl[factor, i] for i in range(nb)], grads)
        put(cross, [t[BLOCK:] for t in terms])
        grads = [(terms[i][:BLOCK] + cross[pattern[factor, i]]).astype(BF16) for i in range(nb)]
    put(g0s, grads)
    gedges = rim(
        g0s.at[0, pl.ds(0, TILE)], g0s.at[nb - 1, pl.ds(BLOCK - TILE, TILE)], ghalo, gh_sem
    )
    rim_start(gedges, ghalo)
    rim_wait(gedges)
    go_v[...] = convolve(g0s[...].reshape(rows, CH), (ghalo[0], ghalo[1]), tap2, tap1, tap0)
    grad_save = pltpu.make_async_copy(go_v, grad_out, save_sem.at[1])
    grad_save.start()

    rim_drain(edges)
    rim_drain(gedges)
    for transfer in (
        wq_swap, wx_swap, wr_swap, spread, sx_swap, sy_swap, ax_swap, ay_swap, cx_swap, cy_swap, bx_swap, by_swap,
        cot_ring, last_ring, mixed_ring, grad_sum, out_sum, gy_swap, gx_swap, lo_turn,
    ):
        transfer.drain()
    conv_save.wait()
    lo_turn.wait()
    grad_save.wait()


def publish(*refs):
    sources, targets, sem = refs[:3], refs[3:6], refs[6]
    copies = [pltpu.make_async_copy(a, b, sem.at[i]) for i, (a, b) in enumerate(zip(sources, targets))]
    for copy in copies:
        copy.start()
    for copy in copies:
        copy.wait()


def on_device(nb, zs, inputs, conv_weight, mixing, pattern, w_in, w_out, cotangent):
    rows, _ = inputs.shape
    levels = nb.bit_length() - 1
    hidden = w_in.shape[1]
    channels = w_in.shape[0]
    far = zs // 2
    vmem = pltpu.VMEM
    dma = pltpu.SemaphoreType.DMA
    blocks = (nb, BLOCK, CH)
    parts = min(4, nb)
    deep = (nb, TOP, hidden)
    scratch = [
        vmem((rows, CH), BF16),
        vmem((rows, CH), BF16),
        vmem(conv_weight.shape, BF16),
        pltpu.SMEM(pattern.shape, jnp.int32),
        vmem((LOCAL, *blocks), BF16),
        vmem((channels, hidden), BF16),
        vmem((hidden, channels), BF16),
        vmem((2, TILE, CH), BF16),
        vmem((2, TILE, CH), BF16),
        *[vmem(blocks, BF16)] * 4,
        *[vmem((levels, *blocks), BF16)] * 2,
        vmem((levels, nb, TILE, CH), BF16),
        vmem((zs, nb, TOP, CH), BF16),
        vmem((nb, TILE, CH), BF16),
        vmem((zs, nb, TILE, CH), BF16),
        vmem((nb * TILE, hidden), F32),
        vmem((zs, *blocks), BF16),
        vmem((rows, hidden), F32),
        *[vmem(deep, BF16)] * 3,
        *[vmem((rows, hidden), BF16)] * 2,
        *[vmem((zs - 1, *blocks), BF16)] * 2,
        vmem((rows, CH), F32),
        *[vmem((zs - 1, *blocks), BF16)] * 2,
        vmem((rows, CH), F32),
        vmem((rows, 2 * CH), F32),
        *[vmem(blocks, BF16)] * 5,
        vmem(blocks, F32),
        vmem(blocks, BF16),
        *[vmem((nb, TOP, CH), BF16)] * 2,
        vmem((rows, CH), BF16),
        dma((7,)),
        dma((2,)),
        dma((2, 2)),
        *[dma((2,))] * 3,
        dma((2, 4)),
        *[dma((2,))] * 4,
        dma((2, far, 2)),
        dma((5,)),
        *[dma((2, far, parts))] * 4,
        dma((1 + nb,)),
        *[dma((2,))] * 6,
        dma((2, 2)),
    ]
    out = jax.ShapeDtypeStruct((rows, CH), BF16)
    hbm = pl.BlockSpec(memory_space=pl.ANY)
    results = pl.pallas_call(
        functools.partial(kernel, nb, zs),
        out_shape=(out, out, out),
        in_specs=[hbm] * 7,
        out_specs=(hbm, hbm, hbm),
        scratch_shapes=scratch,
        compiler_params=pltpu.CompilerParams(
            collective_id=0, has_side_effects=True, vmem_limit_bytes=24 * 1024 * 1024
        ),
    )(*[pltpu.with_memory_space_constraint(v, pltpu.HBM) for v in (
        inputs, conv_weight, mixing, pattern, w_in, w_out, cotangent.reshape(blocks)
    )])
    return pl.pallas_call(
        publish,
        out_shape=(out, out, out),
        in_specs=[pl.BlockSpec(memory_space=pltpu.VMEM)] * 3,
        out_specs=(hbm, hbm, hbm),
        scratch_shapes=[dma((3,))],
        compiler_params=pltpu.CompilerParams(vmem_limit_bytes=4 * 1024 * 1024),
    )(*results)


def solution(mesh):
    seq, zs = mesh.shape["seq"], mesh.shape["ch"]
    nb = 1 << ((seq.bit_length() - 1) // 2)
    return jax.shard_map(
        functools.partial(on_device, nb, zs),
        mesh=mesh,
        in_specs=(
            P("seq", "ch"),
            P(None, "ch"),
            P(None, "seq", None, None),
            P(None, "seq"),
            P(None, "ch"),
            P("ch", None),
            P("seq", "ch"),
        ),
        out_specs=(P("seq", "ch"), P("seq", "ch"), P("seq", "ch")),
        check_vma=False,
    )
```

```python
import functools

import jax
import jax.numpy as jnp
from jax import lax
from jax.experimental import pallas as pl
from jax.experimental.pallas import tpu as pltpu
from jax.sharding import PartitionSpec as P

BLOCK = 64
LOCAL = 2
CH = 128
TILE = 16
SPLIT = BLOCK // TILE
TOP = BLOCK - TILE
MESH = pl.DeviceIdType.MESH
F32 = jnp.float32
BF16 = jnp.bfloat16
root_two_pi = 0.7978845608028654


def mod(value, size):
    return lax.rem(value + size, size)


def both(first, second, axis):
    return jnp.concatenate([first, second], axis=axis)


def forward_factor(weights, state, mates):
    return [
        jnp.dot(w, both(own, mate, 0), preferred_element_type=F32).astype(BF16)
        for w, own, mate in zip(weights, state, mates)
    ]


def transposed_terms(weights, grads):
    return [
        lax.dot_general(w, g, (((0,), (0,)), ((), ())), preferred_element_type=F32)
        for w, g in zip(weights, grads)
    ]


def kernel(nb, zs, *refs):
    (
        inputs, taps_hbm, mixing, pattern_hbm, w_in_hbm, w_out_hbm, cot,
        layer_out, conv_out, grad_out,
        x_v, cv, taps_ref, pattern, mixl, win, wout,
        halo, ghalo, st0, sx, st1, sy, wx, wy, wq,
        cot_all, cb1, cb_all, gb, mixed_all, hid, ga0, ga1, ga2, act, ghid,
        rs_send, rs_recv, rs_own, ro_send, ro_recv, ro_own, term, grad_terms,
        g2, g1s, g1, g0s, g0, cross, out2, cs1, cs2, go_v,
        load_sem, save_sem, halo_sem, wx_sem, wq_sem, wr_sem, wz_sem, sx_sem, sy_sem,
        bx_sem, by_sem, br_sem, ring_sem, cr_sem, mr_sem, ax_sem, ay_sem, cx_sem, cy_sem,
        gy_sem, gx_sem, lo_sem, gh_sem,
    ) = refs
    levels = nb.bit_length() - 1
    rows = nb * BLOCK
    far = zs // 2
    parts = min(4, nb)
    size = nb // parts
    lines_of = size * BLOCK
    count = nb * nb
    s = lax.axis_index("seq")
    z = lax.axis_index("ch")
    y = lax.div(s, nb)
    q = lax.rem(s, nb)
    up = mod(z + 1, zs)
    down = mod(z - 1, zs)
    up2 = mod(z + 2, zs)
    down2 = mod(z - 2, zs)
    quarter = lax.rem(z, SPLIT)
    strip = pl.ds(pl.multiple_of(quarter * TILE, TILE), TILE)

    loads = [
        pltpu.make_async_copy(inputs, x_v, load_sem.at[0]),
        pltpu.make_async_copy(mixing.at[pl.ds(0, LOCAL)], mixl, load_sem.at[1]),
        pltpu.make_async_copy(w_out_hbm, wout, load_sem.at[2]),
        pltpu.make_async_copy(w_in_hbm, win, load_sem.at[3]),
        pltpu.make_async_copy(taps_hbm, taps_ref, load_sem.at[4]),
        pltpu.make_async_copy(pattern_hbm, pattern, load_sem.at[5]),
    ]
    for load in loads:
        load.start()

    barrier = pltpu.get_barrier_semaphore()

    def greet(seq, ch):
        pl.semaphore_signal(barrier, inc=1, device_id=(seq, ch), device_id_type=MESH)

    @pl.when(s > 0)
    def _():
        greet(s - 1, z)

    @pl.when(s < count - 1)
    def _():
        greet(s + 1, z)

    for d in range(1, nb):
        greet(y * nb + mod(q + d, nb), z)
        greet(mod(y + d, nb) * nb + q, z)
    greet(s, up)
    greet(s, down)
    greet(s, up2)
    greet(s, down2)
    ends = jnp.where(s > 0, 1, 0) + jnp.where(s < count - 1, 1, 0)
    pl.semaphore_wait(barrier, 2 * (nb - 1) + 4 + ends)

    def arrival(view, sem):
        pltpu.make_async_copy(view, view, sem).wait()

    class Swap:
        def __init__(self, src, dst, sems, slot, peer, pick_src=None, pick_dst=None, many_src=None, many_dst=None):
            self.src, self.dst, self.sems, self.slot, self.peer = src, dst, sems, slot, peer
            self.pick_src, self.pick_dst = pick_src or first, pick_dst or first
            self.many_src, self.many_dst = many_src or several, many_dst or several

        def recv_sem(self, t):
            return self.sems.at[1]

        def remote(self, t, into):
            return pltpu.make_async_remote_copy(
                src_ref=self.pick_src(self.src, t),
                dst_ref=self.pick_dst(self.dst, into),
                send_sem=self.sems.at[0],
                recv_sem=self.recv_sem(into),
                device_id=(self.peer(t), z),
                device_id_type=MESH,
            )

        def own(self):
            return pltpu.make_async_copy(
                self.pick_src(self.src, self.slot), self.pick_dst(self.dst, self.slot), self.recv_sem(self.slot)
            )

        def start(self):
            for d in range(1, nb):
                self.remote(mod(self.slot + d, nb), self.slot).start()
            self.own().start()

        def wait(self):
            arrival(self.many_dst(self.dst, nb), self.sems.at[1])

        def drain(self):
            arrival(self.many_src(self.src, nb - 1), self.sems.at[0])

    class Stream(Swap):
        def recv_sem(self, t):
            return self.sems.at[1 + t]

        def wait(self, t):
            arrival(self.pick_dst(self.dst, t), self.recv_sem(t))

    def first(ref, t):
        return ref.at[t]

    def several(ref, n):
        return ref.at[pl.ds(0, n)]

    def by_q(t):
        return y * nb + t

    def by_y(t):
        return t * nb + q

    class Turn:
        def __init__(self, src, dst, sems):
            self.src, self.dst, self.sems = src, dst, sems

        def start(self, blocks):
            for t in blocks:
                into = self.dst.at[pl.ds(q * BLOCK, BLOCK)]

                @pl.when(t * nb + y != s)
                def _():
                    pltpu.make_async_remote_copy(
                        src_ref=self.src.at[t], dst_ref=into, send_sem=self.sems.at[0], recv_sem=self.sems.at[1],
                        device_id=(t * nb + y, z), device_id_type=MESH,
                    ).start()

                @pl.when(t * nb + y == s)
                def _():
                    pltpu.make_async_copy(self.src.at[t], into, self.sems.at[1]).start()

        def wait(self):
            arrival(self.dst, self.sems.at[1])

        def drain(self):
            @pl.when(y == q)
            def _():
                arrival(self.src.at[pl.ds(0, nb - 1)], self.sems.at[0])

            @pl.when(y != q)
            def _():
                arrival(self.src, self.sems.at[0])

    def ours(way, p, count=parts):
        return (p < count // 2) == (way == 0)

    class Gather:
        def __init__(self, buf, parts, pick, first_pick, send_sem, sems):
            self.parts = parts
            self.buf, self.pick, self.first_pick, self.send_sem, self.sems = buf, pick, first_pick, send_sem, sems

        def copy(self, way, step, p, chunk):
            part = self.pick(chunk, p)
            return pltpu.make_async_remote_copy(
                src_ref=self.first_pick(p) if step == 0 else part,
                dst_ref=part,
                send_sem=self.send_sem.at[0],
                recv_sem=self.sems.at[way, step, p],
                device_id=(s, up if way == 0 else down),
                device_id_type=MESH,
            )

        def chunk(self, way, step):
            return mod(z - step, zs) if way == 0 else mod(z + step, zs)

        def each(self, step):
            for p in range(self.parts):
                for way in range(2):
                    if step < far - 1 or ours(way, p, self.parts):
                        yield way, p

        def came(self, way, step, p):
            part = self.pick(self.chunk(way, step + 1), p)
            return pltpu.make_async_remote_copy(
                src_ref=part,
                dst_ref=part,
                send_sem=self.send_sem.at[0],
                recv_sem=self.sems.at[way, step, p],
                device_id=(s, up if way == 0 else down),
                device_id_type=MESH,
            )

        def step(self, step):
            for p in range(self.parts):
                for way in range(2):
                    if step > 0:
                        self.came(way, step - 1, p).wait_recv()
                    if step < far - 1 or ours(way, p, self.parts):
                        self.copy(way, step, p, self.chunk(way, step)).start()

        def finish(self):
            for way, p in self.each(far - 1):
                self.came(way, far - 1, p).wait_recv()

        def drain(self):
            arrival(self.buf.at[pl.ds(0, zs - 1)], self.send_sem.at[0])

    class Scatter:
        def __init__(self, send, recv, own, send_sem, sems, pair, terms=None):
            self.send, self.recv, self.own, self.send_sem, self.sems, self.pair = send, recv, own, send_sem, sems, pair
            self.ahead = terms is not None
            self.terms = terms

        def prepare(self, k):
            near = z if k == far else mod(z - k, zs)
            self.term(k)[...] = self.pair(mod(z + k, zs), near)

        def term(self, k):
            return self.terms.at[far - k] if self.ahead else term

        def at(self, way, step, p):
            slot = zs - 2 if step == 0 else 2 * (step - 1) + way
            return slot, pl.ds(p * size, size)

        def copy(self, way, step, p):
            slot, blocks = self.at(way, step, p)
            return pltpu.make_async_remote_copy(
                src_ref=self.send.at[slot, blocks],
                dst_ref=self.recv.at[slot, blocks],
                send_sem=self.send_sem.at[0],
                recv_sem=self.sems.at[way, step, p],
                device_id=(s, up if way == 0 else down),
                device_id_type=MESH,
            )

        def arrived(self, way, step, p):
            if step < 0 or (step == 0 and not ours(way, p)):
                return None
            self.copy(way, step, p).wait_recv()
            slot, blocks = self.at(way, step, p)
            return self.recv[slot, blocks].astype(F32).reshape(lines_of, CH)

        def pass_on(self, way, step, p, value):
            slot, blocks = self.at(way, step, p)
            self.send[slot, blocks] = value.astype(BF16).reshape(size, BLOCK, CH)
            self.copy(way, step, p).start()

        def stage(self, k):
            step = far - k
            value_of = self.term(k)
            if k == far or not self.ahead:
                self.prepare(k)
            todo = [(way, p) for p in range(parts) for way in range(2)]
            if k == far:
                todo = [(way, p) for way, p in todo if ours(way, p)]
            elif k == far - 1:
                todo.sort(key=lambda item: ours(*item))
            for index, (way, p) in enumerate(todo):
                if k == far - 1 and index == parts and self.ahead:
                    for later in range(k - 1, 0, -1):
                        self.prepare(later)
                value = value_of[pl.ds(p * lines_of, lines_of), pl.ds(0 if k == far else way * CH, CH)]
                came = self.arrived(way, step - 1, p)
                self.pass_on(way, step, p, value if came is None else value + came)
            if k == far:
                self.own[...] = value_of[:, pl.ds(CH, CH)]
                if self.ahead and far > 1:
                    self.prepare(k - 1)

        def total(self, p):
            value = self.own[pl.ds(p * lines_of, lines_of), :]
            for way in range(2):
                came = self.arrived(way, far - 1, p)
                if came is not None:
                    value = value + came
            return value

        def finish(self):
            return jnp.concatenate([self.total(p) for p in range(parts)], axis=0)

        def drain(self):
            arrival(self.send, self.send_sem.at[0])

    class Spread:
        def __init__(self):
            hb = nb // 2
            self.cases = [
                (up, down, 1, pl.ds(0, nb)), (down, up, -1, pl.ds(0, nb)),
                (up2, down2, 2, pl.ds(0, hb)), (down2, up2, -2, pl.ds(hb, hb)),
            ]

        def copy(self, case, theirs):
            to, _, shift, slots = self.cases[case]
            index = lax.rem(quarter - shift + 2 * SPLIT, SPLIT) if theirs else quarter
            part = wy.at[pl.ds(0, levels), slots, pl.ds(pl.multiple_of(index * TILE, TILE), TILE)]
            return pltpu.make_async_remote_copy(
                src_ref=part, dst_ref=part, send_sem=wz_sem.at[0, case], recv_sem=wz_sem.at[1, case],
                device_id=(s, to), device_id_type=MESH,
            )

        def start(self):
            for case in range(4):
                self.copy(case, False).start()

        def wait(self):
            for case in range(4):
                self.copy(case, True).wait_recv()

        def drain(self):
            for case in range(4):
                self.copy(case, False).wait_send()

    def rim(src_head, src_tail, dst, sems):
        return (
            pltpu.make_async_remote_copy(
                src_ref=src_tail, dst_ref=dst.at[0], send_sem=sems.at[0, 0], recv_sem=sems.at[1, 0],
                device_id=(s + 1, z), device_id_type=MESH,
            ),
            pltpu.make_async_remote_copy(
                src_ref=src_head, dst_ref=dst.at[1], send_sem=sems.at[0, 1], recv_sem=sems.at[1, 1],
                device_id=(s - 1, z), device_id_type=MESH,
            ),
        )

    def rim_start(pair, dst):
        @pl.when(s < count - 1)
        def _():
            pair[0].start()

        @pl.when(s > 0)
        def _():
            pair[1].start()

        @pl.when(s == 0)
        def _():
            dst[0] = jnp.zeros((TILE, CH), BF16)

        @pl.when(s == count - 1)
        def _():
            dst[1] = jnp.zeros((TILE, CH), BF16)

    def rim_wait(pair):
        @pl.when(s > 0)
        def _():
            pair[0].wait_recv()

        @pl.when(s < count - 1)
        def _():
            pair[1].wait_recv()

    def rim_drain(pair):
        @pl.when(s < count - 1)
        def _():
            pair[0].wait_send()

        @pl.when(s > 0)
        def _():
            pair[1].wait_send()

    def convolve(value, edges, before, same, after):
        value = value.astype(F32)
        line = lax.broadcasted_iota(jnp.int32, value.shape, 0)
        above = edges[0].astype(F32)[TILE - 1 : TILE, :]
        below = edges[1].astype(F32)[0:1, :]
        earlier = jnp.where(line == 0, above, pltpu.roll(value, 1, 0))
        later = jnp.where(line == rows - 1, below, pltpu.roll(value, rows - 1, 0))
        return (before * earlier + same * value + after * later).astype(BF16)

    def put(ref, blocks):
        for i, block in enumerate(blocks):
            ref[i] = block

    def forward_levels(weights, state):
        for level in range(levels):
            state = forward_factor(
                [weights[level, i] for i in range(nb)], state, [state[i ^ (1 << level)] for i in range(nb)]
            )
        return state

    def backward_levels(weights, grads):
        for level in reversed(range(levels)):
            terms = transposed_terms([weights[level, i] for i in range(nb)], grads)
            grads = [
                (terms[i][:BLOCK] + terms[i ^ (1 << level)][BLOCK:]).astype(BF16) for i in range(nb)
            ]
        return grads

    edges = rim(inputs.at[pl.ds(0, TILE)], inputs.at[pl.ds(rows - TILE, TILE)], halo, halo_sem)
    rim_start(edges, halo)
    upper, last = pl.ds(0, TOP), pl.ds(TOP, TILE)
    cot_ring = Gather(
        cot_all, parts,
        lambda chunk, p: cot_all.at[chunk, pl.ds(p * size, size)],
        lambda p: cot.at[pl.ds(p * size, size), upper], ring_sem.at[pl.ds(0, 1)], cr_sem,
    )
    cot_ring.step(0)
    own_cot = pltpu.make_async_copy(cot.at[pl.ds(0, nb), upper], cot_all.at[z], load_sem.at[6])
    own_cot.start()
    low, high = pl.ds(LOCAL, levels), pl.ds(LOCAL + levels, levels)
    every = pl.ds(0, levels)
    wq_swap = Swap(
        mixing, wq, wq_sem, q, by_q,
        lambda ref, t: ref.at[high, t, strip], lambda ref, t: ref.at[every, t],
        lambda ref, n: ref.at[high, pl.ds(0, n), strip], lambda ref, n: ref.at[every, pl.ds(0, n)],
    )
    wq_swap.start()
    wx_swap = Swap(
        mixing, wx, wx_sem, q, by_q,
        lambda ref, t: ref.at[low, t], lambda ref, t: ref.at[every, t],
        lambda ref, n: ref.at[low, pl.ds(0, n)], lambda ref, n: ref.at[every, pl.ds(0, n)],
    )
    wx_swap.start()

    loads[4].wait()
    taps = taps_ref[...].astype(F32)
    tap0, tap1, tap2 = taps[0:1], taps[1:2], taps[2:3]
    loads[0].wait()
    rim_wait(edges)
    cv[...] = convolve(x_v[...], (halo[0], halo[1]), tap0, tap1, tap2)
    conv_save = pltpu.make_async_copy(cv, conv_out, save_sem.at[0])
    conv_save.start()
    st0[...] = cv[...].reshape(nb, BLOCK, CH)
    loads[1].wait()
    loads[5].wait()
    for factor in range(LOCAL):
        state = [st0[i] for i in range(nb)]
        mates = [st0[pattern[factor, i]] for i in range(nb)]
        put(st0, forward_factor([mixl[factor, i] for i in range(nb)], state, mates))

    sx_swap = Swap(st0, sx, sx_sem, q, by_q)
    sx_swap.start()
    bx_swap = Swap(
        cot, cb1, bx_sem, q, by_q,
        lambda ref, t: ref.at[t, last], None, lambda ref, n: ref.at[pl.ds(0, n), last],
    )
    bx_swap.start()
    if far > 1:
        cot_ring.step(1)
    wq_swap.wait()
    wr_swap = Swap(
        wq, wy, wr_sem, y, by_y,
        lambda ref, t: ref.at[every, t], lambda ref, t: ref.at[every, t, strip],
        lambda ref, n: ref.at[every, pl.ds(0, n)], lambda ref, n: ref.at[every, pl.ds(0, n), strip],
    )
    wr_swap.start()
    if far > 2:
        cot_ring.step(2)
    wx_swap.wait()
    sx_swap.wait()
    put(st1, forward_levels(wx, [sx[i] for i in range(nb)]))

    sy_swap = Swap(st1, sy, sy_sem, y, by_y)
    sy_swap.start()
    for step in range(3, far):
        cot_ring.step(step)
    wr_swap.wait()
    spread = Spread()
    spread.start()
    bx_swap.wait()
    by_swap = Swap(
        cb1, cb_all, by_sem, y, by_y, None, lambda ref, t: ref.at[z, t], None, lambda ref, n: ref.at[z, pl.ds(0, n)]
    )
    by_swap.start()

    def channels(index):
        return pl.ds(pl.multiple_of(index * CH, CH), CH)

    def grad_act(buf):
        value = None
        lines = buf.shape[1] * buf.shape[2]
        for c in range(0, zs, 2):
            part = lax.dot_general(
                both(buf[c].reshape(lines, CH), buf[c + 1].reshape(lines, CH), 1), wout[:, pl.ds(c * CH, 2 * CH)],
                (((1,), (1,)), ((), ())), preferred_element_type=F32,
            )
            value = part if value is None else value + part
        return value

    cot_ring.finish()
    own_cot.wait()
    loads[2].wait()
    ga0[...] = grad_act(cot_all).astype(BF16).reshape(ga0.shape)
    ax_swap = Stream(ga0, ga1, ax_sem, q, by_q)
    ax_swap.start()
    cx_swap = Swap(
        cot, cs1, cx_sem, q, by_q,
        lambda ref, t: ref.at[t, upper], None, lambda ref, n: ref.at[pl.ds(0, n), upper],
    )
    cx_swap.start()
    sy_swap.wait()
    spread.wait()
    mixed = forward_levels(wy, [sy[i] for i in range(nb)])
    for i in range(nb):
        mixed_all[z, i] = mixed[i]
    mixed_ring = Gather(
        mixed_all, parts,
        lambda chunk, p: mixed_all.at[chunk, pl.ds(p * size, size)],
        lambda p: mixed_all.at[z, pl.ds(p * size, size)], ring_sem.at[pl.ds(1, 1)], mr_sem,
    )
    mixed_ring.step(0)
    by_swap.wait()
    wide = nb // 2
    last_ring = Gather(
        cb_all, 2,
        lambda chunk, p: cb_all.at[chunk, pl.ds(p * wide, wide)],
        lambda p: cb_all.at[z, pl.ds(p * wide, wide)], ring_sem.at[pl.ds(4, 1)], br_sem,
    )
    last_ring.step(0)

    def add_hidden(a, b, start):
        value = jnp.dot(
            both(mixed_all[a].reshape(rows, CH), mixed_all[b].reshape(rows, CH), 1),
            both(win[channels(a), :], win[channels(b), :], 0),
            preferred_element_type=F32,
        )
        hid[...] = value if start else hid[...] + value

    ay_swap = Swap(ga1, ga2, ay_sem, y, by_y)
    cy_swap = Swap(cs1, cs2, cy_sem, y, by_y)
    loads[3].wait()
    for step in range(1, far):
        mixed_ring.step(step)
        last_ring.step(step)
        add_hidden(mod(z - step, zs), mod(z + step, zs), step == 1)
        if step == 1:
            for d in range(nb):
                t = mod(q + d, nb)
                ax_swap.wait(t)

                @pl.when(t == y)
                def _():
                    ay_swap.own().start()

                @pl.when(t != y)
                def _():
                    ay_swap.remote(t, y).start()
    cx_swap.wait()
    cy_swap.start()
    last_ring.finish()
    gb[...] = grad_act(cb_all)
    mixed_ring.finish()
    add_hidden(z, mod(z + far, zs), far == 1)
    ay_swap.wait()

    @pl.loop(0, nb)
    def _(i):
        lines = pl.ds(pl.multiple_of(i * BLOCK, BLOCK), BLOCK)
        v = hid[lines, :]
        square = v * v
        tanh_val = jnp.tanh(root_two_pi * (v + 0.044715 * square * v))
        plus = 0.5 * (1.0 + tanh_val)
        act[lines, :] = (v * plus).astype(BF16)
        slope = root_two_pi * (1.0 + 3.0 * 0.044715 * square)
        slope = plus + 0.5 * v * (1.0 - tanh_val * tanh_val) * slope
        strip_of = pl.ds(pl.multiple_of(i * TILE, TILE), TILE)
        slope_in = both(ga2[i].astype(F32), gb[strip_of, :], 0)
        ghid[lines, :] = (slope_in * slope).astype(BF16)

    def grad_pair(a, b):
        return lax.dot_general(
            ghid[...], both(win[channels(a), :], win[channels(b), :], 0),
            (((1,), (1,)), ((), ())), preferred_element_type=F32,
        )

    def out_pair(a, b):
        return jnp.dot(
            act[...], both(wout[:, channels(a)], wout[:, channels(b)], 1), preferred_element_type=F32
        )

    grad_sum = Scatter(rs_send, rs_recv, rs_own, ring_sem.at[pl.ds(2, 1)], mr_sem, grad_pair, grad_terms)
    out_sum = Scatter(ro_send, ro_recv, ro_own, ring_sem.at[pl.ds(3, 1)], cr_sem, out_pair)
    for k in range(far, 1, -1):
        grad_sum.stage(k)
    out_sum.stage(far)
    grad_sum.stage(1)
    rest = list(range(far - 1, 0, -1))
    for k in rest[:1]:
        out_sum.stage(k)
    cy_swap.wait()
    total = grad_sum.finish()
    own_grad = both(cs2[...], cb_all[z], 1).astype(F32).reshape(rows, CH)
    grad_mixed = (own_grad + total).astype(BF16).reshape(nb, BLOCK, CH)

    put(g2, backward_levels(wy, [grad_mixed[i] for i in range(nb)]))
    gy_swap = Swap(g2, g1, gy_sem, y, by_y)
    gy_swap.start()
    for k in rest[1:2]:
        out_sum.stage(k)
    for k in rest[2:]:
        out_sum.stage(k)
    gy_swap.wait()
    put(g1s, backward_levels(wx, [g1[i] for i in range(nb)]))
    gx_swap = Swap(g1s, g0, gx_sem, q, by_q)
    gx_swap.start()
    lo_turn = Turn(out2, layer_out, lo_sem)
    for p in range(parts):
        blocks = pl.ds(p * size, size)
        whole = mixed_all[z, blocks].astype(F32).reshape(lines_of, CH) + out_sum.total(p)
        out2[blocks] = whole.astype(BF16).reshape(size, BLOCK, CH)
        lo_turn.start(range(p * size, (p + 1) * size))
    gx_swap.wait()
    grads = [g0[i] for i in range(nb)]
    for factor in reversed(range(LOCAL)):
        terms = transposed_terms([mixl[factor, i] for i in range(nb)], grads)
        put(cross, [t[BLOCK:] for t in terms])
        grads = [(terms[i][:BLOCK] + cross[pattern[factor, i]]).astype(BF16) for i in range(nb)]
    put(g0s, grads)
    gedges = rim(
        g0s.at[0, pl.ds(0, TILE)], g0s.at[nb - 1, pl.ds(BLOCK - TILE, TILE)], ghalo, gh_sem
    )
    rim_start(gedges, ghalo)
    rim_wait(gedges)
    go_v[...] = convolve(g0s[...].reshape(rows, CH), (ghalo[0], ghalo[1]), tap2, tap1, tap0)
    grad_save = pltpu.make_async_copy(go_v, grad_out, save_sem.at[1])
    grad_save.start()

    rim_drain(edges)
    rim_drain(gedges)
    for transfer in (
        wq_swap, wx_swap, wr_swap, spread, sx_swap, sy_swap, ax_swap, ay_swap, cx_swap, cy_swap, bx_swap, by_swap,
        cot_ring, last_ring, mixed_ring, grad_sum, out_sum, gy_swap, gx_swap, lo_turn,
    ):
        transfer.drain()
    conv_save.wait()
    lo_turn.wait()
    grad_save.wait()


def publish(*refs):
    sources, targets, sem = refs[:3], refs[3:6], refs[6]
    copies = [pltpu.make_async_copy(a, b, sem.at[i]) for i, (a, b) in enumerate(zip(sources, targets))]
    for copy in copies:
        copy.start()
    for copy in copies:
        copy.wait()


def on_device(nb, zs, inputs, conv_weight, mixing, pattern, w_in, w_out, cotangent):
    rows, _ = inputs.shape
    levels = nb.bit_length() - 1
    hidden = w_in.shape[1]
    channels = w_in.shape[0]
    far = zs // 2
    vmem = pltpu.VMEM
    dma = pltpu.SemaphoreType.DMA
    blocks = (nb, BLOCK, CH)
    parts = min(4, nb)
    deep = (nb, TOP, hidden)
    scratch = [
        vmem((rows, CH), BF16),
        vmem((rows, CH), BF16),
        vmem(conv_weight.shape, BF16),
        pltpu.SMEM(pattern.shape, jnp.int32),
        vmem((LOCAL, *blocks), BF16),
        vmem((channels, hidden), BF16),
        vmem((hidden, channels), BF16),
        vmem((2, TILE, CH), BF16),
        vmem((2, TILE, CH), BF16),
        *[vmem(blocks, BF16)] * 4,
        *[vmem((levels, *blocks), BF16)] * 2,
        vmem((levels, nb, TILE, CH), BF16),
        vmem((zs, nb, TOP, CH), BF16),
        vmem((nb, TILE, CH), BF16),
        vmem((zs, nb, TILE, CH), BF16),
        vmem((nb * TILE, hidden), F32),
        vmem((zs, *blocks), BF16),
        vmem((rows, hidden), F32),
        *[vmem(deep, BF16)] * 3,
        *[vmem((rows, hidden), BF16)] * 2,
        *[vmem((zs - 1, *blocks), BF16)] * 2,
        vmem((rows, CH), F32),
        *[vmem((zs - 1, *blocks), BF16)] * 2,
        vmem((rows, CH), F32),
        vmem((rows, 2 * CH), F32),
        vmem((far, rows, 2 * CH), F32),
        *[vmem(blocks, BF16)] * 5,
        vmem(blocks, F32),
        vmem(blocks, BF16),
        *[vmem((nb, TOP, CH), BF16)] * 2,
        vmem((rows, CH), BF16),
        dma((7,)),
        dma((2,)),
        dma((2, 2)),
        *[dma((2,))] * 3,
        dma((2, 4)),
        *[dma((2,))] * 4,
        dma((2, far, 2)),
        dma((5,)),
        *[dma((2, far, parts))] * 2,
        dma((1 + nb,)),
        *[dma((2,))] * 6,
        dma((2, 2)),
    ]
    out = jax.ShapeDtypeStruct((rows, CH), BF16)
    hbm = pl.BlockSpec(memory_space=pl.ANY)
    results = pl.pallas_call(
        functools.partial(kernel, nb, zs),
        out_shape=(out, out, out),
        in_specs=[hbm] * 7,
        out_specs=(hbm, hbm, hbm),
        scratch_shapes=scratch,
        compiler_params=pltpu.CompilerParams(
            collective_id=0, has_side_effects=True, vmem_limit_bytes=28 * 1024 * 1024
        ),
    )(*[pltpu.with_memory_space_constraint(v, pltpu.HBM) for v in (
        inputs, conv_weight, mixing, pattern, w_in, w_out, cotangent.reshape(blocks)
    )])
    return pl.pallas_call(
        publish,
        out_shape=(out, out, out),
        in_specs=[pl.BlockSpec(memory_space=pltpu.VMEM)] * 3,
        out_specs=(hbm, hbm, hbm),
        scratch_shapes=[dma((3,))],
        compiler_params=pltpu.CompilerParams(vmem_limit_bytes=4 * 1024 * 1024),
    )(*results)


def solution(mesh):
    seq, zs = mesh.shape["seq"], mesh.shape["ch"]
    nb = 1 << ((seq.bit_length() - 1) // 2)
    return jax.shard_map(
        functools.partial(on_device, nb, zs),
        mesh=mesh,
        in_specs=(
            P("seq", "ch"),
            P(None, "ch"),
            P(None, "seq", None, None),
            P(None, "seq"),
            P(None, "ch"),
            P("ch", None),
            P("seq", "ch"),
        ),
        out_specs=(P("seq", "ch"), P("seq", "ch"), P("seq", "ch")),
        check_vma=False,
    )
```

```python
import functools

import jax
import jax.numpy as jnp
from jax import lax
from jax.experimental import pallas as pl
from jax.experimental.pallas import tpu as pltpu
from jax.sharding import PartitionSpec as P

BLOCK = 64
LOCAL = 2
CH = 128
TILE = 16
SPLIT = BLOCK // TILE
TOP = BLOCK - TILE
MESH = pl.DeviceIdType.MESH
F32 = jnp.float32
BF16 = jnp.bfloat16
root_two_pi = 0.7978845608028654


def mod(value, size):
    return lax.rem(value + size, size)


def both(first, second, axis):
    return jnp.concatenate([first, second], axis=axis)


def forward_factor(weights, state, mates):
    return [
        jnp.dot(w, both(own, mate, 0), preferred_element_type=F32).astype(BF16)
        for w, own, mate in zip(weights, state, mates)
    ]


def transposed_terms(weights, grads):
    return [
        lax.dot_general(w, g, (((0,), (0,)), ((), ())), preferred_element_type=F32)
        for w, g in zip(weights, grads)
    ]


def kernel(nb, zs, *refs):
    (
        inputs, taps_hbm, mixing, pattern_hbm, w_in_hbm, w_out_hbm, cot,
        layer_out, conv_out, grad_out,
        x_v, cv, taps_ref, pattern, mixl, win, wout,
        halo, ghalo, st0, sx, st1, sy, wx, wy, wq,
        cot_all, cb1, cb_all, gb, mixed_all, hid, ga0, ga1, ga2, act, ghid,
        rs_send, rs_recv, rs_own, ro_send, ro_recv, ro_own, term, grad_terms,
        g2, g1s, g1, g0s, g0, cross, out2, cs1, cs2, go_v,
        load_sem, save_sem, halo_sem, wx_sem, wq_sem, wr_sem, wz_sem, sx_sem, sy_sem,
        bx_sem, by_sem, ring_sem, cr_sem, mr_sem, ax_sem, ay_sem, cx_sem, cy_sem,
        gy_sem, gx_sem, lo_sem, gh_sem,
    ) = refs
    levels = nb.bit_length() - 1
    rows = nb * BLOCK
    far = zs // 2
    parts = min(4, nb)
    size = nb // parts
    lines_of = size * BLOCK
    count = nb * nb
    s = lax.axis_index("seq")
    z = lax.axis_index("ch")
    y = lax.div(s, nb)
    q = lax.rem(s, nb)
    up = mod(z + 1, zs)
    down = mod(z - 1, zs)
    up2 = mod(z + 2, zs)
    down2 = mod(z - 2, zs)
    quarter = lax.rem(z, SPLIT)
    strip = pl.ds(pl.multiple_of(quarter * TILE, TILE), TILE)

    loads = [
        pltpu.make_async_copy(inputs, x_v, load_sem.at[0]),
        pltpu.make_async_copy(mixing.at[pl.ds(0, LOCAL)], mixl, load_sem.at[1]),
        pltpu.make_async_copy(w_out_hbm, wout, load_sem.at[2]),
        pltpu.make_async_copy(w_in_hbm, win, load_sem.at[3]),
        pltpu.make_async_copy(taps_hbm, taps_ref, load_sem.at[4]),
        pltpu.make_async_copy(pattern_hbm, pattern, load_sem.at[5]),
    ]
    for load in loads:
        load.start()

    barrier = pltpu.get_barrier_semaphore()

    def greet(seq, ch):
        pl.semaphore_signal(barrier, inc=1, device_id=(seq, ch), device_id_type=MESH)

    @pl.when(s > 0)
    def _():
        greet(s - 1, z)

    @pl.when(s < count - 1)
    def _():
        greet(s + 1, z)

    for d in range(1, nb):
        greet(y * nb + mod(q + d, nb), z)
        greet(mod(y + d, nb) * nb + q, z)
    greet(s, up)
    greet(s, down)
    greet(s, up2)
    greet(s, down2)
    ends = jnp.where(s > 0, 1, 0) + jnp.where(s < count - 1, 1, 0)
    pl.semaphore_wait(barrier, 2 * (nb - 1) + 4 + ends)

    def arrival(view, sem):
        pltpu.make_async_copy(view, view, sem).wait()

    class Swap:
        def __init__(self, src, dst, sems, slot, peer, pick_src=None, pick_dst=None, many_src=None, many_dst=None):
            self.src, self.dst, self.sems, self.slot, self.peer = src, dst, sems, slot, peer
            self.pick_src, self.pick_dst = pick_src or first, pick_dst or first
            self.many_src, self.many_dst = many_src or several, many_dst or several

        def recv_sem(self, t):
            return self.sems.at[1]

        def remote(self, t, into):
            return pltpu.make_async_remote_copy(
                src_ref=self.pick_src(self.src, t),
                dst_ref=self.pick_dst(self.dst, into),
                send_sem=self.sems.at[0],
                recv_sem=self.recv_sem(into),
                device_id=(self.peer(t), z),
                device_id_type=MESH,
            )

        def own(self):
            return pltpu.make_async_copy(
                self.pick_src(self.src, self.slot), self.pick_dst(self.dst, self.slot), self.recv_sem(self.slot)
            )

        def start(self):
            for d in range(1, nb):
                self.remote(mod(self.slot + d, nb), self.slot).start()
            self.own().start()

        def wait(self):
            arrival(self.many_dst(self.dst, nb), self.sems.at[1])

        def drain(self):
            arrival(self.many_src(self.src, nb - 1), self.sems.at[0])

    class Stream(Swap):
        def recv_sem(self, t):
            return self.sems.at[1 + t]

        def wait(self, t):
            arrival(self.pick_dst(self.dst, t), self.recv_sem(t))

    def first(ref, t):
        return ref.at[t]

    def several(ref, n):
        return ref.at[pl.ds(0, n)]

    def by_q(t):
        return y * nb + t

    def by_y(t):
        return t * nb + q

    class Turn:
        def __init__(self, src, dst, sems):
            self.src, self.dst, self.sems = src, dst, sems

        def start(self, blocks):
            for t in blocks:
                into = self.dst.at[pl.ds(q * BLOCK, BLOCK)]

                @pl.when(t * nb + y != s)
                def _():
                    pltpu.make_async_remote_copy(
                        src_ref=self.src.at[t], dst_ref=into, send_sem=self.sems.at[0], recv_sem=self.sems.at[1],
                        device_id=(t * nb + y, z), device_id_type=MESH,
                    ).start()

                @pl.when(t * nb + y == s)
                def _():
                    pltpu.make_async_copy(self.src.at[t], into, self.sems.at[1]).start()

        def wait(self):
            arrival(self.dst, self.sems.at[1])

        def drain(self):
            @pl.when(y == q)
            def _():
                arrival(self.src.at[pl.ds(0, nb - 1)], self.sems.at[0])

            @pl.when(y != q)
            def _():
                arrival(self.src, self.sems.at[0])

    def ours(way, p, count=parts):
        return (p < count // 2) == (way == 0)

    class Gather:
        def __init__(self, buf, parts, pick, first_pick, send_sem, sems):
            self.parts = parts
            self.buf, self.pick, self.first_pick, self.send_sem, self.sems = buf, pick, first_pick, send_sem, sems

        def copy(self, way, step, p, chunk):
            part = self.pick(chunk, p)
            return pltpu.make_async_remote_copy(
                src_ref=self.first_pick(p) if step == 0 else part,
                dst_ref=part,
                send_sem=self.send_sem.at[0],
                recv_sem=self.sems.at[way, step, p],
                device_id=(s, up if way == 0 else down),
                device_id_type=MESH,
            )

        def chunk(self, way, step):
            return mod(z - step, zs) if way == 0 else mod(z + step, zs)

        def each(self, step):
            for p in range(self.parts):
                for way in range(2):
                    if step < far - 1 or ours(way, p, self.parts):
                        yield way, p

        def came(self, way, step, p):
            part = self.pick(self.chunk(way, step + 1), p)
            return pltpu.make_async_remote_copy(
                src_ref=part,
                dst_ref=part,
                send_sem=self.send_sem.at[0],
                recv_sem=self.sems.at[way, step, p],
                device_id=(s, up if way == 0 else down),
                device_id_type=MESH,
            )

        def step(self, step):
            for p in range(self.parts):
                for way in range(2):
                    if step > 0:
                        self.came(way, step - 1, p).wait_recv()
                    if step < far - 1 or ours(way, p, self.parts):
                        self.copy(way, step, p, self.chunk(way, step)).start()

        def finish(self):
            for way, p in self.each(far - 1):
                self.came(way, far - 1, p).wait_recv()

        def drain(self):
            arrival(self.buf.at[pl.ds(0, zs - 1)], self.send_sem.at[0])

    class Scatter:
        def __init__(self, send, recv, own, send_sem, sems, pair, terms=None):
            self.send, self.recv, self.own, self.send_sem, self.sems, self.pair = send, recv, own, send_sem, sems, pair
            self.ahead = terms is not None
            self.terms = terms

        def prepare(self, k):
            near = z if k == far else mod(z - k, zs)
            self.term(k)[...] = self.pair(mod(z + k, zs), near)

        def term(self, k):
            return self.terms.at[far - k] if self.ahead else term

        def at(self, way, step, p):
            slot = zs - 2 if step == 0 else 2 * (step - 1) + way
            return slot, pl.ds(p * size, size)

        def copy(self, way, step, p):
            slot, blocks = self.at(way, step, p)
            return pltpu.make_async_remote_copy(
                src_ref=self.send.at[slot, blocks],
                dst_ref=self.recv.at[slot, blocks],
                send_sem=self.send_sem.at[0],
                recv_sem=self.sems.at[way, step, p],
                device_id=(s, up if way == 0 else down),
                device_id_type=MESH,
            )

        def arrived(self, way, step, p):
            if step < 0 or (step == 0 and not ours(way, p)):
                return None
            self.copy(way, step, p).wait_recv()
            slot, blocks = self.at(way, step, p)
            return self.recv[slot, blocks].astype(F32).reshape(lines_of, CH)

        def pass_on(self, way, step, p, value):
            slot, blocks = self.at(way, step, p)
            self.send[slot, blocks] = value.astype(BF16).reshape(size, BLOCK, CH)
            self.copy(way, step, p).start()

        def stage(self, k):
            step = far - k
            value_of = self.term(k)
            if k == far or not self.ahead:
                self.prepare(k)
            todo = [(way, p) for p in range(parts) for way in range(2)]
            if k == far:
                todo = [(way, p) for way, p in todo if ours(way, p)]
            elif k == far - 1:
                todo.sort(key=lambda item: ours(*item))
            for index, (way, p) in enumerate(todo):
                if k == far - 1 and index == parts and self.ahead:
                    for later in range(k - 1, 0, -1):
                        self.prepare(later)
                value = value_of[pl.ds(p * lines_of, lines_of), pl.ds(0 if k == far else way * CH, CH)]
                came = self.arrived(way, step - 1, p)
                self.pass_on(way, step, p, value if came is None else value + came)
            if k == far:
                self.own[...] = value_of[:, pl.ds(CH, CH)]
                if self.ahead and far > 1:
                    self.prepare(k - 1)

        def total(self, p):
            value = self.own[pl.ds(p * lines_of, lines_of), :]
            for way in range(2):
                came = self.arrived(way, far - 1, p)
                if came is not None:
                    value = value + came
            return value

        def finish(self):
            return jnp.concatenate([self.total(p) for p in range(parts)], axis=0)

        def drain(self):
            arrival(self.send, self.send_sem.at[0])

    class Spread:
        def __init__(self):
            hb = nb // 2
            self.cases = [
                (up, down, 1, pl.ds(0, nb)), (down, up, -1, pl.ds(0, nb)),
                (up2, down2, 2, pl.ds(0, hb)), (down2, up2, -2, pl.ds(hb, hb)),
            ]

        def copy(self, case, level, theirs):
            to, _, shift, slots = self.cases[case]
            index = lax.rem(quarter - shift + 2 * SPLIT, SPLIT) if theirs else quarter
            part = wy.at[level, slots, pl.ds(pl.multiple_of(index * TILE, TILE), TILE)]
            return pltpu.make_async_remote_copy(
                src_ref=part, dst_ref=part, send_sem=wz_sem.at[0], recv_sem=wz_sem.at[1 + 4 * level + case],
                device_id=(s, to), device_id_type=MESH,
            )

        def start(self):
            for level in range(levels):
                for case in range(4):
                    self.copy(case, level, False).start()

        def wait(self, level):
            for case in range(4):
                self.copy(case, level, True).wait_recv()

        def drain(self):
            arrival(wy.at[pl.ds(0, levels), pl.ds(0, nb), pl.ds(0, 3 * TILE)], wz_sem.at[0])

    def rim(src_head, src_tail, dst, sems):
        return (
            pltpu.make_async_remote_copy(
                src_ref=src_tail, dst_ref=dst.at[0], send_sem=sems.at[0, 0], recv_sem=sems.at[1, 0],
                device_id=(s + 1, z), device_id_type=MESH,
            ),
            pltpu.make_async_remote_copy(
                src_ref=src_head, dst_ref=dst.at[1], send_sem=sems.at[0, 1], recv_sem=sems.at[1, 1],
                device_id=(s - 1, z), device_id_type=MESH,
            ),
        )

    def rim_start(pair, dst):
        @pl.when(s < count - 1)
        def _():
            pair[0].start()

        @pl.when(s > 0)
        def _():
            pair[1].start()

        @pl.when(s == 0)
        def _():
            dst[0] = jnp.zeros((TILE, CH), BF16)

        @pl.when(s == count - 1)
        def _():
            dst[1] = jnp.zeros((TILE, CH), BF16)

    def rim_wait(pair):
        @pl.when(s > 0)
        def _():
            pair[0].wait_recv()

        @pl.when(s < count - 1)
        def _():
            pair[1].wait_recv()

    def rim_drain(pair):
        @pl.when(s < count - 1)
        def _():
            pair[0].wait_send()

        @pl.when(s > 0)
        def _():
            pair[1].wait_send()

    def convolve(value, edges, before, same, after):
        value = value.astype(F32)
        line = lax.broadcasted_iota(jnp.int32, value.shape, 0)
        above = edges[0].astype(F32)[TILE - 1 : TILE, :]
        below = edges[1].astype(F32)[0:1, :]
        earlier = jnp.where(line == 0, above, pltpu.roll(value, 1, 0))
        later = jnp.where(line == rows - 1, below, pltpu.roll(value, rows - 1, 0))
        return (before * earlier + same * value + after * later).astype(BF16)

    def put(ref, blocks):
        for i, block in enumerate(blocks):
            ref[i] = block

    def forward_levels(weights, state, before=None):
        for level in range(levels):
            if before is not None:
                before(level)
            state = forward_factor(
                [weights[level, i] for i in range(nb)], state, [state[i ^ (1 << level)] for i in range(nb)]
            )
        return state

    def backward_levels(weights, grads):
        for level in reversed(range(levels)):
            terms = transposed_terms([weights[level, i] for i in range(nb)], grads)
            grads = [
                (terms[i][:BLOCK] + terms[i ^ (1 << level)][BLOCK:]).astype(BF16) for i in range(nb)
            ]
        return grads

    edges = rim(inputs.at[pl.ds(0, TILE)], inputs.at[pl.ds(rows - TILE, TILE)], halo, halo_sem)
    rim_start(edges, halo)
    upper, last = pl.ds(0, TOP), pl.ds(TOP, TILE)
    cot_ring = Gather(
        cot_all, parts,
        lambda chunk, p: cot_all.at[chunk, pl.ds(p * size, size)],
        lambda p: cot.at[pl.ds(p * size, size), upper], ring_sem.at[pl.ds(0, 1)], cr_sem,
    )
    cot_ring.step(0)
    own_cot = pltpu.make_async_copy(cot.at[pl.ds(0, nb), upper], cot_all.at[z], load_sem.at[6])
    own_cot.start()
    low, high = pl.ds(LOCAL, levels), pl.ds(LOCAL + levels, levels)
    every = pl.ds(0, levels)
    wq_swap = Swap(
        mixing, wq, wq_sem, q, by_q,
        lambda ref, t: ref.at[high, t, strip], lambda ref, t: ref.at[every, t],
        lambda ref, n: ref.at[high, pl.ds(0, n), strip], lambda ref, n: ref.at[every, pl.ds(0, n)],
    )
    wq_swap.start()
    wx_swap = Swap(
        mixing, wx, wx_sem, q, by_q,
        lambda ref, t: ref.at[low, t], lambda ref, t: ref.at[every, t],
        lambda ref, n: ref.at[low, pl.ds(0, n)], lambda ref, n: ref.at[every, pl.ds(0, n)],
    )
    wx_swap.start()

    loads[4].wait()
    taps = taps_ref[...].astype(F32)
    tap0, tap1, tap2 = taps[0:1], taps[1:2], taps[2:3]
    loads[0].wait()
    rim_wait(edges)
    cv[...] = convolve(x_v[...], (halo[0], halo[1]), tap0, tap1, tap2)
    conv_save = pltpu.make_async_copy(cv, conv_out, save_sem.at[0])
    conv_save.start()
    st0[...] = cv[...].reshape(nb, BLOCK, CH)
    loads[1].wait()
    loads[5].wait()
    for factor in range(LOCAL):
        state = [st0[i] for i in range(nb)]
        mates = [st0[pattern[factor, i]] for i in range(nb)]
        put(st0, forward_factor([mixl[factor, i] for i in range(nb)], state, mates))

    sx_swap = Swap(st0, sx, sx_sem, q, by_q)
    sx_swap.start()
    bx_swap = Swap(
        cot, cb1, bx_sem, q, by_q,
        lambda ref, t: ref.at[t, last], None, lambda ref, n: ref.at[pl.ds(0, n), last],
    )
    bx_swap.start()
    if far > 1:
        cot_ring.step(1)
    wq_swap.wait()
    wr_swap = Swap(
        wq, wy, wr_sem, y, by_y,
        lambda ref, t: ref.at[every, t], lambda ref, t: ref.at[every, t, strip],
        lambda ref, n: ref.at[every, pl.ds(0, n)], lambda ref, n: ref.at[every, pl.ds(0, n), strip],
    )
    wr_swap.start()
    if far > 2:
        cot_ring.step(2)
    wx_swap.wait()
    sx_swap.wait()
    put(st1, forward_levels(wx, [sx[i] for i in range(nb)]))

    sy_swap = Swap(st1, sy, sy_sem, y, by_y)
    sy_swap.start()
    for step in range(3, far):
        cot_ring.step(step)
    wr_swap.wait()
    spread = Spread()
    spread.start()
    bx_swap.wait()
    by_swap = Swap(
        cb1, cb_all, by_sem, y, by_y, None, lambda ref, t: ref.at[z, t], None, lambda ref, n: ref.at[z, pl.ds(0, n)]
    )
    by_swap.start()

    def channels(index):
        return pl.ds(pl.multiple_of(index * CH, CH), CH)

    def grad_act(buf):
        value = None
        lines = buf.shape[1] * buf.shape[2]
        for c in range(0, zs, 2):
            part = lax.dot_general(
                both(buf[c].reshape(lines, CH), buf[c + 1].reshape(lines, CH), 1), wout[:, pl.ds(c * CH, 2 * CH)],
                (((1,), (1,)), ((), ())), preferred_element_type=F32,
            )
            value = part if value is None else value + part
        return value

    cot_ring.finish()
    own_cot.wait()
    loads[2].wait()
    ga0[...] = grad_act(cot_all).astype(BF16).reshape(ga0.shape)
    ax_swap = Stream(ga0, ga1, ax_sem, q, by_q)
    ax_swap.start()
    cx_swap = Swap(
        cot, cs1, cx_sem, q, by_q,
        lambda ref, t: ref.at[t, upper], None, lambda ref, n: ref.at[pl.ds(0, n), upper],
    )
    cx_swap.start()
    sy_swap.wait()
    by_swap.wait()
    wide = nb // 2
    last_ring = Gather(
        cb_all, 2,
        lambda chunk, p: cb_all.at[chunk, pl.ds(p * wide, wide)],
        lambda p: cb_all.at[z, pl.ds(p * wide, wide)], ring_sem.at[pl.ds(4, 1)], cr_sem,
    )
    last_ring.step(0)
    mixed = forward_levels(wy, [sy[i] for i in range(nb)], spread.wait)
    for i in range(nb):
        mixed_all[z, i] = mixed[i]
    mixed_ring = Gather(
        mixed_all, parts,
        lambda chunk, p: mixed_all.at[chunk, pl.ds(p * size, size)],
        lambda p: mixed_all.at[z, pl.ds(p * size, size)], ring_sem.at[pl.ds(1, 1)], mr_sem,
    )
    mixed_ring.step(0)

    def add_hidden(a, b, start):
        value = jnp.dot(
            both(mixed_all[a].reshape(rows, CH), mixed_all[b].reshape(rows, CH), 1),
            both(win[channels(a), :], win[channels(b), :], 0),
            preferred_element_type=F32,
        )
        hid[...] = value if start else hid[...] + value

    def one_hidden(a):
        return jnp.dot(mixed_all[a].reshape(rows, CH), win[channels(a), :], preferred_element_type=F32)

    ay_swap = Swap(ga1, ga2, ay_sem, y, by_y)
    cy_swap = Swap(cs1, cs2, cy_sem, y, by_y)
    loads[3].wait()
    hid[...] = one_hidden(z)
    for step in range(1, far):
        last_ring.step(step)
        mixed_ring.step(step)
        add_hidden(mod(z - step, zs), mod(z + step, zs), False)
        if step == 1:
            for d in range(nb):
                t = mod(q + d, nb)
                ax_swap.wait(t)

                @pl.when(t == y)
                def _():
                    ay_swap.own().start()

                @pl.when(t != y)
                def _():
                    ay_swap.remote(t, y).start()
    cx_swap.wait()
    cy_swap.start()
    last_ring.finish()
    gb[...] = grad_act(cb_all)
    mixed_ring.finish()
    hid[...] += one_hidden(mod(z + far, zs))
    ay_swap.wait()

    @pl.loop(0, nb)
    def _(i):
        lines = pl.ds(pl.multiple_of(i * BLOCK, BLOCK), BLOCK)
        v = hid[lines, :]
        square = v * v
        tanh_val = jnp.tanh(root_two_pi * (v + 0.044715 * square * v))
        plus = 0.5 * (1.0 + tanh_val)
        act[lines, :] = (v * plus).astype(BF16)
        slope = root_two_pi * (1.0 + 3.0 * 0.044715 * square)
        slope = plus + 0.5 * v * (1.0 - tanh_val * tanh_val) * slope
        strip_of = pl.ds(pl.multiple_of(i * TILE, TILE), TILE)
        slope_in = both(ga2[i].astype(F32), gb[strip_of, :], 0)
        ghid[lines, :] = (slope_in * slope).astype(BF16)

    def grad_pair(a, b):
        return lax.dot_general(
            ghid[...], both(win[channels(a), :], win[channels(b), :], 0),
            (((1,), (1,)), ((), ())), preferred_element_type=F32,
        )

    def out_pair(a, b):
        return jnp.dot(
            act[...], both(wout[:, channels(a)], wout[:, channels(b)], 1), preferred_element_type=F32
        )

    grad_sum = Scatter(rs_send, rs_recv, rs_own, ring_sem.at[pl.ds(2, 1)], mr_sem, grad_pair, grad_terms)
    out_sum = Scatter(ro_send, ro_recv, ro_own, ring_sem.at[pl.ds(3, 1)], cr_sem, out_pair)
    for k in range(far, 1, -1):
        grad_sum.stage(k)
    out_sum.stage(far)
    grad_sum.stage(1)
    rest = list(range(far - 1, 0, -1))
    for k in rest[:1]:
        out_sum.stage(k)
    cy_swap.wait()
    total = grad_sum.finish()
    own_grad = both(cs2[...], cb_all[z], 1).astype(F32).reshape(rows, CH)
    grad_mixed = (own_grad + total).astype(BF16).reshape(nb, BLOCK, CH)

    put(g2, backward_levels(wy, [grad_mixed[i] for i in range(nb)]))
    gy_swap = Swap(g2, g1, gy_sem, y, by_y)
    gy_swap.start()
    for k in rest[1:2]:
        out_sum.stage(k)
    for k in rest[2:]:
        out_sum.stage(k)
    gy_swap.wait()
    put(g1s, backward_levels(wx, [g1[i] for i in range(nb)]))
    gx_swap = Swap(g1s, g0, gx_sem, q, by_q)
    gx_swap.start()
    lo_turn = Turn(out2, layer_out, lo_sem)
    for p in range(parts):
        blocks = pl.ds(p * size, size)
        whole = mixed_all[z, blocks].astype(F32).reshape(lines_of, CH) + out_sum.total(p)
        out2[blocks] = whole.astype(BF16).reshape(size, BLOCK, CH)
        lo_turn.start(range(p * size, (p + 1) * size))
    gx_swap.wait()
    grads = [g0[i] for i in range(nb)]
    for factor in reversed(range(LOCAL)):
        terms = transposed_terms([mixl[factor, i] for i in range(nb)], grads)
        put(cross, [t[BLOCK:] for t in terms])
        grads = [(terms[i][:BLOCK] + cross[pattern[factor, i]]).astype(BF16) for i in range(nb)]
    put(g0s, grads)
    gedges = rim(
        g0s.at[0, pl.ds(0, TILE)], g0s.at[nb - 1, pl.ds(BLOCK - TILE, TILE)], ghalo, gh_sem
    )
    rim_start(gedges, ghalo)
    rim_wait(gedges)
    go_v[...] = convolve(g0s[...].reshape(rows, CH), (ghalo[0], ghalo[1]), tap2, tap1, tap0)
    grad_save = pltpu.make_async_copy(go_v, grad_out, save_sem.at[1])
    grad_save.start()

    rim_drain(edges)
    rim_drain(gedges)
    for transfer in (
        wq_swap, wx_swap, wr_swap, spread, sx_swap, sy_swap, ax_swap, ay_swap, cx_swap, cy_swap, bx_swap, by_swap,
        cot_ring, last_ring, mixed_ring, grad_sum, out_sum, gy_swap, gx_swap, lo_turn,
    ):
        transfer.drain()
    conv_save.wait()
    lo_turn.wait()
    grad_save.wait()


def publish(*refs):
    sources, targets, sem = refs[:3], refs[3:6], refs[6]
    copies = [pltpu.make_async_copy(a, b, sem.at[i]) for i, (a, b) in enumerate(zip(sources, targets))]
    for copy in copies:
        copy.start()
    for copy in copies:
        copy.wait()


def on_device(nb, zs, inputs, conv_weight, mixing, pattern, w_in, w_out, cotangent):
    rows, _ = inputs.shape
    levels = nb.bit_length() - 1
    hidden = w_in.shape[1]
    channels = w_in.shape[0]
    far = zs // 2
    vmem = pltpu.VMEM
    dma = pltpu.SemaphoreType.DMA
    blocks = (nb, BLOCK, CH)
    parts = min(4, nb)
    deep = (nb, TOP, hidden)
    scratch = [
        vmem((rows, CH), BF16),
        vmem((rows, CH), BF16),
        vmem(conv_weight.shape, BF16),
        pltpu.SMEM(pattern.shape, jnp.int32),
        vmem((LOCAL, *blocks), BF16),
        vmem((channels, hidden), BF16),
        vmem((hidden, channels), BF16),
        vmem((2, TILE, CH), BF16),
        vmem((2, TILE, CH), BF16),
        *[vmem(blocks, BF16)] * 4,
        *[vmem((levels, *blocks), BF16)] * 2,
        vmem((levels, nb, TILE, CH), BF16),
        vmem((zs, nb, TOP, CH), BF16),
        vmem((nb, TILE, CH), BF16),
        vmem((zs, nb, TILE, CH), BF16),
        vmem((nb * TILE, hidden), F32),
        vmem((zs, *blocks), BF16),
        vmem((rows, hidden), F32),
        *[vmem(deep, BF16)] * 3,
        *[vmem((rows, hidden), BF16)] * 2,
        *[vmem((zs - 1, *blocks), BF16)] * 2,
        vmem((rows, CH), F32),
        *[vmem((zs - 1, *blocks), BF16)] * 2,
        vmem((rows, CH), F32),
        vmem((rows, 2 * CH), F32),
        vmem((far, rows, 2 * CH), F32),
        *[vmem(blocks, BF16)] * 5,
        vmem(blocks, F32),
        vmem(blocks, BF16),
        *[vmem((nb, TOP, CH), BF16)] * 2,
        vmem((rows, CH), BF16),
        dma((7,)),
        dma((2,)),
        dma((2, 2)),
        *[dma((2,))] * 3,
        dma((1 + 4 * levels,)),
        *[dma((2,))] * 4,
        dma((5,)),
        *[dma((2, far, parts))] * 2,
        dma((1 + nb,)),
        *[dma((2,))] * 6,
        dma((2, 2)),
    ]
    out = jax.ShapeDtypeStruct((rows, CH), BF16)
    hbm = pl.BlockSpec(memory_space=pl.ANY)
    results = pl.pallas_call(
        functools.partial(kernel, nb, zs),
        out_shape=(out, out, out),
        in_specs=[hbm] * 7,
        out_specs=(hbm, hbm, hbm),
        scratch_shapes=scratch,
        compiler_params=pltpu.CompilerParams(
            collective_id=0, has_side_effects=True, vmem_limit_bytes=28 * 1024 * 1024
        ),
    )(*[pltpu.with_memory_space_constraint(v, pltpu.HBM) for v in (
        inputs, conv_weight, mixing, pattern, w_in, w_out, cotangent.reshape(blocks)
    )])
    return pl.pallas_call(
        publish,
        out_shape=(out, out, out),
        in_specs=[pl.BlockSpec(memory_space=pltpu.VMEM)] * 3,
        out_specs=(hbm, hbm, hbm),
        scratch_shapes=[dma((3,))],
        compiler_params=pltpu.CompilerParams(vmem_limit_bytes=4 * 1024 * 1024),
    )(*results)


def solution(mesh):
    seq, zs = mesh.shape["seq"], mesh.shape["ch"]
    nb = 1 << ((seq.bit_length() - 1) // 2)
    return jax.shard_map(
        functools.partial(on_device, nb, zs),
        mesh=mesh,
        in_specs=(
            P("seq", "ch"),
            P(None, "ch"),
            P(None, "seq", None, None),
            P(None, "seq"),
            P(None, "ch"),
            P("ch", None),
            P("seq", "ch"),
        ),
        out_specs=(P("seq", "ch"), P("seq", "ch"), P("seq", "ch")),
        check_vma=False,
    )
```

```python
import functools

import jax
import jax.numpy as jnp
from jax import lax
from jax.experimental import pallas as pl
from jax.experimental.pallas import tpu as pltpu
from jax.sharding import PartitionSpec as P

BLOCK = 64
LOCAL = 2
CH = 128
TILE = 16
SPLIT = BLOCK // TILE
TOP = BLOCK - TILE
MESH = pl.DeviceIdType.MESH
F32 = jnp.float32
BF16 = jnp.bfloat16
root_two_pi = 0.7978845608028654


def mod(value, size):
    return lax.rem(value + size, size)


def both(first, second, axis):
    return jnp.concatenate([first, second], axis=axis)


def forward_factor(weights, state, mates):
    return [
        jnp.dot(w, both(own, mate, 0), preferred_element_type=F32).astype(BF16)
        for w, own, mate in zip(weights, state, mates)
    ]


def transposed_terms(weights, grads):
    return [
        lax.dot_general(w, g, (((0,), (0,)), ((), ())), preferred_element_type=F32)
        for w, g in zip(weights, grads)
    ]


def kernel(nb, zs, *refs):
    (
        inputs, taps_hbm, mixing, pattern_hbm, w_in_hbm, w_out_hbm, cot,
        layer_out, conv_out, grad_out,
        x_v, cv, taps_ref, pattern, mixl, win, wout,
        halo, ghalo, st0, sx, st1, sy, wx, wy, wq,
        cot_all, cb1, cb_all, gb, mixed_all, hid, ga0, ga1, ga2, act, ghid,
        rs_send, rs_recv, rs_own, ro_send, ro_recv, ro_own, terms,
        g2, g1s, g1, g0s, g0, cross, out2, cs1, cs2, go_v,
        load_sem, save_sem, halo_sem, wx_sem, wq_sem, wr_sem, wz_sem, sx_sem, sy_sem,
        bx_sem, by_sem, ring_sem, cr_sem, mr_sem, ax_sem, ay_sem, cx_sem, cy_sem,
        gy_sem, gx_sem, lo_sem, gh_sem,
    ) = refs
    levels = nb.bit_length() - 1
    rows = nb * BLOCK
    far = zs // 2
    parts = min(4, nb)
    size = nb // parts
    lines_of = size * BLOCK
    count = nb * nb
    s = lax.axis_index("seq")
    z = lax.axis_index("ch")
    y = lax.div(s, nb)
    q = lax.rem(s, nb)
    up = mod(z + 1, zs)
    down = mod(z - 1, zs)
    up2 = mod(z + 2, zs)
    down2 = mod(z - 2, zs)
    quarter = lax.rem(z, SPLIT)
    strip = pl.ds(pl.multiple_of(quarter * TILE, TILE), TILE)

    loads = [
        pltpu.make_async_copy(inputs, x_v, load_sem.at[0]),
        pltpu.make_async_copy(mixing.at[pl.ds(0, LOCAL)], mixl, load_sem.at[1]),
        pltpu.make_async_copy(w_out_hbm, wout, load_sem.at[2]),
        pltpu.make_async_copy(w_in_hbm, win, load_sem.at[3]),
        pltpu.make_async_copy(taps_hbm, taps_ref, load_sem.at[4]),
        pltpu.make_async_copy(pattern_hbm, pattern, load_sem.at[5]),
    ]
    for load in loads:
        load.start()

    barrier = pltpu.get_barrier_semaphore()

    def greet(seq, ch):
        pl.semaphore_signal(barrier, inc=1, device_id=(seq, ch), device_id_type=MESH)

    @pl.when(s > 0)
    def _():
        greet(s - 1, z)

    @pl.when(s < count - 1)
    def _():
        greet(s + 1, z)

    for d in range(1, nb):
        greet(y * nb + mod(q + d, nb), z)
        greet(mod(y + d, nb) * nb + q, z)
    greet(s, up)
    greet(s, down)
    greet(s, up2)
    greet(s, down2)
    ends = jnp.where(s > 0, 1, 0) + jnp.where(s < count - 1, 1, 0)
    pl.semaphore_wait(barrier, 2 * (nb - 1) + 4 + ends)

    def arrival(view, sem):
        pltpu.make_async_copy(view, view, sem).wait()

    class Swap:
        def __init__(self, src, dst, sems, slot, peer, pick_src=None, pick_dst=None, many_src=None, many_dst=None):
            self.src, self.dst, self.sems, self.slot, self.peer = src, dst, sems, slot, peer
            self.pick_src, self.pick_dst = pick_src or first, pick_dst or first
            self.many_src, self.many_dst = many_src or several, many_dst or several

        def recv_sem(self, t):
            return self.sems.at[1]

        def remote(self, t, into):
            return pltpu.make_async_remote_copy(
                src_ref=self.pick_src(self.src, t),
                dst_ref=self.pick_dst(self.dst, into),
                send_sem=self.sems.at[0],
                recv_sem=self.recv_sem(into),
                device_id=(self.peer(t), z),
                device_id_type=MESH,
            )

        def own(self):
            return pltpu.make_async_copy(
                self.pick_src(self.src, self.slot), self.pick_dst(self.dst, self.slot), self.recv_sem(self.slot)
            )

        def start(self):
            for d in range(1, nb):
                self.remote(mod(self.slot + d, nb), self.slot).start()
            self.own().start()

        def wait(self):
            arrival(self.many_dst(self.dst, nb), self.sems.at[1])

        def drain(self):
            arrival(self.many_src(self.src, nb - 1), self.sems.at[0])

    class Stream(Swap):
        def recv_sem(self, t):
            return self.sems.at[1 + t]

        def wait(self, t):
            arrival(self.pick_dst(self.dst, t), self.recv_sem(t))

    def first(ref, t):
        return ref.at[t]

    def several(ref, n):
        return ref.at[pl.ds(0, n)]

    def by_q(t):
        return y * nb + t

    def by_y(t):
        return t * nb + q

    class Turn:
        def __init__(self, src, dst, sems):
            self.src, self.dst, self.sems = src, dst, sems

        def start(self, blocks):
            for t in blocks:
                into = self.dst.at[pl.ds(q * BLOCK, BLOCK)]

                @pl.when(t * nb + y != s)
                def _():
                    pltpu.make_async_remote_copy(
                        src_ref=self.src.at[t], dst_ref=into, send_sem=self.sems.at[0], recv_sem=self.sems.at[1],
                        device_id=(t * nb + y, z), device_id_type=MESH,
                    ).start()

                @pl.when(t * nb + y == s)
                def _():
                    pltpu.make_async_copy(self.src.at[t], into, self.sems.at[1]).start()

        def wait(self):
            arrival(self.dst, self.sems.at[1])

        def drain(self):
            @pl.when(y == q)
            def _():
                arrival(self.src.at[pl.ds(0, nb - 1)], self.sems.at[0])

            @pl.when(y != q)
            def _():
                arrival(self.src, self.sems.at[0])

    def ours(way, p, count=parts):
        return (p < count // 2) == (way == 0)

    class Gather:
        def __init__(self, buf, parts, pick, first_pick, send_sem, sems):
            self.parts = parts
            self.buf, self.pick, self.first_pick, self.send_sem, self.sems = buf, pick, first_pick, send_sem, sems

        def copy(self, way, step, p, chunk):
            part = self.pick(chunk, p)
            return pltpu.make_async_remote_copy(
                src_ref=self.first_pick(p) if step == 0 else part,
                dst_ref=part,
                send_sem=self.send_sem.at[0],
                recv_sem=self.sems.at[way, step, p],
                device_id=(s, up if way == 0 else down),
                device_id_type=MESH,
            )

        def chunk(self, way, step):
            return mod(z - step, zs) if way == 0 else mod(z + step, zs)

        def each(self, step):
            for p in range(self.parts):
                for way in range(2):
                    if step < far - 1 or ours(way, p, self.parts):
                        yield way, p

        def came(self, way, step, p):
            part = self.pick(self.chunk(way, step + 1), p)
            return pltpu.make_async_remote_copy(
                src_ref=part,
                dst_ref=part,
                send_sem=self.send_sem.at[0],
                recv_sem=self.sems.at[way, step, p],
                device_id=(s, up if way == 0 else down),
                device_id_type=MESH,
            )

        def step(self, step):
            for p in range(self.parts):
                for way in range(2):
                    if step > 0:
                        self.came(way, step - 1, p).wait_recv()
                    if step < far - 1 or ours(way, p, self.parts):
                        self.copy(way, step, p, self.chunk(way, step)).start()

        def finish(self):
            for way, p in self.each(far - 1):
                self.came(way, far - 1, p).wait_recv()

        def drain(self):
            arrival(self.buf.at[pl.ds(0, zs - 1)], self.send_sem.at[0])

    class Scatter:
        def __init__(self, send, recv, own, send_sem, sems, pair, terms, early):
            self.send, self.recv, self.own, self.send_sem, self.sems, self.pair = send, recv, own, send_sem, sems, pair
            self.terms, self.early = terms, early

        def prepare(self, k):
            near = z if k == far else mod(z - k, zs)
            self.term(k)[...] = self.pair(mod(z + k, zs), near)

        def term(self, k):
            return self.terms.at[far - k]

        def at(self, way, step, p):
            slot = zs - 2 if step == 0 else 2 * (step - 1) + way
            return slot, pl.ds(p * size, size)

        def copy(self, way, step, p):
            slot, blocks = self.at(way, step, p)
            return pltpu.make_async_remote_copy(
                src_ref=self.send.at[slot, blocks],
                dst_ref=self.recv.at[slot, blocks],
                send_sem=self.send_sem.at[0],
                recv_sem=self.sems.at[way, step, p],
                device_id=(s, up if way == 0 else down),
                device_id_type=MESH,
            )

        def arrived(self, way, step, p):
            if step < 0 or (step == 0 and not ours(way, p)):
                return None
            self.copy(way, step, p).wait_recv()
            slot, blocks = self.at(way, step, p)
            return self.recv[slot, blocks].astype(F32).reshape(lines_of, CH)

        def pass_on(self, way, step, p, value):
            slot, blocks = self.at(way, step, p)
            self.send[slot, blocks] = value.astype(BF16).reshape(size, BLOCK, CH)
            self.copy(way, step, p).start()

        def stage(self, k):
            step = far - k
            value_of = self.term(k)
            if k == far or (k == far - 1 and not self.early):
                self.prepare(k)
            todo = [(way, p) for p in range(parts) for way in range(2)]
            if k == far:
                todo = [(way, p) for way, p in todo if ours(way, p)]
            elif k == far - 1:
                todo.sort(key=lambda item: ours(*item))
            for index, (way, p) in enumerate(todo):
                if k == far - 1 and index == parts:
                    for later in range(k - 1, 0, -1):
                        self.prepare(later)
                value = value_of[pl.ds(p * lines_of, lines_of), pl.ds(0 if k == far else way * CH, CH)]
                came = self.arrived(way, step - 1, p)
                self.pass_on(way, step, p, value if came is None else value + came)
            if k == far:
                self.own[...] = value_of[:, pl.ds(CH, CH)]
                if self.early and far > 1:
                    self.prepare(k - 1)

        def total(self, p):
            value = self.own[pl.ds(p * lines_of, lines_of), :]
            for way in range(2):
                came = self.arrived(way, far - 1, p)
                if came is not None:
                    value = value + came
            return value

        def finish(self):
            return jnp.concatenate([self.total(p) for p in range(parts)], axis=0)

        def drain(self):
            arrival(self.send, self.send_sem.at[0])

    class Spread:
        def __init__(self):
            hb = nb // 2
            self.cases = [
                (up, down, 1, pl.ds(0, nb)), (down, up, -1, pl.ds(0, nb)),
                (up2, down2, 2, pl.ds(0, hb)), (down2, up2, -2, pl.ds(hb, hb)),
            ]

        def copy(self, case, level, theirs):
            to, _, shift, slots = self.cases[case]
            index = lax.rem(quarter - shift + 2 * SPLIT, SPLIT) if theirs else quarter
            part = wy.at[level, slots, pl.ds(pl.multiple_of(index * TILE, TILE), TILE)]
            return pltpu.make_async_remote_copy(
                src_ref=part, dst_ref=part, send_sem=wz_sem.at[0], recv_sem=wz_sem.at[1 + 4 * level + case],
                device_id=(s, to), device_id_type=MESH,
            )

        def start(self):
            for level in range(levels):
                for case in range(4):
                    self.copy(case, level, False).start()

        def wait(self, level):
            for case in range(4):
                self.copy(case, level, True).wait_recv()

        def drain(self):
            arrival(wy.at[pl.ds(0, levels), pl.ds(0, nb), pl.ds(0, 3 * TILE)], wz_sem.at[0])

    def rim(src_head, src_tail, dst, sems):
        return (
            pltpu.make_async_remote_copy(
                src_ref=src_tail, dst_ref=dst.at[0], send_sem=sems.at[0, 0], recv_sem=sems.at[1, 0],
                device_id=(s + 1, z), device_id_type=MESH,
            ),
            pltpu.make_async_remote_copy(
                src_ref=src_head, dst_ref=dst.at[1], send_sem=sems.at[0, 1], recv_sem=sems.at[1, 1],
                device_id=(s - 1, z), device_id_type=MESH,
            ),
        )

    def rim_start(pair, dst):
        @pl.when(s < count - 1)
        def _():
            pair[0].start()

        @pl.when(s > 0)
        def _():
            pair[1].start()

        @pl.when(s == 0)
        def _():
            dst[0] = jnp.zeros((TILE, CH), BF16)

        @pl.when(s == count - 1)
        def _():
            dst[1] = jnp.zeros((TILE, CH), BF16)

    def rim_wait(pair):
        @pl.when(s > 0)
        def _():
            pair[0].wait_recv()

        @pl.when(s < count - 1)
        def _():
            pair[1].wait_recv()

    def rim_drain(pair):
        @pl.when(s < count - 1)
        def _():
            pair[0].wait_send()

        @pl.when(s > 0)
        def _():
            pair[1].wait_send()

    def convolve(value, edges, before, same, after):
        value = value.astype(F32)
        line = lax.broadcasted_iota(jnp.int32, value.shape, 0)
        above = edges[0].astype(F32)[TILE - 1 : TILE, :]
        below = edges[1].astype(F32)[0:1, :]
        earlier = jnp.where(line == 0, above, pltpu.roll(value, 1, 0))
        later = jnp.where(line == rows - 1, below, pltpu.roll(value, rows - 1, 0))
        return (before * earlier + same * value + after * later).astype(BF16)

    def put(ref, blocks):
        for i, block in enumerate(blocks):
            ref[i] = block

    def forward_levels(weights, state, before=None):
        for level in range(levels):
            if before is not None:
                before(level)
            state = forward_factor(
                [weights[level, i] for i in range(nb)], state, [state[i ^ (1 << level)] for i in range(nb)]
            )
        return state

    def backward_levels(weights, grads):
        for level in reversed(range(levels)):
            terms = transposed_terms([weights[level, i] for i in range(nb)], grads)
            grads = [
                (terms[i][:BLOCK] + terms[i ^ (1 << level)][BLOCK:]).astype(BF16) for i in range(nb)
            ]
        return grads

    edges = rim(inputs.at[pl.ds(0, TILE)], inputs.at[pl.ds(rows - TILE, TILE)], halo, halo_sem)
    rim_start(edges, halo)
    upper, last = pl.ds(0, TOP), pl.ds(TOP, TILE)
    cot_ring = Gather(
        cot_all, parts,
        lambda chunk, p: cot_all.at[chunk, pl.ds(p * size, size)],
        lambda p: cot.at[pl.ds(p * size, size), upper], ring_sem.at[pl.ds(0, 1)], cr_sem,
    )
    cot_ring.step(0)
    own_cot = pltpu.make_async_copy(cot.at[pl.ds(0, nb), upper], cot_all.at[z], load_sem.at[6])
    own_cot.start()
    low, high = pl.ds(LOCAL, levels), pl.ds(LOCAL + levels, levels)
    every = pl.ds(0, levels)
    wq_swap = Swap(
        mixing, wq, wq_sem, q, by_q,
        lambda ref, t: ref.at[high, t, strip], lambda ref, t: ref.at[every, t],
        lambda ref, n: ref.at[high, pl.ds(0, n), strip], lambda ref, n: ref.at[every, pl.ds(0, n)],
    )
    wq_swap.start()
    wx_swap = Swap(
        mixing, wx, wx_sem, q, by_q,
        lambda ref, t: ref.at[low, t], lambda ref, t: ref.at[every, t],
        lambda ref, n: ref.at[low, pl.ds(0, n)], lambda ref, n: ref.at[every, pl.ds(0, n)],
    )
    wx_swap.start()

    loads[4].wait()
    taps = taps_ref[...].astype(F32)
    tap0, tap1, tap2 = taps[0:1], taps[1:2], taps[2:3]
    loads[0].wait()
    rim_wait(edges)
    cv[...] = convolve(x_v[...], (halo[0], halo[1]), tap0, tap1, tap2)
    conv_save = pltpu.make_async_copy(cv, conv_out, save_sem.at[0])
    conv_save.start()
    st0[...] = cv[...].reshape(nb, BLOCK, CH)
    loads[1].wait()
    loads[5].wait()
    for factor in range(LOCAL):
        state = [st0[i] for i in range(nb)]
        mates = [st0[pattern[factor, i]] for i in range(nb)]
        put(st0, forward_factor([mixl[factor, i] for i in range(nb)], state, mates))

    sx_swap = Swap(st0, sx, sx_sem, q, by_q)
    sx_swap.start()
    bx_swap = Swap(
        cot, cb1, bx_sem, q, by_q,
        lambda ref, t: ref.at[t, last], None, lambda ref, n: ref.at[pl.ds(0, n), last],
    )
    bx_swap.start()
    if far > 1:
        cot_ring.step(1)
    wq_swap.wait()
    wr_swap = Swap(
        wq, wy, wr_sem, y, by_y,
        lambda ref, t: ref.at[every, t], lambda ref, t: ref.at[every, t, strip],
        lambda ref, n: ref.at[every, pl.ds(0, n)], lambda ref, n: ref.at[every, pl.ds(0, n), strip],
    )
    wr_swap.start()
    if far > 2:
        cot_ring.step(2)
    wx_swap.wait()
    sx_swap.wait()
    put(st1, forward_levels(wx, [sx[i] for i in range(nb)]))

    sy_swap = Swap(st1, sy, sy_sem, y, by_y)
    sy_swap.start()
    for step in range(3, far):
        cot_ring.step(step)
    wr_swap.wait()
    spread = Spread()
    spread.start()
    bx_swap.wait()
    by_swap = Swap(
        cb1, cb_all, by_sem, y, by_y, None, lambda ref, t: ref.at[z, t], None, lambda ref, n: ref.at[z, pl.ds(0, n)]
    )
    by_swap.start()

    def channels(index):
        return pl.ds(pl.multiple_of(index * CH, CH), CH)

    def grad_act(buf):
        value = None
        lines = buf.shape[1] * buf.shape[2]
        for c in range(0, zs, 2):
            part = lax.dot_general(
                both(buf[c].reshape(lines, CH), buf[c + 1].reshape(lines, CH), 1), wout[:, pl.ds(c * CH, 2 * CH)],
                (((1,), (1,)), ((), ())), preferred_element_type=F32,
            )
            value = part if value is None else value + part
        return value

    cot_ring.finish()
    own_cot.wait()
    loads[2].wait()
    ga0[...] = grad_act(cot_all).astype(BF16).reshape(ga0.shape)
    ax_swap = Stream(ga0, ga1, ax_sem, q, by_q)
    ax_swap.start()
    cx_swap = Swap(
        cot, cs1, cx_sem, q, by_q,
        lambda ref, t: ref.at[t, upper], None, lambda ref, n: ref.at[pl.ds(0, n), upper],
    )
    cx_swap.start()
    sy_swap.wait()
    by_swap.wait()
    wide = nb // 2
    last_ring = Gather(
        cb_all, 2,
        lambda chunk, p: cb_all.at[chunk, pl.ds(p * wide, wide)],
        lambda p: cb_all.at[z, pl.ds(p * wide, wide)], ring_sem.at[pl.ds(4, 1)], cr_sem,
    )
    last_ring.step(0)
    mixed = forward_levels(wy, [sy[i] for i in range(nb)], spread.wait)
    for i in range(nb):
        mixed_all[z, i] = mixed[i]
    mixed_ring = Gather(
        mixed_all, parts,
        lambda chunk, p: mixed_all.at[chunk, pl.ds(p * size, size)],
        lambda p: mixed_all.at[z, pl.ds(p * size, size)], ring_sem.at[pl.ds(1, 1)], mr_sem,
    )
    mixed_ring.step(0)

    def add_hidden(a, b, start):
        value = jnp.dot(
            both(mixed_all[a].reshape(rows, CH), mixed_all[b].reshape(rows, CH), 1),
            both(win[channels(a), :], win[channels(b), :], 0),
            preferred_element_type=F32,
        )
        hid[...] = value if start else hid[...] + value

    def one_hidden(a):
        return jnp.dot(mixed_all[a].reshape(rows, CH), win[channels(a), :], preferred_element_type=F32)

    ay_swap = Swap(ga1, ga2, ay_sem, y, by_y)
    cy_swap = Swap(cs1, cs2, cy_sem, y, by_y)
    loads[3].wait()
    hid[...] = one_hidden(z)
    for step in range(1, far):
        last_ring.step(step)
        mixed_ring.step(step)
        add_hidden(mod(z - step, zs), mod(z + step, zs), False)
        if step == 1:
            for d in range(nb):
                t = mod(q + d, nb)
                ax_swap.wait(t)

                @pl.when(t == y)
                def _():
                    ay_swap.own().start()

                @pl.when(t != y)
                def _():
                    ay_swap.remote(t, y).start()
    cx_swap.wait()
    cy_swap.start()
    last_ring.finish()
    gb[...] = grad_act(cb_all)
    mixed_ring.finish()
    hid[...] += one_hidden(mod(z + far, zs))
    ay_swap.wait()

    @pl.loop(0, nb)
    def _(i):
        lines = pl.ds(pl.multiple_of(i * BLOCK, BLOCK), BLOCK)
        v = hid[lines, :]
        square = v * v
        tanh_val = jnp.tanh(root_two_pi * (v + 0.044715 * square * v))
        plus = 0.5 * (1.0 + tanh_val)
        act[lines, :] = (v * plus).astype(BF16)
        slope = root_two_pi * (1.0 + 3.0 * 0.044715 * square)
        slope = plus + 0.5 * v * (1.0 - tanh_val * tanh_val) * slope
        strip_of = pl.ds(pl.multiple_of(i * TILE, TILE), TILE)
        slope_in = both(ga2[i].astype(F32), gb[strip_of, :], 0)
        ghid[lines, :] = (slope_in * slope).astype(BF16)

    def grad_pair(a, b):
        return lax.dot_general(
            ghid[...], both(win[channels(a), :], win[channels(b), :], 0),
            (((1,), (1,)), ((), ())), preferred_element_type=F32,
        )

    def out_pair(a, b):
        return jnp.dot(
            act[...], both(wout[:, channels(a)], wout[:, channels(b)], 1), preferred_element_type=F32
        )

    grad_sum = Scatter(rs_send, rs_recv, rs_own, ring_sem.at[pl.ds(2, 1)], mr_sem, grad_pair, terms, True)
    out_sum = Scatter(ro_send, ro_recv, ro_own, ring_sem.at[pl.ds(3, 1)], cr_sem, out_pair, terms, False)
    for k in range(far, 1, -1):
        grad_sum.stage(k)
    out_sum.stage(far)
    grad_sum.stage(1)
    rest = list(range(far - 1, 0, -1))
    for k in rest[:1]:
        out_sum.stage(k)
    cy_swap.wait()
    total = grad_sum.finish()
    own_grad = both(cs2[...], cb_all[z], 1).astype(F32).reshape(rows, CH)
    grad_mixed = (own_grad + total).astype(BF16).reshape(nb, BLOCK, CH)

    put(g2, backward_levels(wy, [grad_mixed[i] for i in range(nb)]))
    gy_swap = Swap(g2, g1, gy_sem, y, by_y)
    gy_swap.start()
    for k in rest[1:2]:
        out_sum.stage(k)
    for k in rest[2:]:
        out_sum.stage(k)
    gy_swap.wait()
    put(g1s, backward_levels(wx, [g1[i] for i in range(nb)]))
    gx_swap = Swap(g1s, g0, gx_sem, q, by_q)
    gx_swap.start()
    lo_turn = Turn(out2, layer_out, lo_sem)
    for p in range(parts):
        blocks = pl.ds(p * size, size)
        whole = mixed_all[z, blocks].astype(F32).reshape(lines_of, CH) + out_sum.total(p)
        out2[blocks] = whole.astype(BF16).reshape(size, BLOCK, CH)
        lo_turn.start(range(p * size, (p + 1) * size))
    gx_swap.wait()
    grads = [g0[i] for i in range(nb)]
    for factor in reversed(range(LOCAL)):
        terms = transposed_terms([mixl[factor, i] for i in range(nb)], grads)
        put(cross, [t[BLOCK:] for t in terms])
        grads = [(terms[i][:BLOCK] + cross[pattern[factor, i]]).astype(BF16) for i in range(nb)]
    put(g0s, grads)
    gedges = rim(
        g0s.at[0, pl.ds(0, TILE)], g0s.at[nb - 1, pl.ds(BLOCK - TILE, TILE)], ghalo, gh_sem
    )
    rim_start(gedges, ghalo)
    rim_wait(gedges)
    go_v[...] = convolve(g0s[...].reshape(rows, CH), (ghalo[0], ghalo[1]), tap2, tap1, tap0)
    grad_save = pltpu.make_async_copy(go_v, grad_out, save_sem.at[1])
    grad_save.start()

    rim_drain(edges)
    rim_drain(gedges)
    for transfer in (
        wq_swap, wx_swap, wr_swap, spread, sx_swap, sy_swap, ax_swap, ay_swap, cx_swap, cy_swap, bx_swap, by_swap,
        cot_ring, last_ring, mixed_ring, grad_sum, out_sum, gy_swap, gx_swap, lo_turn,
    ):
        transfer.drain()
    conv_save.wait()
    lo_turn.wait()
    grad_save.wait()


def publish(*refs):
    sources, targets, sem = refs[:3], refs[3:6], refs[6]
    copies = [pltpu.make_async_copy(a, b, sem.at[i]) for i, (a, b) in enumerate(zip(sources, targets))]
    for copy in copies:
        copy.start()
    for copy in copies:
        copy.wait()


def on_device(nb, zs, inputs, conv_weight, mixing, pattern, w_in, w_out, cotangent):
    rows, _ = inputs.shape
    levels = nb.bit_length() - 1
    hidden = w_in.shape[1]
    channels = w_in.shape[0]
    far = zs // 2
    vmem = pltpu.VMEM
    dma = pltpu.SemaphoreType.DMA
    blocks = (nb, BLOCK, CH)
    parts = min(4, nb)
    deep = (nb, TOP, hidden)
    scratch = [
        vmem((rows, CH), BF16),
        vmem((rows, CH), BF16),
        vmem(conv_weight.shape, BF16),
        pltpu.SMEM(pattern.shape, jnp.int32),
        vmem((LOCAL, *blocks), BF16),
        vmem((channels, hidden), BF16),
        vmem((hidden, channels), BF16),
        vmem((2, TILE, CH), BF16),
        vmem((2, TILE, CH), BF16),
        *[vmem(blocks, BF16)] * 4,
        *[vmem((levels, *blocks), BF16)] * 2,
        vmem((levels, nb, TILE, CH), BF16),
        vmem((zs, nb, TOP, CH), BF16),
        vmem((nb, TILE, CH), BF16),
        vmem((zs, nb, TILE, CH), BF16),
        vmem((nb * TILE, hidden), F32),
        vmem((zs, *blocks), BF16),
        vmem((rows, hidden), F32),
        *[vmem(deep, BF16)] * 3,
        *[vmem((rows, hidden), BF16)] * 2,
        *[vmem((zs - 1, *blocks), BF16)] * 2,
        vmem((rows, CH), F32),
        *[vmem((zs - 1, *blocks), BF16)] * 2,
        vmem((rows, CH), F32),
        vmem((far, rows, 2 * CH), F32),
        *[vmem(blocks, BF16)] * 5,
        vmem(blocks, F32),
        vmem(blocks, BF16),
        *[vmem((nb, TOP, CH), BF16)] * 2,
        vmem((rows, CH), BF16),
        dma((7,)),
        dma((2,)),
        dma((2, 2)),
        *[dma((2,))] * 3,
        dma((1 + 4 * levels,)),
        *[dma((2,))] * 4,
        dma((5,)),
        *[dma((2, far, parts))] * 2,
        dma((1 + nb,)),
        *[dma((2,))] * 6,
        dma((2, 2)),
    ]
    out = jax.ShapeDtypeStruct((rows, CH), BF16)
    hbm = pl.BlockSpec(memory_space=pl.ANY)
    results = pl.pallas_call(
        functools.partial(kernel, nb, zs),
        out_shape=(out, out, out),
        in_specs=[hbm] * 7,
        out_specs=(hbm, hbm, hbm),
        scratch_shapes=scratch,
        compiler_params=pltpu.CompilerParams(
            collective_id=0, has_side_effects=True, vmem_limit_bytes=28 * 1024 * 1024
        ),
    )(*[pltpu.with_memory_space_constraint(v, pltpu.HBM) for v in (
        inputs, conv_weight, mixing, pattern, w_in, w_out, cotangent.reshape(blocks)
    )])
    return pl.pallas_call(
        publish,
        out_shape=(out, out, out),
        in_specs=[pl.BlockSpec(memory_space=pltpu.VMEM)] * 3,
        out_specs=(hbm, hbm, hbm),
        scratch_shapes=[dma((3,))],
        compiler_params=pltpu.CompilerParams(vmem_limit_bytes=4 * 1024 * 1024),
    )(*results)


def solution(mesh):
    seq, zs = mesh.shape["seq"], mesh.shape["ch"]
    nb = 1 << ((seq.bit_length() - 1) // 2)
    return jax.shard_map(
        functools.partial(on_device, nb, zs),
        mesh=mesh,
        in_specs=(
            P("seq", "ch"),
            P(None, "ch"),
            P(None, "seq", None, None),
            P(None, "seq"),
            P(None, "ch"),
            P("ch", None),
            P("seq", "ch"),
        ),
        out_specs=(P("seq", "ch"), P("seq", "ch"), P("seq", "ch")),
        check_vma=False,
    )
```
